256 devices in a mesh: user: 16 (over y_hi, x, core), item: 16 (over y_lo, z).
Axes of the slice: x: 4, y: 4 (y_hi: 2, y_lo: 2; y = y_hi * 2 + y_lo), z: 8, core: 2. Of those that a mesh axis runs over, the one named last changes fastest.
Arguments:
- user_pred: bfloat16 [16384, 128], P('user'), may hold values from -1.75 to 1.75
- user_imp: bfloat16 [16384, 128], P('user'), may hold values from -1.75 to 1.75
- item_pred: bfloat16 [4096, 128], P('item'), may hold values from -1.75 to 1.75
- item_imp: bfloat16 [4096, 128], P('item'), may hold values from -1.75 to 1.75
- uno_user: int32 [16, 16, 64], P('user', 'item'), may hold values from 0 to 7
- uno_item: int32 [16, 16, 64], P('user', 'item'), may hold values from 0 to 1
- obs_user: int32 [16, 16, 16], P('user', 'item'), may hold values from 0 to 7
- obs_item: int32 [16, 16, 16], P('user', 'item'), may hold values from 0 to 1
- obs_count: int32 [16, 16, 16], P('user', 'item'), may hold values from 0 to 1
- obs_label: int32 [16, 16, 16, 128, 128], P('user', 'item'), may hold values from 0 to 2
- obs_prop: bfloat16 [16, 16, 16, 128, 128], P('user', 'item'), may hold values from 0.099609375 to 1
Outputs:
- user_pred_grad: float32 [16384, 128], P(('user', 'item'))
- user_imp_grad: float32 [16384, 128], P(('user', 'item'))
- item_pred_grad: float32 [4096, 128], P(('item', 'user'))
- item_imp_grad: float32 [4096, 128], P(('item', 'user'))
The draws below stay inside these ranges and needn't reach their ends.
Inputs may be any that keep to these rules, and one draw needn't show every extreme that they name: `uno_item`: each device's unobserved slots come in equal groups, one group for each item shard in order. Each device's observed slots come in equal groups of 16 / number of item indices, one group for each item shard in order; only the first obs_count slots of a group hold tiles.
All inputs are finite; a program needn't handle non-finite values.
Results may differ from the reference program's by a relative error of at most 0.0027.
Values may be sent and summed in bfloat16 or wider, within the bound.
A program may use at most 64 MiB of HBM per device.

```python
import math
import jax
import jax.numpy as jnp
from jax import lax

R = 128
TILE = 128
SH = 1024
ISH = 256
UNO_DEV = 64
OBS_DEV = 16
USERS = 16384
ITEMS = 4096
N_USER = 16
N_ITEM = 16


def touch_ends(entries, rng, low, high):
    place = [jax.random.randint(jax.random.fold_in(rng, axis), (), 0, length) for axis, length in enumerate(entries.shape)]
    main_axis = entries.shape.index(max(entries.shape))
    next_to = place[:main_axis] + [(place[main_axis] + 1) % entries.shape[main_axis]] + place[main_axis + 1:]
    return entries.at[tuple(place)].set(low).at[tuple(next_to)].set(high)


def block_levels(stream_key, dims, shards, low, largest):
    gain = 1.0
    for axis_at, parts in shards:
        steps = jax.random.uniform(jax.random.fold_in(jax.random.fold_in(stream_key, 6), axis_at), (parts,), jnp.float32, low / len(shards), largest / len(shards))
        gain = gain * jnp.repeat(jnp.exp(steps), dims[axis_at] // parts).reshape((-1,) + (1,) * (len(dims) - 1 - axis_at))
    return gain


def centred(own_key, extent, width, bound, pieces=(), held_as=jnp.bfloat16):
    factor_of = block_levels(own_key, extent, pieces, -0.22, 0.18) if pieces else 1.0
    array = jax.random.normal(own_key, extent, jnp.float32) * width * factor_of
    return jnp.minimum(jnp.maximum(array, -bound), bound).astype(held_as)


def setup_inputs(seed: int = 0) -> dict:
    streams_of = jax.random.split(jax.random.key(seed), 12)
    return {
        "user_pred": centred(streams_of[0], (USERS, R), 0.3, 1.75, ((0, 16),)),
        "user_imp": centred(streams_of[1], (USERS, R), 0.3, 1.75, ((0, 16),)),
        "item_pred": centred(streams_of[2], (ITEMS, R), 0.3, 1.75, ((0, 16),)),
        "item_imp": centred(streams_of[3], (ITEMS, R), 0.3, 1.75, ((0, 16),)),
        "uno_user": touch_ends(jax.random.randint(streams_of[4], (N_USER, N_ITEM, UNO_DEV), 0, SH // TILE), jax.random.fold_in(streams_of[4], 1), 0, (SH // TILE) - 1).astype(jnp.int32),
        "uno_item": touch_ends(jax.random.randint(streams_of[5], (N_USER, N_ITEM, UNO_DEV), 0, ISH // TILE), jax.random.fold_in(streams_of[5], 1), 0, (ISH // TILE) - 1).astype(jnp.int32),
        "obs_user": touch_ends(jax.random.randint(streams_of[6], (N_USER, N_ITEM, OBS_DEV), 0, SH // TILE), jax.random.fold_in(streams_of[6], 1), 0, (SH // TILE) - 1).astype(jnp.int32),
        "obs_item": touch_ends(jax.random.randint(streams_of[7], (N_USER, N_ITEM, OBS_DEV), 0, ISH // TILE), jax.random.fold_in(streams_of[7], 1), 0, (ISH // TILE) - 1).astype(jnp.int32),
        "obs_count": touch_ends(jax.random.randint(streams_of[8], (N_USER, N_ITEM, N_ITEM), 0, OBS_DEV // N_ITEM + 1), jax.random.fold_in(streams_of[8], 1), 0, (OBS_DEV // N_ITEM + 1) - 1).astype(jnp.int32),
        "obs_label": touch_ends(jax.random.randint(streams_of[9], (N_USER, N_ITEM, OBS_DEV, TILE, TILE), 0, 3), jax.random.fold_in(streams_of[9], 1), 0, 2).astype(jnp.int32),
        "obs_prop": jnp.clip(jnp.exp(math.log(1.0) - 2.306499 * jax.random.uniform(streams_of[10], (N_USER, N_ITEM, OBS_DEV, TILE, TILE), jnp.float32) ** block_levels(streams_of[10], (N_USER, N_ITEM, OBS_DEV, TILE, TILE), ((0, 16), (1, 16)), -0.2, 0.2)), 0.099609375, 1.0).astype(jnp.bfloat16),
    }


loss_weight = 0.015625


def batched(form, first, second):
    return jnp.einsum(form, first.astype(jnp.float32), second.astype(jnp.float32), precision=lax.Precision.HIGHEST)


def reference(user_pred, user_imp, item_pred, item_imp, uno_user, uno_item, obs_user, obs_item, obs_count, obs_label, obs_prop):
    user_blocks = SH // TILE
    item_blocks = ISH // TILE
    all_blocks = ITEMS // TILE
    uno_slots = UNO_DEV // N_ITEM
    obs_slots = OBS_DEV // N_ITEM
    users_both = jnp.stack([user_pred, user_imp]).reshape(2, N_USER, user_blocks, TILE, R)
    items_both = jnp.stack([item_pred, item_imp]).reshape(2, all_blocks, TILE, R)
    uno_shard = (jnp.arange(UNO_DEV) // uno_slots).astype(jnp.int32)
    obs_shard = (jnp.arange(OBS_DEV) // obs_slots).astype(jnp.int32)
    obs_place = (jnp.arange(OBS_DEV) % obs_slots).astype(jnp.int32)

    def device(carry, index):
        user_acc, item_acc = carry
        row_index = index // N_ITEM
        col_index = index % N_ITEM
        own_pred = users_both[0, row_index]
        own_imp = users_both[1, row_index]
        user_ids = uno_user[row_index, col_index]
        item_ids = uno_shard * item_blocks + uno_item[row_index, col_index]
        user_tiles = own_pred[user_ids]
        item_tiles = items_both[0][item_ids]
        logits = batched("tar,tbr->tab", user_tiles, item_tiles)
        imputed = batched("tar,tbr->tab", own_imp[user_ids], items_both[1][item_ids])
        grads = ((jax.nn.sigmoid(logits) - jax.nn.sigmoid(imputed)) * loss_weight).astype(jnp.bfloat16)
        user_part = jax.ops.segment_sum(batched("tab,tbr->tar", grads, item_tiles), user_ids, num_segments=user_blocks)
        item_part = jax.ops.segment_sum(batched("tab,tar->tbr", grads, user_tiles), item_ids, num_segments=all_blocks)

        obs_users = obs_user[row_index, col_index]
        obs_items = obs_shard * item_blocks + obs_item[row_index, col_index]
        ou_tiles = own_pred[obs_users]
        ox_tiles = own_imp[obs_users]
        ov_tiles = items_both[0][obs_items]
        oy_tiles = items_both[1][obs_items]
        ologits = batched("tar,tbr->tab", ou_tiles, ov_tiles)
        oimputed = batched("tar,tbr->tab", ox_tiles, oy_tiles)
        predicted = jax.nn.sigmoid(ologits)
        imputes = jax.nn.sigmoid(oimputed)
        counts = obs_count[row_index, col_index][obs_shard]
        valid = (obs_place < counts).astype(jnp.float32)[:, None, None]
        labels = obs_label[row_index, col_index]
        seen = (labels > 0).astype(jnp.float32)
        clicks = (labels == 2).astype(jnp.float32)
        weight = valid * seen / obs_prop[row_index, col_index].astype(jnp.float32)
        ograds = ((valid * (predicted - imputes) + weight * (imputes - clicks)) * loss_weight).astype(jnp.bfloat16)
        ohgrads = (2.0 * weight * (imputes - clicks) * ologits * ologits * imputes * (1.0 - imputes) * loss_weight).astype(jnp.bfloat16)
        user_part = user_part + jax.ops.segment_sum(batched("tab,tbr->tar", ograds, ov_tiles), obs_users, num_segments=user_blocks)
        user_imp_part = jax.ops.segment_sum(batched("tab,tbr->tar", ohgrads, oy_tiles), obs_users, num_segments=user_blocks)
        item_part = item_part + jax.ops.segment_sum(batched("tab,tar->tbr", ograds, ou_tiles), obs_items, num_segments=all_blocks)
        item_imp_part = jax.ops.segment_sum(batched("tab,tar->tbr", ohgrads, ox_tiles), obs_items, num_segments=all_blocks)
        user_acc = user_acc.at[:, row_index].add(jnp.stack([user_part, user_imp_part]))
        item_acc = item_acc + jnp.stack([item_part, item_imp_part])
        return (user_acc, item_acc), None

    start = (jnp.zeros((2, N_USER, user_blocks, TILE, R), jnp.float32), jnp.zeros((2, all_blocks, TILE, R), jnp.float32))
    (user_acc, item_acc), unused = lax.scan(device, start, jnp.arange(N_USER * N_ITEM, dtype=jnp.int32))
    user_acc = user_acc.reshape(2, USERS, R)
    item_acc = item_acc.reshape(2, ITEMS, R)
    return (user_acc[0], user_acc[1], item_acc[0], item_acc[1])
```

```python
import jax
import jax.numpy as jnp
from jax import lax
from jax.sharding import PartitionSpec as P

loss_weight = 0.015625
META_ROWS = 8


def product(form, first, second):
    return jnp.einsum(form, first, second, preferred_element_type=jnp.float32)


def split_product(form, wide, narrow):
    hi = wide.astype(jnp.bfloat16)
    lo = (wide - hi.astype(jnp.float32)).astype(jnp.bfloat16)
    return product(form, hi, narrow) + product(form, lo, narrow)


def shards(
    user_pred,
    user_imp,
    item_pred,
    item_imp,
    uno_user,
    uno_item,
    obs_user,
    obs_item,
    obs_count,
    obs_label,
    obs_prop,
):
    item_ways = lax.axis_size("item")
    user_ways = lax.axis_size("user")
    tile = obs_label.shape[-1]
    rank = user_pred.shape[1]
    user_rows = user_pred.shape[0]
    shard_rows = item_pred.shape[0]
    user_blocks = user_rows // tile
    item_blocks = shard_rows // tile
    n_blocks = user_blocks * item_blocks
    obs_slots = obs_user.shape[-1] // item_ways

    uno_pos = (uno_user * item_blocks + uno_item).reshape(item_ways, -1)
    uno_counts = jnp.sum(
        (uno_pos[:, :, None] == jnp.arange(n_blocks, dtype=jnp.int32)).astype(jnp.float32), axis=1
    )
    obs_pos = (obs_user * item_blocks + obs_item).reshape(item_ways, obs_slots)
    place = jnp.arange(obs_slots, dtype=jnp.int32)
    valid = (place[None, :] < obs_count.reshape(item_ways, 1)).astype(jnp.float32)
    meta = jnp.zeros((item_ways, META_ROWS, tile), jnp.float32)
    meta = meta.at[:, 0, :n_blocks].set(uno_counts)
    meta = meta.at[:, 1, :obs_slots].set(obs_pos.astype(jnp.float32))
    meta = meta.at[:, 2, :obs_slots].set(valid)
    labels = obs_label.reshape(item_ways, obs_slots * tile, tile).astype(jnp.bfloat16)
    propens = obs_prop.reshape(item_ways, obs_slots * tile, tile)
    package = jnp.concatenate([labels, propens, meta.astype(jnp.bfloat16)], axis=1)
    got = lax.all_to_all(package, "item", 0, 0, tiled=True)
    got_labels = got[:, : obs_slots * tile].reshape(item_ways * obs_slots, tile, tile)
    got_props = got[:, obs_slots * tile : 2 * obs_slots * tile].reshape(item_ways * obs_slots, tile, tile)
    got_meta = got[:, 2 * obs_slots * tile :].astype(jnp.float32)
    counts = jnp.sum(got_meta[:, 0, :n_blocks], axis=0)
    tile_pos = got_meta[:, 1, :obs_slots].reshape(-1).astype(jnp.int32)
    tile_valid = got_meta[:, 2, :obs_slots].reshape(-1)

    logits = product("ar,br->ab", user_pred, item_pred)
    imputed = product("ar,br->ab", user_imp, item_imp)

    def blocked(x):
        return x.reshape(user_blocks, tile, item_blocks, tile).transpose(0, 2, 1, 3).reshape(n_blocks, tile, tile)

    def unblocked(x):
        return x.reshape(user_blocks, item_blocks, tile, tile).transpose(0, 2, 1, 3).reshape(user_rows, shard_rows)

    logit_blocks = blocked(logits)
    imputed_blocks = blocked(imputed)
    uno_grads = ((jax.nn.sigmoid(logit_blocks) - jax.nn.sigmoid(imputed_blocks)) * loss_weight).astype(jnp.bfloat16)

    ologits = logit_blocks[tile_pos]
    predicted = jax.nn.sigmoid(ologits)
    imputes = jax.nn.sigmoid(imputed_blocks[tile_pos])
    tvalid = tile_valid[:, None, None]
    seen = (got_labels > 0).astype(jnp.float32)
    clicks = (got_labels == 2).astype(jnp.float32)
    weight = tvalid * seen / got_props.astype(jnp.float32)
    ograds = ((tvalid * (predicted - imputes) + weight * (imputes - clicks)) * loss_weight).astype(jnp.bfloat16)
    ohgrads = (
        2.0 * weight * (imputes - clicks) * ologits * ologits * imputes * (1.0 - imputes) * loss_weight
    ).astype(jnp.bfloat16)
    onehot = (tile_pos[:, None] == jnp.arange(n_blocks, dtype=jnp.int32)[None, :]).astype(jnp.bfloat16)
    grad_blocks = counts[:, None, None] * uno_grads.astype(jnp.float32) + product("tk,tab->kab", onehot, ograds)
    hgrad_blocks = product("tk,tab->kab", onehot, ohgrads)
    grad_full = unblocked(grad_blocks)
    hgrad_full = unblocked(hgrad_blocks)

    user_part = jnp.stack(
        [split_product("ab,br->ar", grad_full, item_pred), split_product("ab,br->ar", hgrad_full, item_imp)]
    )
    item_part = jnp.stack(
        [split_product("ab,ar->br", grad_full, user_pred), split_product("ab,ar->br", hgrad_full, user_imp)]
    )

    user_chunks = user_part.reshape(2, item_ways, user_rows // item_ways, rank).transpose(1, 0, 2, 3)
    user_got = lax.all_to_all(user_chunks, "item", 0, 0, tiled=True)
    user_share = jnp.sum(user_got, axis=0)
    item_chunks = item_part.reshape(2, user_ways, shard_rows // user_ways, rank).transpose(1, 0, 2, 3)
    item_got = lax.all_to_all(item_chunks, "user", 0, 0, tiled=True)
    item_share = jnp.sum(item_got, axis=0)
    return (user_share[0], user_share[1], item_share[0], item_share[1])


def solution(mesh):
    in_specs = (
        P("user", None),
        P("user", None),
        P("item", None),
        P("item", None),
        P("user", "item", None),
        P("user", "item", None),
        P("user", "item", None),
        P("user", "item", None),
        P("user", "item", None),
        P("user", "item", None, None, None),
        P("user", "item", None, None, None),
    )
    out_specs = (
        P(("user", "item"), None),
        P(("user", "item"), None),
        P(("item", "user"), None),
        P(("item", "user"), None),
    )
    return jax.shard_map(shards, mesh=mesh, in_specs=in_specs, out_specs=out_specs, check_vma=False)
```

```python
import functools

import jax
import jax.numpy as jnp
from jax import lax
from jax.experimental import pallas as pl
from jax.experimental.pallas import tpu as pltpu
from jax.sharding import PartitionSpec as P

MESH = pl.DeviceIdType.MESH

loss_weight = 0.015625
META_ROWS = 8


def product(form, first, second):
    return jnp.einsum(form, first, second, preferred_element_type=jnp.float32)


def exchange_kernel(axis, n, x_ref, y_ref, send_sem, recv_sem, local_sem):
    me = lax.axis_index(axis)
    barrier = pltpu.get_barrier_semaphore()
    for k in range(1, n):
        pl.semaphore_signal(barrier, inc=1, device_id={axis: lax.rem(me + k, n)}, device_id_type=MESH)
    pl.semaphore_wait(barrier, n - 1)
    local = pltpu.make_async_copy(x_ref.at[me], y_ref.at[me], local_sem)
    local.start()
    copies = []
    for k in range(1, n):
        peer = lax.rem(me + k, n)
        copy = pltpu.make_async_remote_copy(
            src_ref=x_ref.at[peer],
            dst_ref=y_ref.at[me],
            send_sem=send_sem.at[k],
            recv_sem=recv_sem.at[k],
            device_id={axis: peer},
            device_id_type=MESH,
        )
        copy.start()
        copies.append(copy)
    for copy in copies:
        copy.wait()
    local.wait()


def exchange(x, axis, collective):
    n = lax.axis_size(axis)
    return pl.pallas_call(
        functools.partial(exchange_kernel, axis, n),
        out_shape=jax.ShapeDtypeStruct(x.shape, x.dtype),
        in_specs=[pl.BlockSpec(memory_space=pl.ANY)],
        out_specs=pl.BlockSpec(memory_space=pl.ANY),
        scratch_shapes=[
            pltpu.SemaphoreType.DMA((n,)),
            pltpu.SemaphoreType.DMA((n,)),
            pltpu.SemaphoreType.DMA(()),
        ],
        compiler_params=pltpu.CompilerParams(collective_id=collective, has_side_effects=True),
    )(x)


def split_product(form, wide, narrow):
    hi = wide.astype(jnp.bfloat16)
    lo = (wide - hi.astype(jnp.float32)).astype(jnp.bfloat16)
    return product(form, hi, narrow) + product(form, lo, narrow)


def shards(
    user_pred,
    user_imp,
    item_pred,
    item_imp,
    uno_user,
    uno_item,
    obs_user,
    obs_item,
    obs_count,
    obs_label,
    obs_prop,
):
    item_ways = lax.axis_size("item")
    user_ways = lax.axis_size("user")
    tile = obs_label.shape[-1]
    rank = user_pred.shape[1]
    user_rows = user_pred.shape[0]
    shard_rows = item_pred.shape[0]
    user_blocks = user_rows // tile
    item_blocks = shard_rows // tile
    n_blocks = user_blocks * item_blocks
    obs_slots = obs_user.shape[-1] // item_ways

    uno_pos = (uno_user * item_blocks + uno_item).reshape(item_ways, -1)
    uno_counts = jnp.sum(
        (uno_pos[:, :, None] == jnp.arange(n_blocks, dtype=jnp.int32)).astype(jnp.float32), axis=1
    )
    obs_pos = (obs_user * item_blocks + obs_item).reshape(item_ways, obs_slots)
    place = jnp.arange(obs_slots, dtype=jnp.int32)
    valid = (place[None, :] < obs_count.reshape(item_ways, 1)).astype(jnp.float32)
    meta = jnp.zeros((item_ways, META_ROWS, tile), jnp.float32)
    meta = meta.at[:, 0, :n_blocks].set(uno_counts)
    meta = meta.at[:, 1, :obs_slots].set(obs_pos.astype(jnp.float32))
    meta = meta.at[:, 2, :obs_slots].set(valid)
    labels = obs_label.reshape(item_ways, obs_slots * tile, tile).astype(jnp.bfloat16)
    propens = obs_prop.reshape(item_ways, obs_slots * tile, tile)
    package = jnp.concatenate([labels, propens, meta.astype(jnp.bfloat16)], axis=1)
    got = exchange(package, "item", 0)
    got_labels = got[:, : obs_slots * tile].reshape(item_ways * obs_slots, tile, tile)
    got_props = got[:, obs_slots * tile : 2 * obs_slots * tile].reshape(item_ways * obs_slots, tile, tile)
    got_meta = got[:, 2 * obs_slots * tile :].astype(jnp.float32)
    counts = jnp.sum(got_meta[:, 0, :n_blocks], axis=0)
    tile_pos = got_meta[:, 1, :obs_slots].reshape(-1).astype(jnp.int32)
    tile_valid = got_meta[:, 2, :obs_slots].reshape(-1)

    logits = product("ar,br->ab", user_pred, item_pred)
    imputed = product("ar,br->ab", user_imp, item_imp)

    def blocked(x):
        return x.reshape(user_blocks, tile, item_blocks, tile).transpose(0, 2, 1, 3).reshape(n_blocks, tile, tile)

    def unblocked(x):
        return x.reshape(user_blocks, item_blocks, tile, tile).transpose(0, 2, 1, 3).reshape(user_rows, shard_rows)

    logit_blocks = blocked(logits)
    imputed_blocks = blocked(imputed)
    uno_grads = ((jax.nn.sigmoid(logit_blocks) - jax.nn.sigmoid(imputed_blocks)) * loss_weight).astype(jnp.bfloat16)

    ologits = logit_blocks[tile_pos]
    predicted = jax.nn.sigmoid(ologits)
    imputes = jax.nn.sigmoid(imputed_blocks[tile_pos])
    tvalid = tile_valid[:, None, None]
    seen = (got_labels > 0).astype(jnp.float32)
    clicks = (got_labels == 2).astype(jnp.float32)
    weight = tvalid * seen / got_props.astype(jnp.float32)
    ograds = ((tvalid * (predicted - imputes) + weight * (imputes - clicks)) * loss_weight).astype(jnp.bfloat16)
    ohgrads = (
        2.0 * weight * (imputes - clicks) * ologits * ologits * imputes * (1.0 - imputes) * loss_weight
    ).astype(jnp.bfloat16)
    onehot = (tile_pos[:, None] == jnp.arange(n_blocks, dtype=jnp.int32)[None, :]).astype(jnp.bfloat16)
    grad_blocks = counts[:, None, None] * uno_grads.astype(jnp.float32) + product("tk,tab->kab", onehot, ograds)
    hgrad_blocks = product("tk,tab->kab", onehot, ohgrads)
    grad_full = unblocked(grad_blocks)
    hgrad_full = unblocked(hgrad_blocks)

    user_part = jnp.stack(
        [split_product("ab,br->ar", grad_full, item_pred), split_product("ab,br->ar", hgrad_full, item_imp)]
    )
    item_part = jnp.stack(
        [split_product("ab,ar->br", grad_full, user_pred), split_product("ab,ar->br", hgrad_full, user_imp)]
    )

    user_chunks = user_part.reshape(2, item_ways, user_rows // item_ways, rank).transpose(1, 0, 2, 3)
    user_got = exchange(user_chunks, "item", 1)
    user_share = jnp.sum(user_got, axis=0)
    item_chunks = item_part.reshape(2, user_ways, shard_rows // user_ways, rank).transpose(1, 0, 2, 3)
    item_got = exchange(item_chunks, "user", 2)
    item_share = jnp.sum(item_got, axis=0)
    return (user_share[0], user_share[1], item_share[0], item_share[1])


def solution(mesh):
    in_specs = (
        P("user", None),
        P("user", None),
        P("item", None),
        P("item", None),
        P("user", "item", None),
        P("user", "item", None),
        P("user", "item", None),
        P("user", "item", None),
        P("user", "item", None),
        P("user", "item", None, None, None),
        P("user", "item", None, None, None),
    )
    out_specs = (
        P(("user", "item"), None),
        P(("user", "item"), None),
        P(("item", "user"), None),
        P(("item", "user"), None),
    )
    return jax.shard_map(shards, mesh=mesh, in_specs=in_specs, out_specs=out_specs, check_vma=False)
```

```python
import functools

import jax
import jax.numpy as jnp
from jax import lax
from jax.experimental import pallas as pl
from jax.experimental.pallas import tpu as pltpu
from jax.sharding import PartitionSpec as P

MESH = pl.DeviceIdType.MESH

loss_weight = 0.015625
META_ROWS = 8


def product(form, first, second):
    return jnp.einsum(form, first, second, preferred_element_type=jnp.float32)


def exchange_kernel(axes, *refs):
    count = len(axes)
    x_refs, y_refs = refs[:count], refs[count : 2 * count]
    send_sem, recv_sem, local_sem = refs[2 * count :]
    barrier = pltpu.get_barrier_semaphore()
    for axis in axes:
        n = lax.axis_size(axis)
        me = lax.axis_index(axis)
        for k in range(1, n):
            pl.semaphore_signal(barrier, inc=1, device_id={axis: lax.rem(me + k, n)}, device_id_type=MESH)
    pl.semaphore_wait(barrier, sum(lax.axis_size(axis) - 1 for axis in axes))
    copies = []
    slot = 0
    for which, axis in enumerate(axes):
        n = lax.axis_size(axis)
        me = lax.axis_index(axis)
        x_ref, y_ref = x_refs[which], y_refs[which]
        local = pltpu.make_async_copy(x_ref.at[me], y_ref.at[me], local_sem.at[which])
        local.start()
        copies.append(local)
        for k in range(1, n):
            peer = lax.rem(me + k, n)
            copy = pltpu.make_async_remote_copy(
                src_ref=x_ref.at[peer],
                dst_ref=y_ref.at[me],
                send_sem=send_sem.at[slot],
                recv_sem=recv_sem.at[slot],
                device_id={axis: peer},
                device_id_type=MESH,
            )
            copy.start()
            copies.append(copy)
            slot += 1
    for copy in copies:
        copy.wait()


def exchange(pairs, collective):
    axes = tuple(axis for _, axis in pairs)
    arrays = [x for x, _ in pairs]
    slots = sum(lax.axis_size(axis) - 1 for axis in axes)
    return pl.pallas_call(
        functools.partial(exchange_kernel, axes),
        out_shape=[jax.ShapeDtypeStruct(x.shape, x.dtype) for x in arrays],
        in_specs=[pl.BlockSpec(memory_space=pl.ANY)] * len(arrays),
        out_specs=[pl.BlockSpec(memory_space=pl.ANY)] * len(arrays),
        scratch_shapes=[
            pltpu.SemaphoreType.DMA((slots,)),
            pltpu.SemaphoreType.DMA((slots,)),
            pltpu.SemaphoreType.DMA((len(arrays),)),
        ],
        compiler_params=pltpu.CompilerParams(collective_id=collective, has_side_effects=True),
    )(*arrays)


def split_product(form, wide, narrow):
    hi = wide.astype(jnp.bfloat16)
    lo = (wide - hi.astype(jnp.float32)).astype(jnp.bfloat16)
    return product(form, hi, narrow) + product(form, lo, narrow)


def shards(
    user_pred,
    user_imp,
    item_pred,
    item_imp,
    uno_user,
    uno_item,
    obs_user,
    obs_item,
    obs_count,
    obs_label,
    obs_prop,
):
    item_ways = lax.axis_size("item")
    user_ways = lax.axis_size("user")
    tile = obs_label.shape[-1]
    rank = user_pred.shape[1]
    user_rows = user_pred.shape[0]
    shard_rows = item_pred.shape[0]
    user_blocks = user_rows // tile
    item_blocks = shard_rows // tile
    n_blocks = user_blocks * item_blocks
    obs_slots = obs_user.shape[-1] // item_ways

    uno_pos = (uno_user * item_blocks + uno_item).reshape(item_ways, -1)
    uno_counts = jnp.sum(
        (uno_pos[:, :, None] == jnp.arange(n_blocks, dtype=jnp.int32)).astype(jnp.float32), axis=1
    )
    obs_pos = (obs_user * item_blocks + obs_item).reshape(item_ways, obs_slots)
    place = jnp.arange(obs_slots, dtype=jnp.int32)
    valid = (place[None, :] < obs_count.reshape(item_ways, 1)).astype(jnp.float32)
    meta = jnp.zeros((item_ways, META_ROWS, tile), jnp.float32)
    meta = meta.at[:, 0, :n_blocks].set(uno_counts)
    meta = meta.at[:, 1, :obs_slots].set(obs_pos.astype(jnp.float32))
    meta = meta.at[:, 2, :obs_slots].set(valid)
    labels = obs_label.reshape(item_ways, obs_slots * tile, tile).astype(jnp.bfloat16)
    propens = obs_prop.reshape(item_ways, obs_slots * tile, tile)
    package = jnp.concatenate([labels, propens, meta.astype(jnp.bfloat16)], axis=1)
    (got,) = exchange([(package, "item")], 0)
    got_labels = got[:, : obs_slots * tile].reshape(item_ways * obs_slots, tile, tile)
    got_props = got[:, obs_slots * tile : 2 * obs_slots * tile].reshape(item_ways * obs_slots, tile, tile)
    got_meta = got[:, 2 * obs_slots * tile :].astype(jnp.float32)
    counts = jnp.sum(got_meta[:, 0, :n_blocks], axis=0)
    tile_pos = got_meta[:, 1, :obs_slots].reshape(-1).astype(jnp.int32)
    tile_valid = got_meta[:, 2, :obs_slots].reshape(-1)

    logits = product("ar,br->ab", user_pred, item_pred)
    imputed = product("ar,br->ab", user_imp, item_imp)

    def blocked(x):
        return x.reshape(user_blocks, tile, item_blocks, tile).transpose(0, 2, 1, 3).reshape(n_blocks, tile, tile)

    def unblocked(x):
        return x.reshape(user_blocks, item_blocks, tile, tile).transpose(0, 2, 1, 3).reshape(user_rows, shard_rows)

    logit_blocks = blocked(logits)
    imputed_blocks = blocked(imputed)
    uno_grads = ((jax.nn.sigmoid(logit_blocks) - jax.nn.sigmoid(imputed_blocks)) * loss_weight).astype(jnp.bfloat16)

    ologits = logit_blocks[tile_pos]
    predicted = jax.nn.sigmoid(ologits)
    imputes = jax.nn.sigmoid(imputed_blocks[tile_pos])
    tvalid = tile_valid[:, None, None]
    seen = (got_labels > 0).astype(jnp.float32)
    clicks = (got_labels == 2).astype(jnp.float32)
    weight = tvalid * seen / got_props.astype(jnp.float32)
    ograds = ((tvalid * (predicted - imputes) + weight * (imputes - clicks)) * loss_weight).astype(jnp.bfloat16)
    ohgrads = (
        2.0 * weight * (imputes - clicks) * ologits * ologits * imputes * (1.0 - imputes) * loss_weight
    ).astype(jnp.bfloat16)
    onehot = (tile_pos[:, None] == jnp.arange(n_blocks, dtype=jnp.int32)[None, :]).astype(jnp.bfloat16)
    grad_blocks = counts[:, None, None] * uno_grads.astype(jnp.float32) + product("tk,tab->kab", onehot, ograds)
    hgrad_blocks = product("tk,tab->kab", onehot, ohgrads)
    grad_full = unblocked(grad_blocks)
    hgrad_full = unblocked(hgrad_blocks)

    user_part = jnp.stack(
        [split_product("ab,br->ar", grad_full, item_pred), split_product("ab,br->ar", hgrad_full, item_imp)]
    )
    item_part = jnp.stack(
        [split_product("ab,ar->br", grad_full, user_pred), split_product("ab,ar->br", hgrad_full, user_imp)]
    )

    user_chunks = user_part.reshape(2, item_ways, user_rows // item_ways, rank).transpose(1, 0, 2, 3)
    item_chunks = item_part.reshape(2, user_ways, shard_rows // user_ways, rank).transpose(1, 0, 2, 3)
    user_got, item_got = exchange([(user_chunks, "item"), (item_chunks, "user")], 1)
    user_share = jnp.sum(user_got, axis=0)
    item_share = jnp.sum(item_got, axis=0)
    return (user_share[0], user_share[1], item_share[0], item_share[1])


def solution(mesh):
    in_specs = (
        P("user", None),
        P("user", None),
        P("item", None),
        P("item", None),
        P("user", "item", None),
        P("user", "item", None),
        P("user", "item", None),
        P("user", "item", None),
        P("user", "item", None),
        P("user", "item", None, None, None),
        P("user", "item", None, None, None),
    )
    out_specs = (
        P(("user", "item"), None),
        P(("user", "item"), None),
        P(("item", "user"), None),
        P(("item", "user"), None),
    )
    return jax.shard_map(shards, mesh=mesh, in_specs=in_specs, out_specs=out_specs, check_vma=False)
```

```python
import functools

import jax
import jax.numpy as jnp
from jax import lax
from jax.experimental import pallas as pl
from jax.experimental.pallas import tpu as pltpu
from jax.sharding import PartitionSpec as P

MESH = pl.DeviceIdType.MESH

loss_weight = 0.015625
META_ROWS = 8


def product(form, first, second):
    return jnp.einsum(form, first, second, preferred_element_type=jnp.float32)


def dense_blocks(tile, item_blocks, up_ref, ui_ref, vp_ref, vi_ref, s_ref, m_ref, d_ref):
    def block(k, carry):
        users = pl.ds(pl.multiple_of((k // item_blocks) * tile, tile), tile)
        items = pl.ds(pl.multiple_of((k % item_blocks) * tile, tile), tile)
        dims = (((1,), (1,)), ((), ()))
        logits = lax.dot_general(up_ref[users, :], vp_ref[items, :], dims, preferred_element_type=jnp.float32)
        imputed = lax.dot_general(ui_ref[users, :], vi_ref[items, :], dims, preferred_element_type=jnp.float32)
        s_ref[k] = logits
        m_ref[k] = imputed
        d_ref[k] = ((jax.nn.sigmoid(logits) - jax.nn.sigmoid(imputed)) * loss_weight).astype(d_ref.dtype)
        return carry

    lax.fori_loop(0, s_ref.shape[0], block, 0)


def exchange_kernel(axes, count, work_in, work, *refs):
    x_refs, y_refs = refs[:count], refs[count + work_in : 2 * count + work_in]
    send_sem, recv_sem, local_sem = refs[-3:]
    work_refs = refs[count : count + work_in] + refs[2 * count + work_in : -3]
    barrier = pltpu.get_barrier_semaphore()
    for axis in axes:
        n = lax.axis_size(axis)
        me = lax.axis_index(axis)
        for k in range(1, n):
            pl.semaphore_signal(barrier, inc=1, device_id={axis: lax.rem(me + k, n)}, device_id_type=MESH)
    pl.semaphore_wait(barrier, sum(lax.axis_size(axis) - 1 for axis in axes))
    copies = []
    slot = 0
    for which, axis in enumerate(axes):
        n = lax.axis_size(axis)
        me = lax.axis_index(axis)
        x_ref, y_ref = x_refs[which], y_refs[which]
        local = pltpu.make_async_copy(x_ref.at[me], y_ref.at[me], local_sem.at[which])
        local.start()
        copies.append(local)
        for k in range(1, n):
            peer = lax.rem(me + k, n)
            copy = pltpu.make_async_remote_copy(
                src_ref=x_ref.at[peer],
                dst_ref=y_ref.at[me],
                send_sem=send_sem.at[slot],
                recv_sem=recv_sem.at[slot],
                device_id={axis: peer},
                device_id_type=MESH,
            )
            copy.start()
            copies.append(copy)
            slot += 1
    if work is not None:
        work(*work_refs)
    for copy in copies:
        copy.wait()


def exchange(pairs, collective, work=None, work_inputs=(), work_outputs=()):
    axes = tuple(axis for _, axis in pairs)
    arrays = [x for x, _ in pairs]
    slots = sum(lax.axis_size(axis) - 1 for axis in axes)
    vmem = pl.BlockSpec(memory_space=pltpu.VMEM)
    return pl.pallas_call(
        functools.partial(exchange_kernel, axes, len(arrays), len(work_inputs), work),
        out_shape=[jax.ShapeDtypeStruct(x.shape, x.dtype) for x in arrays] + list(work_outputs),
        in_specs=[pl.BlockSpec(memory_space=pl.ANY)] * len(arrays) + [vmem] * len(work_inputs),
        out_specs=[pl.BlockSpec(memory_space=pl.ANY)] * len(arrays) + [vmem] * len(work_outputs),
        scratch_shapes=[
            pltpu.SemaphoreType.DMA((slots,)),
            pltpu.SemaphoreType.DMA((slots,)),
            pltpu.SemaphoreType.DMA((len(arrays),)),
        ],
        compiler_params=pltpu.CompilerParams(collective_id=collective, has_side_effects=True),
    )(*arrays, *work_inputs)


def split_product(form, wide, narrow):
    hi = wide.astype(jnp.bfloat16)
    lo = (wide - hi.astype(jnp.float32)).astype(jnp.bfloat16)
    return product(form, hi, narrow) + product(form, lo, narrow)


def shards(
    user_pred,
    user_imp,
    item_pred,
    item_imp,
    uno_user,
    uno_item,
    obs_user,
    obs_item,
    obs_count,
    obs_label,
    obs_prop,
):
    item_ways = lax.axis_size("item")
    user_ways = lax.axis_size("user")
    tile = obs_label.shape[-1]
    rank = user_pred.shape[1]
    user_rows = user_pred.shape[0]
    shard_rows = item_pred.shape[0]
    user_blocks = user_rows // tile
    item_blocks = shard_rows // tile
    n_blocks = user_blocks * item_blocks
    obs_slots = obs_user.shape[-1] // item_ways

    uno_pos = (uno_user * item_blocks + uno_item).reshape(item_ways, -1)
    uno_counts = jnp.sum(
        (uno_pos[:, :, None] == jnp.arange(n_blocks, dtype=jnp.int32)).astype(jnp.float32), axis=1
    )
    obs_pos = (obs_user * item_blocks + obs_item).reshape(item_ways, obs_slots)
    place = jnp.arange(obs_slots, dtype=jnp.int32)
    valid = (place[None, :] < obs_count.reshape(item_ways, 1)).astype(jnp.float32)
    meta = jnp.zeros((item_ways, META_ROWS, tile), jnp.float32)
    meta = meta.at[:, 0, :n_blocks].set(uno_counts)
    meta = meta.at[:, 1, :obs_slots].set(obs_pos.astype(jnp.float32))
    meta = meta.at[:, 2, :obs_slots].set(valid)
    labels = obs_label.reshape(item_ways, obs_slots * tile, tile).astype(jnp.bfloat16)
    propens = obs_prop.reshape(item_ways, obs_slots * tile, tile)
    package = jnp.concatenate([labels, propens, meta.astype(jnp.bfloat16)], axis=1)
    block_shape = (n_blocks, tile, tile)
    got, logit_blocks, imputed_blocks, uno_grads = exchange(
        [(package, "item")],
        0,
        functools.partial(dense_blocks, tile, item_blocks),
        (user_pred, user_imp, item_pred, item_imp),
        (
            jax.ShapeDtypeStruct(block_shape, jnp.float32),
            jax.ShapeDtypeStruct(block_shape, jnp.float32),
            jax.ShapeDtypeStruct(block_shape, jnp.bfloat16),
        ),
    )
    got_labels = got[:, : obs_slots * tile].reshape(item_ways * obs_slots, tile, tile)
    got_props = got[:, obs_slots * tile : 2 * obs_slots * tile].reshape(item_ways * obs_slots, tile, tile)
    got_meta = got[:, 2 * obs_slots * tile :].astype(jnp.float32)
    counts = jnp.sum(got_meta[:, 0, :n_blocks], axis=0)
    tile_pos = got_meta[:, 1, :obs_slots].reshape(-1).astype(jnp.int32)
    tile_valid = got_meta[:, 2, :obs_slots].reshape(-1)

    def unblocked(x):
        return x.reshape(user_blocks, item_blocks, tile, tile).transpose(0, 2, 1, 3).reshape(user_rows, shard_rows)

    ologits = logit_blocks[tile_pos]
    predicted = jax.nn.sigmoid(ologits)
    imputes = jax.nn.sigmoid(imputed_blocks[tile_pos])
    tvalid = tile_valid[:, None, None]
    seen = (got_labels > 0).astype(jnp.float32)
    clicks = (got_labels == 2).astype(jnp.float32)
    weight = tvalid * seen / got_props.astype(jnp.float32)
    ograds = ((tvalid * (predicted - imputes) + weight * (imputes - clicks)) * loss_weight).astype(jnp.bfloat16)
    ohgrads = (
        2.0 * weight * (imputes - clicks) * ologits * ologits * imputes * (1.0 - imputes) * loss_weight
    ).astype(jnp.bfloat16)
    onehot = (tile_pos[:, None] == jnp.arange(n_blocks, dtype=jnp.int32)[None, :]).astype(jnp.bfloat16)
    grad_blocks = counts[:, None, None] * uno_grads.astype(jnp.float32) + product("tk,tab->kab", onehot, ograds)
    hgrad_blocks = product("tk,tab->kab", onehot, ohgrads)
    grad_full = unblocked(grad_blocks)
    hgrad_full = unblocked(hgrad_blocks)

    user_part = jnp.stack(
        [split_product("ab,br->ar", grad_full, item_pred), split_product("ab,br->ar", hgrad_full, item_imp)]
    )
    item_part = jnp.stack(
        [split_product("ab,ar->br", grad_full, user_pred), split_product("ab,ar->br", hgrad_full, user_imp)]
    )

    user_chunks = user_part.reshape(2, item_ways, user_rows // item_ways, rank).transpose(1, 0, 2, 3)
    item_chunks = item_part.reshape(2, user_ways, shard_rows // user_ways, rank).transpose(1, 0, 2, 3)
    user_got, item_got = exchange([(user_chunks, "item"), (item_chunks, "user")], 1)
    user_share = jnp.sum(user_got, axis=0)
    item_share = jnp.sum(item_got, axis=0)
    return (user_share[0], user_share[1], item_share[0], item_share[1])


def solution(mesh):
    in_specs = (
        P("user", None),
        P("user", None),
        P("item", None),
        P("item", None),
        P("user", "item", None),
        P("user", "item", None),
        P("user", "item", None),
        P("user", "item", None),
        P("user", "item", None),
        P("user", "item", None, None, None),
        P("user", "item", None, None, None),
    )
    out_specs = (
        P(("user", "item"), None),
        P(("user", "item"), None),
        P(("item", "user"), None),
        P(("item", "user"), None),
    )
    return jax.shard_map(shards, mesh=mesh, in_specs=in_specs, out_specs=out_specs, check_vma=False)
```

```python
import functools

import jax
import jax.numpy as jnp
from jax import lax
from jax.experimental import pallas as pl
from jax.experimental.pallas import tpu as pltpu
from jax.sharding import PartitionSpec as P

MESH = pl.DeviceIdType.MESH

loss_weight = 0.015625
META_ROWS = 8


def product(form, first, second):
    return jnp.einsum(form, first, second, preferred_element_type=jnp.float32)


def dense_blocks(tile, item_blocks, up_ref, ui_ref, vp_ref, vi_ref, s_ref, m_ref, d_ref):
    def block(k, carry):
        users = pl.ds(pl.multiple_of((k // item_blocks) * tile, tile), tile)
        items = pl.ds(pl.multiple_of((k % item_blocks) * tile, tile), tile)
        dims = (((1,), (1,)), ((), ()))
        logits = lax.dot_general(up_ref[users, :], vp_ref[items, :], dims, preferred_element_type=jnp.float32)
        imputed = lax.dot_general(ui_ref[users, :], vi_ref[items, :], dims, preferred_element_type=jnp.float32)
        s_ref[k] = logits
        m_ref[k] = imputed
        d_ref[k] = ((jax.nn.sigmoid(logits) - jax.nn.sigmoid(imputed)) * loss_weight).astype(d_ref.dtype)
        return carry

    lax.fori_loop(0, s_ref.shape[0], block, 0)


def exchange_kernel(axes, count, work_in, work, *refs):
    x_refs, y_refs = refs[:count], refs[count + work_in : 2 * count + work_in]
    send_sem, recv_sem, local_sem = refs[-3:]
    work_refs = refs[count : count + work_in] + refs[2 * count + work_in : -3]
    barrier = pltpu.get_barrier_semaphore()
    for axis in axes:
        n = lax.axis_size(axis)
        me = lax.axis_index(axis)
        for k in range(1, n):
            pl.semaphore_signal(barrier, inc=1, device_id={axis: lax.rem(me + k, n)}, device_id_type=MESH)
    pl.semaphore_wait(barrier, sum(lax.axis_size(axis) - 1 for axis in axes))
    copies = []
    slot = 0
    for which, axis in enumerate(axes):
        n = lax.axis_size(axis)
        me = lax.axis_index(axis)
        x_ref, y_ref = x_refs[which], y_refs[which]
        local = pltpu.make_async_copy(x_ref.at[me], y_ref.at[me], local_sem.at[which])
        local.start()
        copies.append(local)
        for k in range(1, n):
            peer = lax.rem(me + k, n)
            copy = pltpu.make_async_remote_copy(
                src_ref=x_ref.at[peer],
                dst_ref=y_ref.at[me],
                send_sem=send_sem.at[slot],
                recv_sem=recv_sem.at[slot],
                device_id={axis: peer},
                device_id_type=MESH,
            )
            copy.start()
            copies.append(copy)
            slot += 1
    if work is not None:
        work(*work_refs)
    for copy in copies:
        copy.wait()


def exchange(pairs, collective, work=None, work_inputs=(), work_outputs=()):
    axes = tuple(axis for _, axis in pairs)
    arrays = [x for x, _ in pairs]
    slots = sum(lax.axis_size(axis) - 1 for axis in axes)
    vmem = pl.BlockSpec(memory_space=pltpu.VMEM)
    return pl.pallas_call(
        functools.partial(exchange_kernel, axes, len(arrays), len(work_inputs), work),
        out_shape=[jax.ShapeDtypeStruct(x.shape, x.dtype) for x in arrays] + list(work_outputs),
        in_specs=[pl.BlockSpec(memory_space=pl.ANY)] * len(arrays) + [vmem] * len(work_inputs),
        out_specs=[pl.BlockSpec(memory_space=pl.ANY)] * len(arrays) + [vmem] * len(work_outputs),
        scratch_shapes=[
            pltpu.SemaphoreType.DMA((slots,)),
            pltpu.SemaphoreType.DMA((slots,)),
            pltpu.SemaphoreType.DMA((len(arrays),)),
        ],
        compiler_params=pltpu.CompilerParams(collective_id=collective, has_side_effects=True),
    )(*arrays, *work_inputs)


def tile_kernel(
    tile, user_blocks, item_blocks, n_tiles, obs_slots,
    pos_ref, count_ref, valid_ref,
    s_ref, m_ref, d_ref, got_ref, up_ref, ui_ref, vp_ref, vi_ref,
    user_out, item_out,
    g_acc, h_acc, user_acc, item_acc,
):
    n_blocks = user_blocks * item_blocks
    for k in range(n_blocks):
        g_acc[k] = count_ref[k] * d_ref[k].astype(jnp.float32)
        h_acc[k] = jnp.zeros((tile, tile), jnp.float32)

    def observed(t, carry):
        pos = pos_ref[t]
        valid = valid_ref[t]
        ologits = s_ref[pos]
        predicted = jax.nn.sigmoid(ologits)
        imputes = jax.nn.sigmoid(m_ref[pos])
        origin = t // obs_slots
        slot = t % obs_slots
        labels = got_ref[origin, pl.ds(slot * tile, tile), :].astype(jnp.float32)
        propens = got_ref[origin, pl.ds((obs_slots + slot) * tile, tile), :].astype(jnp.float32)
        seen = (labels > 0).astype(jnp.float32)
        clicks = (labels == 2).astype(jnp.float32)
        weight = valid * seen / propens
        ograds = ((valid * (predicted - imputes) + weight * (imputes - clicks)) * loss_weight).astype(jnp.bfloat16)
        ohgrads = (
            2.0 * weight * (imputes - clicks) * ologits * ologits * imputes * (1.0 - imputes) * loss_weight
        ).astype(jnp.bfloat16)
        g_acc[pos] += ograds.astype(jnp.float32)
        h_acc[pos] += ohgrads.astype(jnp.float32)
        return carry

    lax.fori_loop(0, n_tiles, observed, 0)

    user_acc[...] = jnp.zeros(user_acc.shape, jnp.float32)
    item_acc[...] = jnp.zeros(item_acc.shape, jnp.float32)
    forward = (((1,), (0,)), ((), ()))
    backward = (((0,), (0,)), ((), ()))
    for ub in range(user_blocks):
        users = pl.ds(ub * tile, tile)
        for ib in range(item_blocks):
            items = pl.ds(ib * tile, tile)
            k = ub * item_blocks + ib
            for model, acc, u_ref, v_ref in ((0, g_acc, up_ref, vp_ref), (1, h_acc, ui_ref, vi_ref)):
                wide = acc[k]
                hi = wide.astype(jnp.bfloat16)
                lo = (wide - hi.astype(jnp.float32)).astype(jnp.bfloat16)
                v = v_ref[items, :]
                u = u_ref[users, :]
                user_acc[model, users, :] += lax.dot_general(
                    hi, v, forward, preferred_element_type=jnp.float32
                ) + lax.dot_general(lo, v, forward, preferred_element_type=jnp.float32)
                item_acc[model, items, :] += lax.dot_general(
                    hi, u, backward, preferred_element_type=jnp.float32
                ) + lax.dot_general(lo, u, backward, preferred_element_type=jnp.float32)
    user_rows = user_out.shape[2]
    for dest in range(user_out.shape[0]):
        user_out[dest] = user_acc[:, pl.ds(dest * user_rows, user_rows), :]
    item_rows = item_out.shape[2]
    for dest in range(item_out.shape[0]):
        item_out[dest] = item_acc[:, pl.ds(dest * item_rows, item_rows), :]


def shards(
    user_pred,
    user_imp,
    item_pred,
    item_imp,
    uno_user,
    uno_item,
    obs_user,
    obs_item,
    obs_count,
    obs_label,
    obs_prop,
):
    item_ways = lax.axis_size("item")
    user_ways = lax.axis_size("user")
    tile = obs_label.shape[-1]
    rank = user_pred.shape[1]
    user_rows = user_pred.shape[0]
    shard_rows = item_pred.shape[0]
    user_blocks = user_rows // tile
    item_blocks = shard_rows // tile
    n_blocks = user_blocks * item_blocks
    obs_slots = obs_user.shape[-1] // item_ways

    uno_pos = (uno_user * item_blocks + uno_item).reshape(item_ways, -1)
    uno_counts = jnp.sum(
        (uno_pos[:, :, None] == jnp.arange(n_blocks, dtype=jnp.int32)).astype(jnp.float32), axis=1
    )
    obs_pos = (obs_user * item_blocks + obs_item).reshape(item_ways, obs_slots)
    place = jnp.arange(obs_slots, dtype=jnp.int32)
    valid = (place[None, :] < obs_count.reshape(item_ways, 1)).astype(jnp.float32)
    meta = jnp.zeros((item_ways, META_ROWS, tile), jnp.float32)
    meta = meta.at[:, 0, :n_blocks].set(uno_counts)
    meta = meta.at[:, 1, :obs_slots].set(obs_pos.astype(jnp.float32))
    meta = meta.at[:, 2, :obs_slots].set(valid)
    labels = obs_label.reshape(item_ways, obs_slots * tile, tile).astype(jnp.bfloat16)
    propens = obs_prop.reshape(item_ways, obs_slots * tile, tile)
    package = jnp.concatenate([labels, propens, meta.astype(jnp.bfloat16)], axis=1)
    block_shape = (n_blocks, tile, tile)
    got, logit_blocks, imputed_blocks, uno_grads = exchange(
        [(package, "item")],
        0,
        functools.partial(dense_blocks, tile, item_blocks),
        (user_pred, user_imp, item_pred, item_imp),
        (
            jax.ShapeDtypeStruct(block_shape, jnp.float32),
            jax.ShapeDtypeStruct(block_shape, jnp.float32),
            jax.ShapeDtypeStruct(block_shape, jnp.bfloat16),
        ),
    )
    got_meta = got[:, 2 * obs_slots * tile :].astype(jnp.float32)
    counts = jnp.sum(got_meta[:, 0, :n_blocks], axis=0)
    tile_pos = got_meta[:, 1, :obs_slots].reshape(-1).astype(jnp.int32)
    tile_valid = got_meta[:, 2, :obs_slots].reshape(-1)

    vmem = pl.BlockSpec(memory_space=pltpu.VMEM)
    smem = pl.BlockSpec(memory_space=pltpu.SMEM)
    user_chunks, item_chunks = pl.pallas_call(
        functools.partial(tile_kernel, tile, user_blocks, item_blocks, item_ways * obs_slots, obs_slots),
        out_shape=[
            jax.ShapeDtypeStruct((item_ways, 2, user_rows // item_ways, rank), jnp.float32),
            jax.ShapeDtypeStruct((user_ways, 2, shard_rows // user_ways, rank), jnp.float32),
        ],
        in_specs=[smem] * 3 + [vmem] * 8,
        out_specs=[vmem, vmem],
        scratch_shapes=[
            pltpu.VMEM((n_blocks, tile, tile), jnp.float32),
            pltpu.VMEM((n_blocks, tile, tile), jnp.float32),
            pltpu.VMEM((2, user_rows, rank), jnp.float32),
            pltpu.VMEM((2, shard_rows, rank), jnp.float32),
        ],
    )(
        tile_pos, counts, tile_valid,
        logit_blocks, imputed_blocks, uno_grads, got, user_pred, user_imp, item_pred, item_imp,
    )
    user_got, item_got = exchange([(user_chunks, "item"), (item_chunks, "user")], 1)
    user_share = jnp.sum(user_got, axis=0)
    item_share = jnp.sum(item_got, axis=0)
    return (user_share[0], user_share[1], item_share[0], item_share[1])


def solution(mesh):
    in_specs = (
        P("user", None),
        P("user", None),
        P("item", None),
        P("item", None),
        P("user", "item", None),
        P("user", "item", None),
        P("user", "item", None),
        P("user", "item", None),
        P("user", "item", None),
        P("user", "item", None, None, None),
        P("user", "item", None, None, None),
    )
    out_specs = (
        P(("user", "item"), None),
        P(("user", "item"), None),
        P(("item", "user"), None),
        P(("item", "user"), None),
    )
    return jax.shard_map(shards, mesh=mesh, in_specs=in_specs, out_specs=out_specs, check_vma=False)
```

```python
import functools

import jax
import jax.numpy as jnp
from jax import lax
from jax.experimental import pallas as pl
from jax.experimental.pallas import tpu as pltpu
from jax.sharding import PartitionSpec as P

MESH = pl.DeviceIdType.MESH

loss_weight = 0.015625


def product(form, first, second):
    return jnp.einsum(form, first, second, preferred_element_type=jnp.float32)


def dense_blocks(tile, item_blocks, up_ref, ui_ref, vp_ref, vi_ref, s_ref, m_ref, d_ref):
    def block(k, carry):
        users = pl.ds(pl.multiple_of((k // item_blocks) * tile, tile), tile)
        items = pl.ds(pl.multiple_of((k % item_blocks) * tile, tile), tile)
        dims = (((1,), (1,)), ((), ()))
        logits = lax.dot_general(up_ref[users, :], vp_ref[items, :], dims, preferred_element_type=jnp.float32)
        imputed = lax.dot_general(ui_ref[users, :], vi_ref[items, :], dims, preferred_element_type=jnp.float32)
        s_ref[k] = logits
        m_ref[k] = imputed
        d_ref[k] = ((jax.nn.sigmoid(logits) - jax.nn.sigmoid(imputed)) * loss_weight).astype(d_ref.dtype)
        return carry

    lax.fori_loop(0, s_ref.shape[0], block, 0)


def exchange_kernel(axes, count, work_in, work, *refs):
    x_refs, y_refs = refs[:count], refs[count + work_in : 2 * count + work_in]
    send_sem, recv_sem, local_sem = refs[-3:]
    work_refs = refs[count : count + work_in] + refs[2 * count + work_in : -3]
    barrier = pltpu.get_barrier_semaphore()
    for axis in axes:
        n = lax.axis_size(axis)
        me = lax.axis_index(axis)
        for k in range(1, n):
            pl.semaphore_signal(barrier, inc=1, device_id={axis: lax.rem(me + k, n)}, device_id_type=MESH)
    pl.semaphore_wait(barrier, sum(lax.axis_size(axis) - 1 for axis in axes))
    copies = []
    slot = 0
    for which, axis in enumerate(axes):
        n = lax.axis_size(axis)
        me = lax.axis_index(axis)
        x_ref, y_ref = x_refs[which], y_refs[which]
        local = pltpu.make_async_copy(x_ref.at[me], y_ref.at[me], local_sem.at[which])
        local.start()
        copies.append(local)
        for k in range(1, n):
            peer = lax.rem(me + k, n)
            copy = pltpu.make_async_remote_copy(
                src_ref=x_ref.at[peer],
                dst_ref=y_ref.at[me],
                send_sem=send_sem.at[slot],
                recv_sem=recv_sem.at[slot],
                device_id={axis: peer},
                device_id_type=MESH,
            )
            copy.start()
            copies.append(copy)
            slot += 1
    if work is not None:
        work(*work_refs)
    for copy in copies:
        copy.wait()


def exchange(pairs, collective, work=None, work_inputs=(), work_outputs=()):
    axes = tuple(axis for _, axis in pairs)
    arrays = [x for x, _ in pairs]
    slots = sum(lax.axis_size(axis) - 1 for axis in axes)
    vmem = pl.BlockSpec(memory_space=pltpu.VMEM)
    return pl.pallas_call(
        functools.partial(exchange_kernel, axes, len(arrays), len(work_inputs), work),
        out_shape=[jax.ShapeDtypeStruct(x.shape, x.dtype) for x in arrays] + list(work_outputs),
        in_specs=[pl.BlockSpec(memory_space=pl.ANY)] * len(arrays) + [vmem] * len(work_inputs),
        out_specs=[pl.BlockSpec(memory_space=pl.ANY)] * len(arrays) + [vmem] * len(work_outputs),
        scratch_shapes=[
            pltpu.SemaphoreType.DMA((slots,)),
            pltpu.SemaphoreType.DMA((slots,)),
            pltpu.SemaphoreType.DMA((len(arrays),)),
        ],
        compiler_params=pltpu.CompilerParams(collective_id=collective, has_side_effects=True),
    )(*arrays, *work_inputs)


def reduce_kernel(axes, *refs):
    count = len(axes)
    x_refs, out_refs = refs[:count], refs[count : 2 * count]
    land_refs = refs[2 * count : 3 * count]
    send_sem, recv_sem, local_sem = refs[3 * count :]
    barrier = pltpu.get_barrier_semaphore()
    for axis in axes:
        n = lax.axis_size(axis)
        me = lax.axis_index(axis)
        for k in range(1, n):
            pl.semaphore_signal(barrier, inc=1, device_id={axis: lax.rem(me + k, n)}, device_id_type=MESH)
    pl.semaphore_wait(barrier, sum(lax.axis_size(axis) - 1 for axis in axes))
    copies = []
    slot = 0
    for which, axis in enumerate(axes):
        n = lax.axis_size(axis)
        me = lax.axis_index(axis)
        x_ref, land = x_refs[which], land_refs[which]
        local = pltpu.make_async_copy(x_ref.at[me], land.at[me], local_sem.at[which])
        local.start()
        copies.append(local)
        for k in range(1, n):
            peer = lax.rem(me + k, n)
            copy = pltpu.make_async_remote_copy(
                src_ref=x_ref.at[peer],
                dst_ref=land.at[me],
                send_sem=send_sem.at[slot],
                recv_sem=recv_sem.at[slot],
                device_id={axis: peer},
                device_id_type=MESH,
            )
            copy.start()
            copies.append(copy)
            slot += 1
    for copy in copies:
        copy.wait()
    for which in range(count):
        land = land_refs[which]
        total = land[0]
        for source in range(1, land.shape[0]):
            total = total + land[source]
        out_refs[which][...] = total


def reduce_exchange(pairs, collective):
    axes = tuple(axis for _, axis in pairs)
    arrays = [x for x, _ in pairs]
    slots = sum(lax.axis_size(axis) - 1 for axis in axes)
    return pl.pallas_call(
        functools.partial(reduce_kernel, axes),
        out_shape=[jax.ShapeDtypeStruct(x.shape[1:], x.dtype) for x in arrays],
        in_specs=[pl.BlockSpec(memory_space=pl.ANY)] * len(arrays),
        out_specs=[pl.BlockSpec(memory_space=pltpu.VMEM)] * len(arrays),
        scratch_shapes=[pltpu.VMEM(x.shape, x.dtype) for x in arrays]
        + [
            pltpu.SemaphoreType.DMA((slots,)),
            pltpu.SemaphoreType.DMA((slots,)),
            pltpu.SemaphoreType.DMA((len(arrays),)),
        ],
        compiler_params=pltpu.CompilerParams(collective_id=collective, has_side_effects=True),
    )(*arrays)


def tile_kernel(
    tile, user_blocks, item_blocks, obs_slots,
    meta_ref,
    s_ref, m_ref, d_ref, lab_ref, prop_ref, up_ref, ui_ref, vp_ref, vi_ref,
    user_out, item_out,
    g_acc, h_acc, user_acc, item_acc,
):
    n_blocks = user_blocks * item_blocks
    origins = meta_ref.shape[0]
    for k in range(n_blocks):
        count = meta_ref[0, k]
        for origin in range(1, origins):
            count = count + meta_ref[origin, k]
        g_acc[k] = count.astype(jnp.float32) * d_ref[k].astype(jnp.float32)
        h_acc[k] = jnp.zeros((tile, tile), jnp.float32)

    def observed(t, carry):
        origin = t // obs_slots
        slot = t % obs_slots
        pos = meta_ref[origin, n_blocks + slot]
        valid = meta_ref[origin, n_blocks + obs_slots + slot].astype(jnp.float32)
        ologits = s_ref[pos]
        predicted = jax.nn.sigmoid(ologits)
        imputes = jax.nn.sigmoid(m_ref[pos])
        labels = lab_ref[origin, pl.ds(slot * tile, tile), :].astype(jnp.float32)
        propens = prop_ref[origin, pl.ds(slot * tile, tile), :].astype(jnp.float32)
        seen = (labels > 0).astype(jnp.float32)
        clicks = (labels == 2).astype(jnp.float32)
        weight = valid * seen / propens
        ograds = ((valid * (predicted - imputes) + weight * (imputes - clicks)) * loss_weight).astype(jnp.bfloat16)
        ohgrads = (
            2.0 * weight * (imputes - clicks) * ologits * ologits * imputes * (1.0 - imputes) * loss_weight
        ).astype(jnp.bfloat16)
        g_acc[pos] += ograds.astype(jnp.float32)
        h_acc[pos] += ohgrads.astype(jnp.float32)
        return carry

    lax.fori_loop(0, origins * obs_slots, observed, 0)

    user_acc[...] = jnp.zeros(user_acc.shape, jnp.float32)
    item_acc[...] = jnp.zeros(item_acc.shape, jnp.float32)
    forward = (((1,), (0,)), ((), ()))
    backward = (((0,), (0,)), ((), ()))
    for ub in range(user_blocks):
        users = pl.ds(ub * tile, tile)
        for ib in range(item_blocks):
            items = pl.ds(ib * tile, tile)
            k = ub * item_blocks + ib
            for model, acc, u_ref, v_ref in ((0, g_acc, up_ref, vp_ref), (1, h_acc, ui_ref, vi_ref)):
                wide = acc[k]
                hi = wide.astype(jnp.bfloat16)
                lo = (wide - hi.astype(jnp.float32)).astype(jnp.bfloat16)
                v = v_ref[items, :]
                u = u_ref[users, :]
                user_acc[model, users, :] += lax.dot_general(
                    hi, v, forward, preferred_element_type=jnp.float32
                ) + lax.dot_general(lo, v, forward, preferred_element_type=jnp.float32)
                item_acc[model, items, :] += lax.dot_general(
                    hi, u, backward, preferred_element_type=jnp.float32
                ) + lax.dot_general(lo, u, backward, preferred_element_type=jnp.float32)
    user_rows = user_out.shape[2]
    for dest in range(user_out.shape[0]):
        user_out[dest] = user_acc[:, pl.ds(dest * user_rows, user_rows), :]
    item_rows = item_out.shape[2]
    for dest in range(item_out.shape[0]):
        item_out[dest] = item_acc[:, pl.ds(dest * item_rows, item_rows), :]


def shards(
    user_pred,
    user_imp,
    item_pred,
    item_imp,
    uno_user,
    uno_item,
    obs_user,
    obs_item,
    obs_count,
    obs_label,
    obs_prop,
):
    item_ways = lax.axis_size("item")
    user_ways = lax.axis_size("user")
    tile = obs_label.shape[-1]
    rank = user_pred.shape[1]
    user_rows = user_pred.shape[0]
    shard_rows = item_pred.shape[0]
    user_blocks = user_rows // tile
    item_blocks = shard_rows // tile
    n_blocks = user_blocks * item_blocks
    obs_slots = obs_user.shape[-1] // item_ways

    uno_pos = (uno_user * item_blocks + uno_item).reshape(item_ways, -1)
    uno_counts = jnp.sum((uno_pos[:, :, None] == jnp.arange(n_blocks, dtype=jnp.int32)).astype(jnp.int32), axis=1)
    obs_pos = (obs_user * item_blocks + obs_item).reshape(item_ways, obs_slots)
    place = jnp.arange(obs_slots, dtype=jnp.int32)
    valid = (place[None, :] < obs_count.reshape(item_ways, 1)).astype(jnp.int32)
    meta = jnp.concatenate(
        [uno_counts, obs_pos, valid, jnp.zeros((item_ways, tile - n_blocks - 2 * obs_slots), jnp.int32)], axis=1
    )
    labels = obs_label.reshape(item_ways, obs_slots * tile, tile).astype(jnp.bfloat16)
    propens = obs_prop.reshape(item_ways, obs_slots * tile, tile)
    block_shape = (n_blocks, tile, tile)
    got_labels, got_props, got_meta, logit_blocks, imputed_blocks, uno_grads = exchange(
        [(labels, "item"), (propens, "item"), (meta, "item")],
        0,
        functools.partial(dense_blocks, tile, item_blocks),
        (user_pred, user_imp, item_pred, item_imp),
        (
            jax.ShapeDtypeStruct(block_shape, jnp.float32),
            jax.ShapeDtypeStruct(block_shape, jnp.float32),
            jax.ShapeDtypeStruct(block_shape, jnp.bfloat16),
        ),
    )

    vmem = pl.BlockSpec(memory_space=pltpu.VMEM)
    smem = pl.BlockSpec(memory_space=pltpu.SMEM)
    user_chunks, item_chunks = pl.pallas_call(
        functools.partial(tile_kernel, tile, user_blocks, item_blocks, obs_slots),
        out_shape=[
            jax.ShapeDtypeStruct((item_ways, 2, user_rows // item_ways, rank), jnp.float32),
            jax.ShapeDtypeStruct((user_ways, 2, shard_rows // user_ways, rank), jnp.float32),
        ],
        in_specs=[smem] + [vmem] * 9,
        out_specs=[vmem, vmem],
        scratch_shapes=[
            pltpu.VMEM((n_blocks, tile, tile), jnp.float32),
            pltpu.VMEM((n_blocks, tile, tile), jnp.float32),
            pltpu.VMEM((2, user_rows, rank), jnp.float32),
            pltpu.VMEM((2, shard_rows, rank), jnp.float32),
        ],
    )(
        got_meta,
        logit_blocks, imputed_blocks, uno_grads, got_labels, got_props, user_pred, user_imp, item_pred, item_imp,
    )
    user_share, item_share = reduce_exchange([(user_chunks, "item"), (item_chunks, "user")], 1)
    return (user_share[0], user_share[1], item_share[0], item_share[1])


def solution(mesh):
    in_specs = (
        P("user", None),
        P("user", None),
        P("item", None),
        P("item", None),
        P("user", "item", None),
        P("user", "item", None),
        P("user", "item", None),
        P("user", "item", None),
        P("user", "item", None),
        P("user", "item", None, None, None),
        P("user", "item", None, None, None),
    )
    out_specs = (
        P(("user", "item"), None),
        P(("user", "item"), None),
        P(("item", "user"), None),
        P(("item", "user"), None),
    )
    return jax.shard_map(shards, mesh=mesh, in_specs=in_specs, out_specs=out_specs, check_vma=False)
```

```python
import functools

import jax
import jax.numpy as jnp
from jax import lax
from jax.experimental import pallas as pl
from jax.experimental.pallas import tpu as pltpu
from jax.sharding import PartitionSpec as P

MESH = pl.DeviceIdType.MESH

loss_weight = 0.015625
ITEM_RING = 8


def product(form, first, second):
    return jnp.einsum(form, first, second, preferred_element_type=jnp.float32)


def dense_blocks(tile, item_blocks, up_ref, ui_ref, vp_ref, vi_ref, s_ref, m_ref, d_ref):
    def block(k, carry):
        users = pl.ds(pl.multiple_of((k // item_blocks) * tile, tile), tile)
        items = pl.ds(pl.multiple_of((k % item_blocks) * tile, tile), tile)
        dims = (((1,), (1,)), ((), ()))
        logits = lax.dot_general(up_ref[users, :], vp_ref[items, :], dims, preferred_element_type=jnp.float32)
        imputed = lax.dot_general(ui_ref[users, :], vi_ref[items, :], dims, preferred_element_type=jnp.float32)
        s_ref[k] = logits
        m_ref[k] = imputed
        d_ref[k] = ((jax.nn.sigmoid(logits) - jax.nn.sigmoid(imputed)) * loss_weight).astype(d_ref.dtype)
        return carry

    lax.fori_loop(0, s_ref.shape[0], block, 0)


def exchange_kernel(axes, count, work_in, work, *refs):
    x_refs, y_refs = refs[:count], refs[count + work_in : 2 * count + work_in]
    send_sem, recv_sem, local_sem = refs[-3:]
    work_refs = refs[count : count + work_in] + refs[2 * count + work_in : -3]
    barrier = pltpu.get_barrier_semaphore()
    for axis in axes:
        n = lax.axis_size(axis)
        me = lax.axis_index(axis)
        for k in range(1, n):
            pl.semaphore_signal(barrier, inc=1, device_id={axis: lax.rem(me + k, n)}, device_id_type=MESH)
    pl.semaphore_wait(barrier, sum(lax.axis_size(axis) - 1 for axis in axes))
    copies = []
    slot = 0
    for which, axis in enumerate(axes):
        n = lax.axis_size(axis)
        me = lax.axis_index(axis)
        x_ref, y_ref = x_refs[which], y_refs[which]
        local = pltpu.make_async_copy(x_ref.at[me], y_ref.at[me], local_sem.at[which])
        local.start()
        copies.append(local)
        for k in range(1, n):
            peer = lax.rem(me + k, n)
            copy = pltpu.make_async_remote_copy(
                src_ref=x_ref.at[peer],
                dst_ref=y_ref.at[me],
                send_sem=send_sem.at[slot],
                recv_sem=recv_sem.at[slot],
                device_id={axis: peer},
                device_id_type=MESH,
            )
            copy.start()
            copies.append(copy)
            slot += 1
    if work is not None:
        work(*work_refs)
    for copy in copies:
        copy.wait()


def exchange(pairs, collective, work=None, work_inputs=(), work_outputs=()):
    axes = tuple(axis for _, axis in pairs)
    arrays = [x for x, _ in pairs]
    slots = sum(lax.axis_size(axis) - 1 for axis in axes)
    vmem = pl.BlockSpec(memory_space=pltpu.VMEM)
    return pl.pallas_call(
        functools.partial(exchange_kernel, axes, len(arrays), len(work_inputs), work),
        out_shape=[jax.ShapeDtypeStruct(x.shape, x.dtype) for x in arrays] + list(work_outputs),
        in_specs=[pl.BlockSpec(memory_space=pl.ANY)] * len(arrays) + [vmem] * len(work_inputs),
        out_specs=[pl.BlockSpec(memory_space=pl.ANY)] * len(arrays) + [vmem] * len(work_outputs),
        scratch_shapes=[
            pltpu.SemaphoreType.DMA((slots,)),
            pltpu.SemaphoreType.DMA((slots,)),
            pltpu.SemaphoreType.DMA((len(arrays),)),
        ],
        compiler_params=pltpu.CompilerParams(collective_id=collective, has_side_effects=True),
    )(*arrays, *work_inputs)


def reduce_kernel(ring, *refs):
    (user_x, item_x, user_pred_out, user_imp_out, item_pred_out, item_imp_out,
     own, partner_land, stage, ring_land, item_land, send_sem, recv_sem, local_sem) = refs
    item_n = lax.axis_size("item")
    user_n = lax.axis_size("user")
    me = lax.axis_index("item")
    me_user = lax.axis_index("user")
    layer = me // ring
    spot = me % ring
    layers = item_n // ring
    barrier = pltpu.get_barrier_semaphore()
    for k in range(1, layers):
        pl.semaphore_signal(barrier, inc=1, device_id={"item": lax.rem(me + k * ring, item_n)}, device_id_type=MESH)
    for k in range(1, ring):
        pl.semaphore_signal(
            barrier, inc=1, device_id={"item": layer * ring + lax.rem(spot + k, ring)}, device_id_type=MESH
        )
    for k in range(1, user_n):
        pl.semaphore_signal(barrier, inc=1, device_id={"user": lax.rem(me_user + k, user_n)}, device_id_type=MESH)
    pl.semaphore_wait(barrier, (layers - 1) + (ring - 1) + (user_n - 1))

    item_copies = []
    local_item = pltpu.make_async_copy(item_x.at[me_user], item_land.at[me_user], local_sem.at[0])
    local_item.start()
    item_copies.append(local_item)
    for k in range(1, user_n):
        peer = lax.rem(me_user + k, user_n)
        copy = pltpu.make_async_remote_copy(
            src_ref=item_x.at[peer],
            dst_ref=item_land.at[me_user],
            send_sem=send_sem.at[k - 1],
            recv_sem=recv_sem.at[k - 1],
            device_id={"user": peer},
            device_id_type=MESH,
        )
        copy.start()
        item_copies.append(copy)
    base = user_n - 1

    local_own = pltpu.make_async_copy(user_x.at[pl.ds(layer * ring, ring)], own, local_sem.at[1])
    local_own.start()
    layer_copies = []
    for k in range(1, layers):
        other = lax.rem(layer + k, layers)
        copy = pltpu.make_async_remote_copy(
            src_ref=user_x.at[pl.ds(other * ring, ring)],
            dst_ref=partner_land.at[k - 1],
            send_sem=send_sem.at[base + k - 1],
            recv_sem=recv_sem.at[base + k - 1],
            device_id={"item": other * ring + spot},
            device_id_type=MESH,
        )
        copy.start()
        layer_copies.append(copy)
    base += layers - 1
    local_own.wait()
    for copy in layer_copies:
        copy.wait()
    total = own[...]
    for k in range(layers - 1):
        total = total + partner_land[k]
    stage[...] = total

    ring_copies = []
    for k in range(1, ring):
        peer = lax.rem(spot + k, ring)
        copy = pltpu.make_async_remote_copy(
            src_ref=stage.at[peer],
            dst_ref=ring_land.at[spot],
            send_sem=send_sem.at[base + k - 1],
            recv_sem=recv_sem.at[base + k - 1],
            device_id={"item": layer * ring + peer},
            device_id_type=MESH,
        )
        copy.start()
        ring_copies.append(copy)
    for copy in ring_copies:
        copy.wait()
    user_total = stage[spot]
    for k in range(1, ring):
        user_total = user_total + ring_land[lax.rem(spot + k, ring)]
    user_pred_out[...] = user_total[0]
    user_imp_out[...] = user_total[1]

    for copy in item_copies:
        copy.wait()
    item_total = item_land[0]
    for source in range(1, user_n):
        item_total = item_total + item_land[source]
    item_pred_out[...] = item_total[0]
    item_imp_out[...] = item_total[1]


def reduce_exchange(user_x, item_x, ring):
    item_n = lax.axis_size("item")
    user_n = lax.axis_size("user")
    layers = item_n // ring
    slots = (user_n - 1) + (layers - 1) + (ring - 1)
    layer_shape = (ring,) + user_x.shape[1:]
    vmem = pl.BlockSpec(memory_space=pltpu.VMEM)
    return pl.pallas_call(
        functools.partial(reduce_kernel, ring),
        out_shape=[jax.ShapeDtypeStruct(user_x.shape[2:], user_x.dtype)] * 2
        + [jax.ShapeDtypeStruct(item_x.shape[2:], item_x.dtype)] * 2,
        in_specs=[pl.BlockSpec(memory_space=pl.ANY)] * 2,
        out_specs=[vmem] * 4,
        scratch_shapes=[
            pltpu.VMEM(layer_shape, user_x.dtype),
            pltpu.VMEM((layers - 1,) + layer_shape, user_x.dtype),
            pltpu.VMEM(layer_shape, user_x.dtype),
            pltpu.VMEM(layer_shape, user_x.dtype),
            pltpu.VMEM(item_x.shape, item_x.dtype),
            pltpu.SemaphoreType.DMA((slots,)),
            pltpu.SemaphoreType.DMA((slots,)),
            pltpu.SemaphoreType.DMA((2,)),
        ],
        compiler_params=pltpu.CompilerParams(collective_id=1, has_side_effects=True),
    )(user_x, item_x)


def tile_kernel(
    tile, user_blocks, item_blocks, obs_slots,
    meta_ref,
    s_ref, m_ref, d_ref, lab_ref, prop_ref, up_ref, ui_ref, vp_ref, vi_ref,
    user_out, item_out,
    g_acc, h_acc, user_acc, item_acc,
):
    n_blocks = user_blocks * item_blocks
    origins = meta_ref.shape[0]
    for k in range(n_blocks):
        count = meta_ref[0, k]
        for origin in range(1, origins):
            count = count + meta_ref[origin, k]
        g_acc[k] = count.astype(jnp.float32) * d_ref[k].astype(jnp.float32)
        h_acc[k] = jnp.zeros((tile, tile), jnp.float32)

    def observed(t, carry):
        origin = t // obs_slots
        slot = t % obs_slots
        pos = meta_ref[origin, n_blocks + slot]
        valid = meta_ref[origin, n_blocks + obs_slots + slot].astype(jnp.float32)
        ologits = s_ref[pos]
        predicted = jax.nn.sigmoid(ologits)
        imputes = jax.nn.sigmoid(m_ref[pos])
        labels = lab_ref[origin, pl.ds(slot * tile, tile), :].astype(jnp.float32)
        propens = prop_ref[origin, pl.ds(slot * tile, tile), :].astype(jnp.float32)
        seen = (labels > 0).astype(jnp.float32)
        clicks = (labels == 2).astype(jnp.float32)
        weight = valid * seen / propens
        ograds = ((valid * (predicted - imputes) + weight * (imputes - clicks)) * loss_weight).astype(jnp.bfloat16)
        ohgrads = (
            2.0 * weight * (imputes - clicks) * ologits * ologits * imputes * (1.0 - imputes) * loss_weight
        ).astype(jnp.bfloat16)
        g_acc[pos] += ograds.astype(jnp.float32)
        h_acc[pos] += ohgrads.astype(jnp.float32)
        return carry

    lax.fori_loop(0, origins * obs_slots, observed, 0)

    user_acc[...] = jnp.zeros(user_acc.shape, jnp.float32)
    item_acc[...] = jnp.zeros(item_acc.shape, jnp.float32)
    forward = (((1,), (0,)), ((), ()))
    backward = (((0,), (0,)), ((), ()))
    for ub in range(user_blocks):
        users = pl.ds(ub * tile, tile)
        for ib in range(item_blocks):
            items = pl.ds(ib * tile, tile)
            k = ub * item_blocks + ib
            for model, acc, u_ref, v_ref in ((0, g_acc, up_ref, vp_ref), (1, h_acc, ui_ref, vi_ref)):
                wide = acc[k]
                hi = wide.astype(jnp.bfloat16)
                lo = (wide - hi.astype(jnp.float32)).astype(jnp.bfloat16)
                v = v_ref[items, :]
                u = u_ref[users, :]
                user_acc[model, users, :] += lax.dot_general(
                    hi, v, forward, preferred_element_type=jnp.float32
                ) + lax.dot_general(lo, v, forward, preferred_element_type=jnp.float32)
                item_acc[model, items, :] += lax.dot_general(
                    hi, u, backward, preferred_element_type=jnp.float32
                ) + lax.dot_general(lo, u, backward, preferred_element_type=jnp.float32)
    user_rows = user_out.shape[2]
    for dest in range(user_out.shape[0]):
        user_out[dest] = user_acc[:, pl.ds(dest * user_rows, user_rows), :]
    item_rows = item_out.shape[2]
    for dest in range(item_out.shape[0]):
        item_out[dest] = item_acc[:, pl.ds(dest * item_rows, item_rows), :]


def shards(
    user_pred,
    user_imp,
    item_pred,
    item_imp,
    uno_user,
    uno_item,
    obs_user,
    obs_item,
    obs_count,
    obs_label,
    obs_prop,
):
    item_ways = lax.axis_size("item")
    user_ways = lax.axis_size("user")
    tile = obs_label.shape[-1]
    rank = user_pred.shape[1]
    user_rows = user_pred.shape[0]
    shard_rows = item_pred.shape[0]
    user_blocks = user_rows // tile
    item_blocks = shard_rows // tile
    n_blocks = user_blocks * item_blocks
    obs_slots = obs_user.shape[-1] // item_ways

    uno_pos = (uno_user * item_blocks + uno_item).reshape(item_ways, -1)
    uno_counts = jnp.sum((uno_pos[:, :, None] == jnp.arange(n_blocks, dtype=jnp.int32)).astype(jnp.int32), axis=1)
    obs_pos = (obs_user * item_blocks + obs_item).reshape(item_ways, obs_slots)
    place = jnp.arange(obs_slots, dtype=jnp.int32)
    valid = (place[None, :] < obs_count.reshape(item_ways, 1)).astype(jnp.int32)
    meta = jnp.concatenate(
        [uno_counts, obs_pos, valid, jnp.zeros((item_ways, tile - n_blocks - 2 * obs_slots), jnp.int32)], axis=1
    )
    labels = obs_label.reshape(item_ways, obs_slots * tile, tile).astype(jnp.bfloat16)
    propens = obs_prop.reshape(item_ways, obs_slots * tile, tile)
    block_shape = (n_blocks, tile, tile)
    got_labels, got_props, got_meta, logit_blocks, imputed_blocks, uno_grads = exchange(
        [(labels, "item"), (propens, "item"), (meta, "item")],
        0,
        functools.partial(dense_blocks, tile, item_blocks),
        (user_pred, user_imp, item_pred, item_imp),
        (
            jax.ShapeDtypeStruct(block_shape, jnp.float32),
            jax.ShapeDtypeStruct(block_shape, jnp.float32),
            jax.ShapeDtypeStruct(block_shape, jnp.bfloat16),
        ),
    )

    vmem = pl.BlockSpec(memory_space=pltpu.VMEM)
    smem = pl.BlockSpec(memory_space=pltpu.SMEM)
    user_chunks, item_chunks = pl.pallas_call(
        functools.partial(tile_kernel, tile, user_blocks, item_blocks, obs_slots),
        out_shape=[
            jax.ShapeDtypeStruct((item_ways, 2, user_rows // item_ways, rank), jnp.float32),
            jax.ShapeDtypeStruct((user_ways, 2, shard_rows // user_ways, rank), jnp.float32),
        ],
        in_specs=[smem] + [vmem] * 9,
        out_specs=[vmem, vmem],
        scratch_shapes=[
            pltpu.VMEM((n_blocks, tile, tile), jnp.float32),
            pltpu.VMEM((n_blocks, tile, tile), jnp.float32),
            pltpu.VMEM((2, user_rows, rank), jnp.float32),
            pltpu.VMEM((2, shard_rows, rank), jnp.float32),
        ],
    )(
        got_meta,
        logit_blocks, imputed_blocks, uno_grads, got_labels, got_props, user_pred, user_imp, item_pred, item_imp,
    )
    ring = ITEM_RING if item_ways % ITEM_RING == 0 else item_ways
    return tuple(reduce_exchange(user_chunks, item_chunks, ring))


def solution(mesh):
    in_specs = (
        P("user", None),
        P("user", None),
        P("item", None),
        P("item", None),
        P("user", "item", None),
        P("user", "item", None),
        P("user", "item", None),
        P("user", "item", None),
        P("user", "item", None),
        P("user", "item", None, None, None),
        P("user", "item", None, None, None),
    )
    out_specs = (
        P(("user", "item"), None),
        P(("user", "item"), None),
        P(("item", "user"), None),
        P(("item", "user"), None),
    )
    return jax.shard_map(shards, mesh=mesh, in_specs=in_specs, out_specs=out_specs, check_vma=False)
```

```python
import functools

import jax
import jax.numpy as jnp
from jax import lax
from jax.experimental import pallas as pl
from jax.experimental.pallas import tpu as pltpu
from jax.sharding import PartitionSpec as P

MESH = pl.DeviceIdType.MESH

loss_weight = 0.015625


def product(form, first, second):
    return jnp.einsum(form, first, second, preferred_element_type=jnp.float32)


def dense_blocks(tile, item_blocks, up_ref, ui_ref, vp_ref, vi_ref, s_ref, m_ref, d_ref):
    def block(k, carry):
        users = pl.ds(pl.multiple_of((k // item_blocks) * tile, tile), tile)
        items = pl.ds(pl.multiple_of((k % item_blocks) * tile, tile), tile)
        dims = (((1,), (1,)), ((), ()))
        logits = lax.dot_general(up_ref[users, :], vp_ref[items, :], dims, preferred_element_type=jnp.float32)
        imputed = lax.dot_general(ui_ref[users, :], vi_ref[items, :], dims, preferred_element_type=jnp.float32)
        s_ref[k] = logits
        m_ref[k] = imputed
        d_ref[k] = ((jax.nn.sigmoid(logits) - jax.nn.sigmoid(imputed)) * loss_weight).astype(d_ref.dtype)
        return carry

    lax.fori_loop(0, s_ref.shape[0], block, 0)


def exchange_kernel(axes, count, work_in, work, *refs):
    x_refs, y_refs = refs[:count], refs[count + work_in : 2 * count + work_in]
    send_sem, recv_sem, local_sem = refs[-3:]
    work_refs = refs[count : count + work_in] + refs[2 * count + work_in : -3]
    barrier = pltpu.get_barrier_semaphore()
    for axis in axes:
        n = lax.axis_size(axis)
        me = lax.axis_index(axis)
        for k in range(1, n):
            pl.semaphore_signal(barrier, inc=1, device_id={axis: lax.rem(me + k, n)}, device_id_type=MESH)
    pl.semaphore_wait(barrier, sum(lax.axis_size(axis) - 1 for axis in axes))
    copies = []
    slot = 0
    for which, axis in enumerate(axes):
        n = lax.axis_size(axis)
        me = lax.axis_index(axis)
        x_ref, y_ref = x_refs[which], y_refs[which]
        local = pltpu.make_async_copy(x_ref.at[me], y_ref.at[me], local_sem.at[which])
        local.start()
        copies.append(local)
        for k in range(1, n):
            peer = lax.rem(me + k, n)
            copy = pltpu.make_async_remote_copy(
                src_ref=x_ref.at[peer],
                dst_ref=y_ref.at[me],
                send_sem=send_sem.at[slot],
                recv_sem=recv_sem.at[slot],
                device_id={axis: peer},
                device_id_type=MESH,
            )
            copy.start()
            copies.append(copy)
            slot += 1
    if work is not None:
        work(*work_refs)
    for copy in copies:
        copy.wait()


def exchange(pairs, collective, work=None, work_inputs=(), work_outputs=()):
    axes = tuple(axis for _, axis in pairs)
    arrays = [x for x, _ in pairs]
    slots = sum(lax.axis_size(axis) - 1 for axis in axes)
    vmem = pl.BlockSpec(memory_space=pltpu.VMEM)
    return pl.pallas_call(
        functools.partial(exchange_kernel, axes, len(arrays), len(work_inputs), work),
        out_shape=[jax.ShapeDtypeStruct(x.shape, x.dtype) for x in arrays] + list(work_outputs),
        in_specs=[pl.BlockSpec(memory_space=pl.ANY)] * len(arrays) + [vmem] * len(work_inputs),
        out_specs=[pl.BlockSpec(memory_space=pl.ANY)] * len(arrays) + [vmem] * len(work_outputs),
        scratch_shapes=[
            pltpu.SemaphoreType.DMA((slots,)),
            pltpu.SemaphoreType.DMA((slots,)),
            pltpu.SemaphoreType.DMA((len(arrays),)),
        ],
        compiler_params=pltpu.CompilerParams(collective_id=collective, has_side_effects=True),
    )(*arrays, *work_inputs)


def reduce_kernel(axes, *refs):
    count = len(axes)
    x_refs, out_refs = refs[:count], refs[count : 2 * count]
    land_refs = refs[2 * count : 3 * count]
    send_sem, recv_sem, local_sem = refs[3 * count :]
    barrier = pltpu.get_barrier_semaphore()
    for axis in axes:
        n = lax.axis_size(axis)
        me = lax.axis_index(axis)
        for k in range(1, n):
            pl.semaphore_signal(barrier, inc=1, device_id={axis: lax.rem(me + k, n)}, device_id_type=MESH)
    pl.semaphore_wait(barrier, sum(lax.axis_size(axis) - 1 for axis in axes))
    copies = []
    slot = 0
    for which, axis in enumerate(axes):
        n = lax.axis_size(axis)
        me = lax.axis_index(axis)
        x_ref, land = x_refs[which], land_refs[which]
        local = pltpu.make_async_copy(x_ref.at[me], land.at[me], local_sem.at[which])
        local.start()
        copies.append(local)
        for k in range(1, n):
            peer = lax.rem(me + k, n)
            copy = pltpu.make_async_remote_copy(
                src_ref=x_ref.at[peer],
                dst_ref=land.at[me],
                send_sem=send_sem.at[slot],
                recv_sem=recv_sem.at[slot],
                device_id={axis: peer},
                device_id_type=MESH,
            )
            copy.start()
            copies.append(copy)
            slot += 1
    for copy in copies:
        copy.wait()
    for which in range(count):
        land = land_refs[which]
        total = land[0]
        for source in range(1, land.shape[0]):
            total = total + land[source]
        out_refs[which][...] = total


def reduce_exchange(pairs, collective):
    axes = tuple(axis for _, axis in pairs)
    arrays = [x for x, _ in pairs]
    slots = sum(lax.axis_size(axis) - 1 for axis in axes)
    return pl.pallas_call(
        functools.partial(reduce_kernel, axes),
        out_shape=[jax.ShapeDtypeStruct(x.shape[1:], x.dtype) for x in arrays],
        in_specs=[pl.BlockSpec(memory_space=pl.ANY)] * len(arrays),
        out_specs=[pl.BlockSpec(memory_space=pltpu.VMEM)] * len(arrays),
        scratch_shapes=[pltpu.VMEM(x.shape, x.dtype) for x in arrays]
        + [
            pltpu.SemaphoreType.DMA((slots,)),
            pltpu.SemaphoreType.DMA((slots,)),
            pltpu.SemaphoreType.DMA((len(arrays),)),
        ],
        compiler_params=pltpu.CompilerParams(collective_id=collective, has_side_effects=True),
    )(*arrays)


def tile_kernel(
    tile, user_blocks, item_blocks, obs_slots,
    meta_ref,
    lab_ref, prop_ref, up_ref, ui_ref, vp_ref, vi_ref,
    user_out, item_out,
    s_ref, m_ref, d_ref, g_acc, h_acc, user_acc, item_acc,
):
    n_blocks = user_blocks * item_blocks
    dense_blocks(tile, item_blocks, up_ref, ui_ref, vp_ref, vi_ref, s_ref, m_ref, d_ref)
    origins = meta_ref.shape[0]
    for k in range(n_blocks):
        count = meta_ref[0, k]
        for origin in range(1, origins):
            count = count + meta_ref[origin, k]
        g_acc[k] = count.astype(jnp.float32) * d_ref[k].astype(jnp.float32)
        h_acc[k] = jnp.zeros((tile, tile), jnp.float32)

    def observed(t, carry):
        origin = t // obs_slots
        slot = t % obs_slots
        pos = meta_ref[origin, n_blocks + slot]
        valid = meta_ref[origin, n_blocks + obs_slots + slot].astype(jnp.float32)
        ologits = s_ref[pos]
        predicted = jax.nn.sigmoid(ologits)
        imputes = jax.nn.sigmoid(m_ref[pos])
        labels = lab_ref[origin, pl.ds(slot * tile, tile), :].astype(jnp.float32)
        propens = prop_ref[origin, pl.ds(slot * tile, tile), :].astype(jnp.float32)
        seen = (labels > 0).astype(jnp.float32)
        clicks = (labels == 2).astype(jnp.float32)
        weight = valid * seen / propens
        ograds = ((valid * (predicted - imputes) + weight * (imputes - clicks)) * loss_weight).astype(jnp.bfloat16)
        ohgrads = (
            2.0 * weight * (imputes - clicks) * ologits * ologits * imputes * (1.0 - imputes) * loss_weight
        ).astype(jnp.bfloat16)
        g_acc[pos] += ograds.astype(jnp.float32)
        h_acc[pos] += ohgrads.astype(jnp.float32)
        return carry

    lax.fori_loop(0, origins * obs_slots, observed, 0)

    user_acc[...] = jnp.zeros(user_acc.shape, jnp.float32)
    item_acc[...] = jnp.zeros(item_acc.shape, jnp.float32)
    forward = (((1,), (0,)), ((), ()))
    backward = (((0,), (0,)), ((), ()))
    for ub in range(user_blocks):
        users = pl.ds(ub * tile, tile)
        for ib in range(item_blocks):
            items = pl.ds(ib * tile, tile)
            k = ub * item_blocks + ib
            for model, acc, u_ref, v_ref in ((0, g_acc, up_ref, vp_ref), (1, h_acc, ui_ref, vi_ref)):
                wide = acc[k]
                hi = wide.astype(jnp.bfloat16)
                lo = (wide - hi.astype(jnp.float32)).astype(jnp.bfloat16)
                v = v_ref[items, :]
                u = u_ref[users, :]
                user_acc[model, users, :] += lax.dot_general(
                    hi, v, forward, preferred_element_type=jnp.float32
                ) + lax.dot_general(lo, v, forward, preferred_element_type=jnp.float32)
                item_acc[model, items, :] += lax.dot_general(
                    hi, u, backward, preferred_element_type=jnp.float32
                ) + lax.dot_general(lo, u, backward, preferred_element_type=jnp.float32)
    user_rows = user_out.shape[2]
    for dest in range(user_out.shape[0]):
        user_out[dest] = user_acc[:, pl.ds(dest * user_rows, user_rows), :]
    item_rows = item_out.shape[2]
    for dest in range(item_out.shape[0]):
        item_out[dest] = item_acc[:, pl.ds(dest * item_rows, item_rows), :]


def shards(
    user_pred,
    user_imp,
    item_pred,
    item_imp,
    uno_user,
    uno_item,
    obs_user,
    obs_item,
    obs_count,
    obs_label,
    obs_prop,
):
    item_ways = lax.axis_size("item")
    user_ways = lax.axis_size("user")
    tile = obs_label.shape[-1]
    rank = user_pred.shape[1]
    user_rows = user_pred.shape[0]
    shard_rows = item_pred.shape[0]
    user_blocks = user_rows // tile
    item_blocks = shard_rows // tile
    n_blocks = user_blocks * item_blocks
    obs_slots = obs_user.shape[-1] // item_ways

    uno_pos = (uno_user * item_blocks + uno_item).reshape(item_ways, -1)
    uno_counts = jnp.sum((uno_pos[:, :, None] == jnp.arange(n_blocks, dtype=jnp.int32)).astype(jnp.int32), axis=1)
    obs_pos = (obs_user * item_blocks + obs_item).reshape(item_ways, obs_slots)
    place = jnp.arange(obs_slots, dtype=jnp.int32)
    valid = (place[None, :] < obs_count.reshape(item_ways, 1)).astype(jnp.int32)
    meta = jnp.concatenate(
        [uno_counts, obs_pos, valid, jnp.zeros((item_ways, tile - n_blocks - 2 * obs_slots), jnp.int32)], axis=1
    )
    labels = obs_label.reshape(item_ways, obs_slots * tile, tile).astype(jnp.bfloat16)
    propens = obs_prop.reshape(item_ways, obs_slots * tile, tile)
    got_labels, got_props, got_meta = exchange([(labels, "item"), (propens, "item"), (meta, "item")], 0)

    vmem = pl.BlockSpec(memory_space=pltpu.VMEM)
    smem = pl.BlockSpec(memory_space=pltpu.SMEM)
    user_chunks, item_chunks = pl.pallas_call(
        functools.partial(tile_kernel, tile, user_blocks, item_blocks, obs_slots),
        out_shape=[
            jax.ShapeDtypeStruct((item_ways, 2, user_rows // item_ways, rank), jnp.float32),
            jax.ShapeDtypeStruct((user_ways, 2, shard_rows // user_ways, rank), jnp.float32),
        ],
        in_specs=[smem] + [vmem] * 6,
        out_specs=[vmem, vmem],
        scratch_shapes=[
            pltpu.VMEM((n_blocks, tile, tile), jnp.float32),
            pltpu.VMEM((n_blocks, tile, tile), jnp.float32),
            pltpu.VMEM((n_blocks, tile, tile), jnp.bfloat16),
            pltpu.VMEM((n_blocks, tile, tile), jnp.float32),
            pltpu.VMEM((n_blocks, tile, tile), jnp.float32),
            pltpu.VMEM((2, user_rows, rank), jnp.float32),
            pltpu.VMEM((2, shard_rows, rank), jnp.float32),
        ],
    )(
        got_meta, got_labels, got_props, user_pred, user_imp, item_pred, item_imp,
    )
    user_share, item_share = reduce_exchange([(user_chunks, "item"), (item_chunks, "user")], 1)
    return (user_share[0], user_share[1], item_share[0], item_share[1])


def solution(mesh):
    in_specs = (
        P("user", None),
        P("user", None),
        P("item", None),
        P("item", None),
        P("user", "item", None),
        P("user", "item", None),
        P("user", "item", None),
        P("user", "item", None),
        P("user", "item", None),
        P("user", "item", None, None, None),
        P("user", "item", None, None, None),
    )
    out_specs = (
        P(("user", "item"), None),
        P(("user", "item"), None),
        P(("item", "user"), None),
        P(("item", "user"), None),
    )
    return jax.shard_map(shards, mesh=mesh, in_specs=in_specs, out_specs=out_specs, check_vma=False)
```

```python
import functools

import jax
import jax.numpy as jnp
from jax import lax
from jax.experimental import pallas as pl
from jax.experimental.pallas import tpu as pltpu
from jax.sharding import PartitionSpec as P

MESH = pl.DeviceIdType.MESH

loss_weight = 0.015625


def product(form, first, second):
    return jnp.einsum(form, first, second, preferred_element_type=jnp.float32)


def exchange_kernel(axes, count, work_in, work, *refs):
    x_refs, y_refs = refs[:count], refs[count + work_in : 2 * count + work_in]
    send_sem, recv_sem, local_sem = refs[-3:]
    work_refs = refs[count : count + work_in] + refs[2 * count + work_in : -3]
    barrier = pltpu.get_barrier_semaphore()
    for axis in axes:
        n = lax.axis_size(axis)
        me = lax.axis_index(axis)
        for k in range(1, n):
            pl.semaphore_signal(barrier, inc=1, device_id={axis: lax.rem(me + k, n)}, device_id_type=MESH)
    pl.semaphore_wait(barrier, sum(lax.axis_size(axis) - 1 for axis in axes))
    copies = []
    slot = 0
    for which, axis in enumerate(axes):
        n = lax.axis_size(axis)
        me = lax.axis_index(axis)
        x_ref, y_ref = x_refs[which], y_refs[which]
        local = pltpu.make_async_copy(x_ref.at[me], y_ref.at[me], local_sem.at[which])
        local.start()
        copies.append(local)
        for k in range(1, n):
            peer = lax.rem(me + k, n)
            copy = pltpu.make_async_remote_copy(
                src_ref=x_ref.at[peer],
                dst_ref=y_ref.at[me],
                send_sem=send_sem.at[slot],
                recv_sem=recv_sem.at[slot],
                device_id={axis: peer},
                device_id_type=MESH,
            )
            copy.start()
            copies.append(copy)
            slot += 1
    if work is not None:
        work(*work_refs)
    for copy in copies:
        copy.wait()


def exchange(pairs, collective, work=None, work_inputs=(), work_outputs=()):
    axes = tuple(axis for _, axis in pairs)
    arrays = [x for x, _ in pairs]
    slots = sum(lax.axis_size(axis) - 1 for axis in axes)
    vmem = pl.BlockSpec(memory_space=pltpu.VMEM)
    return pl.pallas_call(
        functools.partial(exchange_kernel, axes, len(arrays), len(work_inputs), work),
        out_shape=[jax.ShapeDtypeStruct(x.shape, x.dtype) for x in arrays] + list(work_outputs),
        in_specs=[pl.BlockSpec(memory_space=pl.ANY)] * len(arrays) + [vmem] * len(work_inputs),
        out_specs=[pl.BlockSpec(memory_space=pl.ANY)] * len(arrays) + [vmem] * len(work_outputs),
        scratch_shapes=[
            pltpu.SemaphoreType.DMA((slots,)),
            pltpu.SemaphoreType.DMA((slots,)),
            pltpu.SemaphoreType.DMA((len(arrays),)),
        ],
        compiler_params=pltpu.CompilerParams(collective_id=collective, has_side_effects=True),
    )(*arrays, *work_inputs)


def reduce_kernel(axes, *refs):
    count = len(axes)
    x_refs, out_refs = refs[:count], refs[count : 2 * count]
    land_refs = refs[2 * count : 3 * count]
    send_sem, recv_sem, local_sem = refs[3 * count :]
    barrier = pltpu.get_barrier_semaphore()
    for axis in axes:
        n = lax.axis_size(axis)
        me = lax.axis_index(axis)
        for k in range(1, n):
            pl.semaphore_signal(barrier, inc=1, device_id={axis: lax.rem(me + k, n)}, device_id_type=MESH)
    pl.semaphore_wait(barrier, sum(lax.axis_size(axis) - 1 for axis in axes))
    copies = []
    slot = 0
    for which, axis in enumerate(axes):
        n = lax.axis_size(axis)
        me = lax.axis_index(axis)
        x_ref, land = x_refs[which], land_refs[which]
        local = pltpu.make_async_copy(x_ref.at[me], land.at[me], local_sem.at[which])
        local.start()
        copies.append(local)
        for k in range(1, n):
            peer = lax.rem(me + k, n)
            copy = pltpu.make_async_remote_copy(
                src_ref=x_ref.at[peer],
                dst_ref=land.at[me],
                send_sem=send_sem.at[slot],
                recv_sem=recv_sem.at[slot],
                device_id={axis: peer},
                device_id_type=MESH,
            )
            copy.start()
            copies.append(copy)
            slot += 1
    for copy in copies:
        copy.wait()
    for which in range(count):
        land = land_refs[which]
        total = land[0]
        for source in range(1, land.shape[0]):
            total = total + land[source]
        out_refs[which][...] = total


def reduce_exchange(pairs, collective):
    axes = tuple(axis for _, axis in pairs)
    arrays = [x for x, _ in pairs]
    slots = sum(lax.axis_size(axis) - 1 for axis in axes)
    return pl.pallas_call(
        functools.partial(reduce_kernel, axes),
        out_shape=[jax.ShapeDtypeStruct(x.shape[1:], x.dtype) for x in arrays],
        in_specs=[pl.BlockSpec(memory_space=pl.ANY)] * len(arrays),
        out_specs=[pl.BlockSpec(memory_space=pltpu.VMEM)] * len(arrays),
        scratch_shapes=[pltpu.VMEM(x.shape, x.dtype) for x in arrays]
        + [
            pltpu.SemaphoreType.DMA((slots,)),
            pltpu.SemaphoreType.DMA((slots,)),
            pltpu.SemaphoreType.DMA((len(arrays),)),
        ],
        compiler_params=pltpu.CompilerParams(collective_id=collective, has_side_effects=True),
    )(*arrays)


def tile_kernel(
    tile, user_blocks, item_blocks, obs_slots,
    meta_ref,
    lab_ref, prop_ref, up_ref, ui_ref, vp_ref, vi_ref,
    user_out, item_out,
    s_ref, m_ref, user_acc, item_acc,
):
    n_blocks = user_blocks * item_blocks
    origins = meta_ref.shape[0]
    forward = (((1,), (0,)), ((), ()))
    backward = (((0,), (0,)), ((), ()))
    outer = (((1,), (1,)), ((), ()))
    user_acc[...] = jnp.zeros(user_acc.shape, jnp.float32)
    item_acc[...] = jnp.zeros(item_acc.shape, jnp.float32)

    def add_products(ub, ib, grads, hgrads, scale):
        users = pl.ds(pl.multiple_of(ub * tile, tile), tile)
        items = pl.ds(pl.multiple_of(ib * tile, tile), tile)
        for model, g, u_ref, v_ref in ((0, grads, up_ref, vp_ref), (1, hgrads, ui_ref, vi_ref)):
            if g is None:
                continue
            user_term = lax.dot_general(g, v_ref[items, :], forward, preferred_element_type=jnp.float32)
            item_term = lax.dot_general(g, u_ref[users, :], backward, preferred_element_type=jnp.float32)
            if scale is not None:
                user_term = scale * user_term
                item_term = scale * item_term
            user_acc[model, users, :] += user_term
            item_acc[model, items, :] += item_term

    def unobserved(k, carry):
        ub = k // item_blocks
        ib = k % item_blocks
        users = pl.ds(pl.multiple_of(ub * tile, tile), tile)
        items = pl.ds(pl.multiple_of(ib * tile, tile), tile)
        logits = lax.dot_general(up_ref[users, :], vp_ref[items, :], outer, preferred_element_type=jnp.float32)
        imputed = lax.dot_general(ui_ref[users, :], vi_ref[items, :], outer, preferred_element_type=jnp.float32)
        s_ref[k] = logits
        m_ref[k] = imputed
        grads = ((jax.nn.sigmoid(logits) - jax.nn.sigmoid(imputed)) * loss_weight).astype(jnp.bfloat16)
        count = meta_ref[0, k]
        for origin in range(1, origins):
            count = count + meta_ref[origin, k]
        add_products(ub, ib, grads, None, count.astype(jnp.float32))
        return carry

    lax.fori_loop(0, n_blocks, unobserved, 0)

    def observed(t, carry):
        origin = t // obs_slots
        slot = t % obs_slots
        pos = meta_ref[origin, n_blocks + slot]
        valid = meta_ref[origin, n_blocks + obs_slots + slot].astype(jnp.float32)
        ologits = s_ref[pos]
        predicted = jax.nn.sigmoid(ologits)
        imputes = jax.nn.sigmoid(m_ref[pos])
        labels = lab_ref[origin, pl.ds(slot * tile, tile), :].astype(jnp.float32)
        propens = prop_ref[origin, pl.ds(slot * tile, tile), :].astype(jnp.float32)
        seen = (labels > 0).astype(jnp.float32)
        clicks = (labels == 2).astype(jnp.float32)
        weight = valid * seen / propens
        ograds = ((valid * (predicted - imputes) + weight * (imputes - clicks)) * loss_weight).astype(jnp.bfloat16)
        ohgrads = (
            2.0 * weight * (imputes - clicks) * ologits * ologits * imputes * (1.0 - imputes) * loss_weight
        ).astype(jnp.bfloat16)
        add_products(pos // item_blocks, pos % item_blocks, ograds, ohgrads, None)
        return carry

    lax.fori_loop(0, origins * obs_slots, observed, 0)

    user_rows = user_out.shape[2]
    for dest in range(user_out.shape[0]):
        user_out[dest] = user_acc[:, pl.ds(dest * user_rows, user_rows), :]
    item_rows = item_out.shape[2]
    for dest in range(item_out.shape[0]):
        item_out[dest] = item_acc[:, pl.ds(dest * item_rows, item_rows), :]


def shards(
    user_pred,
    user_imp,
    item_pred,
    item_imp,
    uno_user,
    uno_item,
    obs_user,
    obs_item,
    obs_count,
    obs_label,
    obs_prop,
):
    item_ways = lax.axis_size("item")
    user_ways = lax.axis_size("user")
    tile = obs_label.shape[-1]
    rank = user_pred.shape[1]
    user_rows = user_pred.shape[0]
    shard_rows = item_pred.shape[0]
    user_blocks = user_rows // tile
    item_blocks = shard_rows // tile
    n_blocks = user_blocks * item_blocks
    obs_slots = obs_user.shape[-1] // item_ways

    uno_pos = (uno_user * item_blocks + uno_item).reshape(item_ways, -1)
    uno_counts = jnp.sum((uno_pos[:, :, None] == jnp.arange(n_blocks, dtype=jnp.int32)).astype(jnp.int32), axis=1)
    obs_pos = (obs_user * item_blocks + obs_item).reshape(item_ways, obs_slots)
    place = jnp.arange(obs_slots, dtype=jnp.int32)
    valid = (place[None, :] < obs_count.reshape(item_ways, 1)).astype(jnp.int32)
    meta = jnp.concatenate(
        [uno_counts, obs_pos, valid, jnp.zeros((item_ways, tile - n_blocks - 2 * obs_slots), jnp.int32)], axis=1
    )
    labels = obs_label.reshape(item_ways, obs_slots * tile, tile).astype(jnp.bfloat16)
    propens = obs_prop.reshape(item_ways, obs_slots * tile, tile)
    got_labels, got_props, got_meta = exchange([(labels, "item"), (propens, "item"), (meta, "item")], 0)

    vmem = pl.BlockSpec(memory_space=pltpu.VMEM)
    smem = pl.BlockSpec(memory_space=pltpu.SMEM)
    user_chunks, item_chunks = pl.pallas_call(
        functools.partial(tile_kernel, tile, user_blocks, item_blocks, obs_slots),
        out_shape=[
            jax.ShapeDtypeStruct((item_ways, 2, user_rows // item_ways, rank), jnp.float32),
            jax.ShapeDtypeStruct((user_ways, 2, shard_rows // user_ways, rank), jnp.float32),
        ],
        in_specs=[smem] + [vmem] * 6,
        out_specs=[vmem, vmem],
        scratch_shapes=[
            pltpu.VMEM((n_blocks, tile, tile), jnp.float32),
            pltpu.VMEM((n_blocks, tile, tile), jnp.float32),
            pltpu.VMEM((2, user_rows, rank), jnp.float32),
            pltpu.VMEM((2, shard_rows, rank), jnp.float32),
        ],
    )(
        got_meta, got_labels, got_props, user_pred, user_imp, item_pred, item_imp,
    )
    user_share, item_share = reduce_exchange([(user_chunks, "item"), (item_chunks, "user")], 1)
    return (user_share[0], user_share[1], item_share[0], item_share[1])


def solution(mesh):
    in_specs = (
        P("user", None),
        P("user", None),
        P("item", None),
        P("item", None),
        P("user", "item", None),
        P("user", "item", None),
        P("user", "item", None),
        P("user", "item", None),
        P("user", "item", None),
        P("user", "item", None, None, None),
        P("user", "item", None, None, None),
    )
    out_specs = (
        P(("user", "item"), None),
        P(("user", "item"), None),
        P(("item", "user"), None),
        P(("item", "user"), None),
    )
    return jax.shard_map(shards, mesh=mesh, in_specs=in_specs, out_specs=out_specs, check_vma=False)
```

```python
import functools

import jax
import jax.numpy as jnp
from jax import lax
from jax.experimental import pallas as pl
from jax.experimental.pallas import tpu as pltpu
from jax.sharding import PartitionSpec as P

MESH = pl.DeviceIdType.MESH

loss_weight = 0.015625


def product(form, first, second):
    return jnp.einsum(form, first, second, preferred_element_type=jnp.float32)


def dense_blocks(tile, item_blocks, up_ref, ui_ref, vp_ref, vi_ref, s_ref, m_ref, d_ref):
    def block(k, carry):
        users = pl.ds(pl.multiple_of((k // item_blocks) * tile, tile), tile)
        items = pl.ds(pl.multiple_of((k % item_blocks) * tile, tile), tile)
        dims = (((1,), (1,)), ((), ()))
        logits = lax.dot_general(up_ref[users, :], vp_ref[items, :], dims, preferred_element_type=jnp.float32)
        imputed = lax.dot_general(ui_ref[users, :], vi_ref[items, :], dims, preferred_element_type=jnp.float32)
        s_ref[k] = logits
        m_ref[k] = imputed
        d_ref[k] = ((jax.nn.sigmoid(logits) - jax.nn.sigmoid(imputed)) * loss_weight).astype(d_ref.dtype)
        return carry

    lax.fori_loop(0, s_ref.shape[0], block, 0)


def exchange_kernel(axes, whole, count, work_in, work, *refs):
    x_refs, y_refs = refs[:count], refs[count + work_in : 2 * count + work_in]
    send_sem, recv_sem, local_sem = refs[-3:]
    work_refs = refs[count : count + work_in] + refs[2 * count + work_in : -3]
    barrier = pltpu.get_barrier_semaphore()
    for axis in axes:
        n = lax.axis_size(axis)
        me = lax.axis_index(axis)
        for k in range(1, n):
            pl.semaphore_signal(barrier, inc=1, device_id={axis: lax.rem(me + k, n)}, device_id_type=MESH)
    pl.semaphore_wait(barrier, sum(lax.axis_size(axis) - 1 for axis in axes))
    copies = []
    slot = 0
    for which, axis in enumerate(axes):
        n = lax.axis_size(axis)
        me = lax.axis_index(axis)
        x_ref, y_ref = x_refs[which], y_refs[which]
        local = pltpu.make_async_copy(x_ref if whole[which] else x_ref.at[me], y_ref.at[me], local_sem.at[which])
        local.start()
        copies.append(local)
        for k in range(1, n):
            peer = lax.rem(me + k, n)
            copy = pltpu.make_async_remote_copy(
                src_ref=x_ref if whole[which] else x_ref.at[peer],
                dst_ref=y_ref.at[me],
                send_sem=send_sem.at[slot],
                recv_sem=recv_sem.at[slot],
                device_id={axis: peer},
                device_id_type=MESH,
            )
            copy.start()
            copies.append(copy)
            slot += 1
    if work is not None:
        work(*work_refs)
    for copy in copies:
        copy.wait()


def exchange(pairs, collective, work=None, work_inputs=(), work_outputs=(), whole=None):
    axes = tuple(axis for _, axis in pairs)
    arrays = [x for x, _ in pairs]
    whole = tuple(whole) if whole is not None else (False,) * len(arrays)
    shapes = [(lax.axis_size(axis),) + x.shape if w else x.shape for (x, axis), w in zip(pairs, whole)]
    slots = sum(lax.axis_size(axis) - 1 for axis in axes)
    vmem = pl.BlockSpec(memory_space=pltpu.VMEM)
    return pl.pallas_call(
        functools.partial(exchange_kernel, axes, whole, len(arrays), len(work_inputs), work),
        out_shape=[jax.ShapeDtypeStruct(shape, x.dtype) for shape, x in zip(shapes, arrays)] + list(work_outputs),
        in_specs=[pl.BlockSpec(memory_space=pl.ANY)] * len(arrays) + [vmem] * len(work_inputs),
        out_specs=[pl.BlockSpec(memory_space=pl.ANY)] * len(arrays) + [vmem] * len(work_outputs),
        scratch_shapes=[
            pltpu.SemaphoreType.DMA((slots,)),
            pltpu.SemaphoreType.DMA((slots,)),
            pltpu.SemaphoreType.DMA((len(arrays),)),
        ],
        compiler_params=pltpu.CompilerParams(collective_id=collective, has_side_effects=True),
    )(*arrays, *work_inputs)


def reduce_kernel(axes, *refs):
    count = len(axes)
    x_refs, out_refs = refs[:count], refs[count : 2 * count]
    land_refs = refs[2 * count : 3 * count]
    send_sem, recv_sem, local_sem = refs[3 * count :]
    barrier = pltpu.get_barrier_semaphore()
    for axis in axes:
        n = lax.axis_size(axis)
        me = lax.axis_index(axis)
        for k in range(1, n):
            pl.semaphore_signal(barrier, inc=1, device_id={axis: lax.rem(me + k, n)}, device_id_type=MESH)
    pl.semaphore_wait(barrier, sum(lax.axis_size(axis) - 1 for axis in axes))
    copies = []
    slot = 0
    for which, axis in enumerate(axes):
        n = lax.axis_size(axis)
        me = lax.axis_index(axis)
        x_ref, land = x_refs[which], land_refs[which]
        local = pltpu.make_async_copy(x_ref.at[me], land.at[me], local_sem.at[which])
        local.start()
        copies.append(local)
        for k in range(1, n):
            peer = lax.rem(me + k, n)
            copy = pltpu.make_async_remote_copy(
                src_ref=x_ref.at[peer],
                dst_ref=land.at[me],
                send_sem=send_sem.at[slot],
                recv_sem=recv_sem.at[slot],
                device_id={axis: peer},
                device_id_type=MESH,
            )
            copy.start()
            copies.append(copy)
            slot += 1
    for copy in copies:
        copy.wait()
    for which in range(count):
        land = land_refs[which]
        total = land[0]
        for source in range(1, land.shape[0]):
            total = total + land[source]
        out_refs[which][...] = total


def reduce_exchange(pairs, collective):
    axes = tuple(axis for _, axis in pairs)
    arrays = [x for x, _ in pairs]
    slots = sum(lax.axis_size(axis) - 1 for axis in axes)
    return pl.pallas_call(
        functools.partial(reduce_kernel, axes),
        out_shape=[jax.ShapeDtypeStruct(x.shape[1:], x.dtype) for x in arrays],
        in_specs=[pl.BlockSpec(memory_space=pl.ANY)] * len(arrays),
        out_specs=[pl.BlockSpec(memory_space=pltpu.VMEM)] * len(arrays),
        scratch_shapes=[pltpu.VMEM(x.shape, x.dtype) for x in arrays]
        + [
            pltpu.SemaphoreType.DMA((slots,)),
            pltpu.SemaphoreType.DMA((slots,)),
            pltpu.SemaphoreType.DMA((len(arrays),)),
        ],
        compiler_params=pltpu.CompilerParams(collective_id=collective, has_side_effects=True),
    )(*arrays)


def tile_kernel(
    tile, user_blocks, item_blocks, obs_slots,
    uu_ref, ui_idx_ref, ou_ref, oi_ref, oc_ref,
    lab_ref, prop_ref, up_ref, ui_ref, vp_ref, vi_ref,
    user_out, item_out,
    count_ref, pos_ref, valid_ref,
    s_ref, m_ref, d_ref, g_acc, h_acc, user_acc, item_acc,
):
    n_blocks = user_blocks * item_blocks
    origins = uu_ref.shape[0]
    shard = lax.axis_index("item")
    uno_slots = uu_ref.shape[1] // origins
    for k in range(n_blocks):
        count_ref[k] = 0

    def tally(t, carry):
        origin = t // uno_slots
        slot = shard * uno_slots + t % uno_slots
        k = uu_ref[origin, slot] * item_blocks + ui_idx_ref[origin, slot]
        count_ref[k] = count_ref[k] + 1
        return carry

    lax.fori_loop(0, origins * uno_slots, tally, 0)
    for t in range(origins * obs_slots):
        origin, place = t // obs_slots, t % obs_slots
        slot = shard * obs_slots + place
        pos_ref[t] = ou_ref[origin, slot] * item_blocks + oi_ref[origin, slot]
        valid_ref[t] = jnp.where(place < oc_ref[origin, shard], 1.0, 0.0).astype(jnp.float32)
    dense_blocks(tile, item_blocks, up_ref, ui_ref, vp_ref, vi_ref, s_ref, m_ref, d_ref)
    for k in range(n_blocks):
        g_acc[k] = count_ref[k].astype(jnp.float32) * d_ref[k].astype(jnp.float32)
        h_acc[k] = jnp.zeros((tile, tile), jnp.float32)

    def observed(t, carry):
        origin = t // obs_slots
        slot = t % obs_slots
        pos = pos_ref[t]
        valid = valid_ref[t]
        ologits = s_ref[pos]
        predicted = jax.nn.sigmoid(ologits)
        imputes = jax.nn.sigmoid(m_ref[pos])
        labels = lab_ref[origin, pl.ds(slot * tile, tile), :].astype(jnp.float32)
        propens = prop_ref[origin, pl.ds(slot * tile, tile), :].astype(jnp.float32)
        seen = (labels > 0).astype(jnp.float32)
        clicks = (labels == 2).astype(jnp.float32)
        weight = valid * seen / propens
        ograds = ((valid * (predicted - imputes) + weight * (imputes - clicks)) * loss_weight).astype(jnp.bfloat16)
        ohgrads = (
            2.0 * weight * (imputes - clicks) * ologits * ologits * imputes * (1.0 - imputes) * loss_weight
        ).astype(jnp.bfloat16)
        g_acc[pos] += ograds.astype(jnp.float32)
        h_acc[pos] += ohgrads.astype(jnp.float32)
        return carry

    lax.fori_loop(0, origins * obs_slots, observed, 0)

    user_acc[...] = jnp.zeros(user_acc.shape, jnp.float32)
    item_acc[...] = jnp.zeros(item_acc.shape, jnp.float32)
    forward = (((1,), (0,)), ((), ()))
    backward = (((0,), (0,)), ((), ()))
    for ub in range(user_blocks):
        users = pl.ds(ub * tile, tile)
        for ib in range(item_blocks):
            items = pl.ds(ib * tile, tile)
            k = ub * item_blocks + ib
            for model, acc, u_ref, v_ref in ((0, g_acc, up_ref, vp_ref), (1, h_acc, ui_ref, vi_ref)):
                wide = acc[k]
                hi = wide.astype(jnp.bfloat16)
                lo = (wide - hi.astype(jnp.float32)).astype(jnp.bfloat16)
                v = v_ref[items, :]
                u = u_ref[users, :]
                user_acc[model, users, :] += lax.dot_general(
                    hi, v, forward, preferred_element_type=jnp.float32
                ) + lax.dot_general(lo, v, forward, preferred_element_type=jnp.float32)
                item_acc[model, items, :] += lax.dot_general(
                    hi, u, backward, preferred_element_type=jnp.float32
                ) + lax.dot_general(lo, u, backward, preferred_element_type=jnp.float32)
    user_rows = user_out.shape[2]
    for dest in range(user_out.shape[0]):
        user_out[dest] = user_acc[:, pl.ds(dest * user_rows, user_rows), :]
    item_rows = item_out.shape[2]
    for dest in range(item_out.shape[0]):
        item_out[dest] = item_acc[:, pl.ds(dest * item_rows, item_rows), :]


def shards(
    user_pred,
    user_imp,
    item_pred,
    item_imp,
    uno_user,
    uno_item,
    obs_user,
    obs_item,
    obs_count,
    obs_label,
    obs_prop,
):
    item_ways = lax.axis_size("item")
    user_ways = lax.axis_size("user")
    tile = obs_label.shape[-1]
    rank = user_pred.shape[1]
    user_rows = user_pred.shape[0]
    shard_rows = item_pred.shape[0]
    user_blocks = user_rows // tile
    item_blocks = shard_rows // tile
    n_blocks = user_blocks * item_blocks
    obs_slots = obs_user.shape[-1] // item_ways

    labels = obs_label.reshape(item_ways, obs_slots * tile, tile).astype(jnp.bfloat16)
    propens = obs_prop.reshape(item_ways, obs_slots * tile, tile)
    indices = [x.reshape(x.shape[-1]) for x in (uno_user, uno_item, obs_user, obs_item, obs_count)]
    got_labels, got_props, *got_indices = exchange(
        [(labels, "item"), (propens, "item")] + [(x, "item") for x in indices],
        0,
        whole=[False, False] + [True] * len(indices),
    )
    vmem = pl.BlockSpec(memory_space=pltpu.VMEM)
    smem = pl.BlockSpec(memory_space=pltpu.SMEM)
    user_chunks, item_chunks = pl.pallas_call(
        functools.partial(tile_kernel, tile, user_blocks, item_blocks, obs_slots),
        out_shape=[
            jax.ShapeDtypeStruct((item_ways, 2, user_rows // item_ways, rank), jnp.float32),
            jax.ShapeDtypeStruct((user_ways, 2, shard_rows // user_ways, rank), jnp.float32),
        ],
        in_specs=[smem] * 5 + [vmem] * 6,
        out_specs=[vmem, vmem],
        scratch_shapes=[
            pltpu.SMEM((n_blocks,), jnp.int32),
            pltpu.SMEM((item_ways * obs_slots,), jnp.int32),
            pltpu.SMEM((item_ways * obs_slots,), jnp.float32),
            pltpu.VMEM((n_blocks, tile, tile), jnp.float32),
            pltpu.VMEM((n_blocks, tile, tile), jnp.float32),
            pltpu.VMEM((n_blocks, tile, tile), jnp.bfloat16),
            pltpu.VMEM((n_blocks, tile, tile), jnp.float32),
            pltpu.VMEM((n_blocks, tile, tile), jnp.float32),
            pltpu.VMEM((2, user_rows, rank), jnp.float32),
            pltpu.VMEM((2, shard_rows, rank), jnp.float32),
        ],
    )(
        *got_indices, got_labels, got_props, user_pred, user_imp, item_pred, item_imp,
    )
    user_share, item_share = reduce_exchange([(user_chunks, "item"), (item_chunks, "user")], 1)
    return (user_share[0], user_share[1], item_share[0], item_share[1])


def solution(mesh):
    in_specs = (
        P("user", None),
        P("user", None),
        P("item", None),
        P("item", None),
        P("user", "item", None),
        P("user", "item", None),
        P("user", "item", None),
        P("user", "item", None),
        P("user", "item", None),
        P("user", "item", None, None, None),
        P("user", "item", None, None, None),
    )
    out_specs = (
        P(("user", "item"), None),
        P(("user", "item"), None),
        P(("item", "user"), None),
        P(("item", "user"), None),
    )
    return jax.shard_map(shards, mesh=mesh, in_specs=in_specs, out_specs=out_specs, check_vma=False)
```

```python
import functools

import jax
import jax.numpy as jnp
from jax import lax
from jax.experimental import pallas as pl
from jax.experimental.pallas import tpu as pltpu
from jax.sharding import PartitionSpec as P

MESH = pl.DeviceIdType.MESH

loss_weight = 0.015625


def product(form, first, second):
    return jnp.einsum(form, first, second, preferred_element_type=jnp.float32)


def exchange_kernel(axes, whole, count, work_in, work, *refs):
    x_refs, y_refs = refs[:count], refs[count + work_in : 2 * count + work_in]
    send_sem, recv_sem, local_sem = refs[-3:]
    work_refs = refs[count : count + work_in] + refs[2 * count + work_in : -3]
    barrier = pltpu.get_barrier_semaphore()
    for axis in axes:
        n = lax.axis_size(axis)
        me = lax.axis_index(axis)
        for k in range(1, n):
            pl.semaphore_signal(barrier, inc=1, device_id={axis: lax.rem(me + k, n)}, device_id_type=MESH)
    pl.semaphore_wait(barrier, sum(lax.axis_size(axis) - 1 for axis in axes))
    copies = []
    slot = 0
    for which, axis in enumerate(axes):
        n = lax.axis_size(axis)
        me = lax.axis_index(axis)
        x_ref, y_ref = x_refs[which], y_refs[which]
        local = pltpu.make_async_copy(x_ref if whole[which] else x_ref.at[me], y_ref.at[me], local_sem.at[which])
        local.start()
        copies.append(local)
        for k in range(1, n):
            peer = lax.rem(me + k, n)
            copy = pltpu.make_async_remote_copy(
                src_ref=x_ref if whole[which] else x_ref.at[peer],
                dst_ref=y_ref.at[me],
                send_sem=send_sem.at[slot],
                recv_sem=recv_sem.at[slot],
                device_id={axis: peer},
                device_id_type=MESH,
            )
            copy.start()
            copies.append(copy)
            slot += 1
    if work is not None:
        work(*work_refs)
    for copy in copies:
        copy.wait()


def exchange(pairs, collective, work=None, work_inputs=(), work_outputs=(), whole=None):
    axes = tuple(axis for _, axis in pairs)
    arrays = [x for x, _ in pairs]
    whole = tuple(whole) if whole is not None else (False,) * len(arrays)
    shapes = [(lax.axis_size(axis),) + x.shape if w else x.shape for (x, axis), w in zip(pairs, whole)]
    slots = sum(lax.axis_size(axis) - 1 for axis in axes)
    vmem = pl.BlockSpec(memory_space=pltpu.VMEM)
    return pl.pallas_call(
        functools.partial(exchange_kernel, axes, whole, len(arrays), len(work_inputs), work),
        out_shape=[jax.ShapeDtypeStruct(shape, x.dtype) for shape, x in zip(shapes, arrays)] + list(work_outputs),
        in_specs=[pl.BlockSpec(memory_space=pl.ANY)] * len(arrays) + [vmem] * len(work_inputs),
        out_specs=[pl.BlockSpec(memory_space=pl.ANY)] * len(arrays) + [vmem] * len(work_outputs),
        scratch_shapes=[
            pltpu.SemaphoreType.DMA((slots,)),
            pltpu.SemaphoreType.DMA((slots,)),
            pltpu.SemaphoreType.DMA((len(arrays),)),
        ],
        compiler_params=pltpu.CompilerParams(collective_id=collective, has_side_effects=True),
    )(*arrays, *work_inputs)


def reduce_kernel(axes, *refs):
    count = len(axes)
    x_refs, out_refs = refs[:count], refs[count : 2 * count]
    land_refs = refs[2 * count : 3 * count]
    send_sem, recv_sem, local_sem = refs[3 * count :]
    barrier = pltpu.get_barrier_semaphore()
    for axis in axes:
        n = lax.axis_size(axis)
        me = lax.axis_index(axis)
        for k in range(1, n):
            pl.semaphore_signal(barrier, inc=1, device_id={axis: lax.rem(me + k, n)}, device_id_type=MESH)
    pl.semaphore_wait(barrier, sum(lax.axis_size(axis) - 1 for axis in axes))
    copies = []
    slot = 0
    for which, axis in enumerate(axes):
        n = lax.axis_size(axis)
        me = lax.axis_index(axis)
        x_ref, land = x_refs[which], land_refs[which]
        local = pltpu.make_async_copy(x_ref.at[me], land.at[me], local_sem.at[which])
        local.start()
        copies.append(local)
        for k in range(1, n):
            peer = lax.rem(me + k, n)
            copy = pltpu.make_async_remote_copy(
                src_ref=x_ref.at[peer],
                dst_ref=land.at[me],
                send_sem=send_sem.at[slot],
                recv_sem=recv_sem.at[slot],
                device_id={axis: peer},
                device_id_type=MESH,
            )
            copy.start()
            copies.append(copy)
            slot += 1
    for copy in copies:
        copy.wait()
    for which in range(count):
        land = land_refs[which]
        total = land[0]
        for source in range(1, land.shape[0]):
            total = total + land[source]
        out_refs[which][...] = total


def reduce_exchange(pairs, collective):
    axes = tuple(axis for _, axis in pairs)
    arrays = [x for x, _ in pairs]
    slots = sum(lax.axis_size(axis) - 1 for axis in axes)
    return pl.pallas_call(
        functools.partial(reduce_kernel, axes),
        out_shape=[jax.ShapeDtypeStruct(x.shape[1:], x.dtype) for x in arrays],
        in_specs=[pl.BlockSpec(memory_space=pl.ANY)] * len(arrays),
        out_specs=[pl.BlockSpec(memory_space=pltpu.VMEM)] * len(arrays),
        scratch_shapes=[pltpu.VMEM(x.shape, x.dtype) for x in arrays]
        + [
            pltpu.SemaphoreType.DMA((slots,)),
            pltpu.SemaphoreType.DMA((slots,)),
            pltpu.SemaphoreType.DMA((len(arrays),)),
        ],
        compiler_params=pltpu.CompilerParams(collective_id=collective, has_side_effects=True),
    )(*arrays)


def observed_grads(valid, ologits, imputed, labels, propens):
    predicted = jax.nn.sigmoid(ologits)
    imputes = jax.nn.sigmoid(imputed)
    seen = (labels > 0).astype(jnp.float32)
    clicks = (labels == 2).astype(jnp.float32)
    weight = valid * seen / propens
    ograds = ((valid * (predicted - imputes) + weight * (imputes - clicks)) * loss_weight).astype(jnp.bfloat16)
    ohgrads = (
        2.0 * weight * (imputes - clicks) * ologits * ologits * imputes * (1.0 - imputes) * loss_weight
    ).astype(jnp.bfloat16)
    return ograds, ohgrads


def gather_kernel(
    tile, item_blocks, obs_slots,
    lab_x, prop_x, uu_x, ui_x, ou_x, oi_x, oc_x, up_ref, uimp_ref, vp_ref, vi_ref,
    d_out, g_out, h_out, count_out, pos_out,
    lab_land, prop_land, uu_land, ui_land, ou_land, oi_land, oc_land, s_ref, m_ref,
    send_sem, recv_sem, local_sem,
):
    n = lax.axis_size("item")
    me = lax.axis_index("item")
    barrier = pltpu.get_barrier_semaphore()
    for k in range(1, n):
        pl.semaphore_signal(barrier, inc=1, device_id={"item": lax.rem(me + k, n)}, device_id_type=MESH)
    pl.semaphore_wait(barrier, n - 1)

    index_pairs = ((uu_x, uu_land), (ui_x, ui_land), (ou_x, ou_land), (oi_x, oi_land), (oc_x, oc_land))
    tile_pairs = ((lab_x, lab_land), (prop_x, prop_land))

    def send(which, src, dst, k):
        copy = pltpu.make_async_remote_copy(
            src_ref=src,
            dst_ref=dst,
            send_sem=send_sem.at[which, k - 1],
            recv_sem=recv_sem.at[which, k - 1],
            device_id={"item": lax.rem(me + k, n)},
            device_id_type=MESH,
        )
        copy.start()
        return copy

    index_copies = []
    for which, (x, land) in enumerate(index_pairs):
        local = pltpu.make_async_copy(x, land.at[me], local_sem.at[which])
        local.start()
        index_copies.append(local)
        for k in range(1, n):
            index_copies.append(send(which, x, land.at[me], k))
    tile_local = []
    tile_copies = [[] for _ in range(n)]
    for which, (x, land) in enumerate(tile_pairs):
        slot = len(index_pairs) + which
        local = pltpu.make_async_copy(x.at[me], land.at[me], local_sem.at[slot])
        local.start()
        tile_local.append(local)
        for k in range(1, n):
            tile_copies[k].append(send(slot, x.at[lax.rem(me + k, n)], land.at[me], k))

    dims = (((1,), (1,)), ((), ()))

    def block(k, carry):
        users = pl.ds(pl.multiple_of((k // item_blocks) * tile, tile), tile)
        items = pl.ds(pl.multiple_of((k % item_blocks) * tile, tile), tile)
        logits = lax.dot_general(up_ref[users, :], vp_ref[items, :], dims, preferred_element_type=jnp.float32)
        imputed = lax.dot_general(uimp_ref[users, :], vi_ref[items, :], dims, preferred_element_type=jnp.float32)
        s_ref[k] = logits
        m_ref[k] = imputed
        d_out[k] = ((jax.nn.sigmoid(logits) - jax.nn.sigmoid(imputed)) * loss_weight).astype(d_out.dtype)
        return carry

    lax.fori_loop(0, s_ref.shape[0], block, 0)

    for copy in index_copies:
        copy.wait()
    uno_slots = uu_land.shape[1] // n

    def tally(t, carry):
        origin = t // uno_slots
        slot = me * uno_slots + t % uno_slots
        count_out[t] = uu_land[origin, slot] * item_blocks + ui_land[origin, slot]
        return carry

    lax.fori_loop(0, n * uno_slots, tally, 0)

    def origin_tiles(origin):
        for place in range(obs_slots):
            slot = me * obs_slots + place
            t = origin * obs_slots + place
            pos = ou_land[origin, slot] * item_blocks + oi_land[origin, slot]
            pos_out[t] = pos
            valid = jnp.where(place < oc_land[origin, me], 1.0, 0.0).astype(jnp.float32)
            labels = lab_land[origin, pl.ds(place * tile, tile), :].astype(jnp.float32)
            propens = prop_land[origin, pl.ds(place * tile, tile), :].astype(jnp.float32)
            ograds, ohgrads = observed_grads(valid, s_ref[pos], m_ref[pos], labels, propens)
            g_out[t] = ograds
            h_out[t] = ohgrads

    for copy in tile_local:
        copy.wait()
    origin_tiles(me)
    for k in range(1, n):
        for copy in tile_copies[k]:
            copy.wait()
        origin_tiles(lax.rem(me + n - k, n))


def exchange_tiles(labels, propens, indices, factors, tile, item_blocks, obs_slots):
    n = lax.axis_size("item")
    n_blocks = (factors[0].shape[0] // tile) * item_blocks
    n_tiles = n * obs_slots
    vmem = pl.BlockSpec(memory_space=pltpu.VMEM)
    smem = pl.BlockSpec(memory_space=pltpu.SMEM)
    anyspace = pl.BlockSpec(memory_space=pl.ANY)
    return pl.pallas_call(
        functools.partial(gather_kernel, tile, item_blocks, obs_slots),
        out_shape=[
            jax.ShapeDtypeStruct((n_blocks, tile, tile), jnp.bfloat16),
            jax.ShapeDtypeStruct((n_tiles, tile, tile), jnp.bfloat16),
            jax.ShapeDtypeStruct((n_tiles, tile, tile), jnp.bfloat16),
            jax.ShapeDtypeStruct((indices[0].shape[0],), jnp.int32),
            jax.ShapeDtypeStruct((n_tiles,), jnp.int32),
        ],
        in_specs=[anyspace] * 7 + [vmem] * 4,
        out_specs=[vmem] * 3 + [smem] * 2,
        scratch_shapes=[
            pltpu.VMEM((n,) + labels.shape[1:], labels.dtype),
            pltpu.VMEM((n,) + propens.shape[1:], propens.dtype),
        ]
        + [pltpu.SMEM((n,) + x.shape, x.dtype) for x in indices]
        + [
            pltpu.VMEM((n_blocks, tile, tile), jnp.float32),
            pltpu.VMEM((n_blocks, tile, tile), jnp.float32),
            pltpu.SemaphoreType.DMA((7, n - 1)),
            pltpu.SemaphoreType.DMA((7, n - 1)),
            pltpu.SemaphoreType.DMA((7,)),
        ],
        compiler_params=pltpu.CompilerParams(collective_id=0, has_side_effects=True),
    )(labels, propens, *indices, *factors)


def tile_kernel(
    tile, user_blocks, item_blocks,
    slot_ref, pos_ref, d_ref, gt_ref, ht_ref, up_ref, ui_ref, vp_ref, vi_ref,
    user_out, item_out,
    count_ref, g_acc, h_acc, user_acc, item_acc,
):
    n_blocks = user_blocks * item_blocks
    for k in range(n_blocks):
        count_ref[k] = 0

    def tally(t, carry):
        k = slot_ref[t]
        count_ref[k] = count_ref[k] + 1
        return carry

    lax.fori_loop(0, slot_ref.shape[0], tally, 0)
    for k in range(n_blocks):
        g_acc[k] = count_ref[k].astype(jnp.float32) * d_ref[k].astype(jnp.float32)
        h_acc[k] = jnp.zeros((tile, tile), jnp.float32)

    def observed(t, carry):
        pos = pos_ref[t]
        g_acc[pos] += gt_ref[t].astype(jnp.float32)
        h_acc[pos] += ht_ref[t].astype(jnp.float32)
        return carry

    lax.fori_loop(0, gt_ref.shape[0], observed, 0)

    user_acc[...] = jnp.zeros(user_acc.shape, jnp.float32)
    item_acc[...] = jnp.zeros(item_acc.shape, jnp.float32)
    forward = (((1,), (0,)), ((), ()))
    backward = (((0,), (0,)), ((), ()))
    for ub in range(user_blocks):
        users = pl.ds(ub * tile, tile)
        for ib in range(item_blocks):
            items = pl.ds(ib * tile, tile)
            k = ub * item_blocks + ib
            for model, acc, u_ref, v_ref in ((0, g_acc, up_ref, vp_ref), (1, h_acc, ui_ref, vi_ref)):
                wide = acc[k]
                hi = wide.astype(jnp.bfloat16)
                lo = (wide - hi.astype(jnp.float32)).astype(jnp.bfloat16)
                v = v_ref[items, :]
                u = u_ref[users, :]
                user_acc[model, users, :] += lax.dot_general(
                    hi, v, forward, preferred_element_type=jnp.float32
                ) + lax.dot_general(lo, v, forward, preferred_element_type=jnp.float32)
                item_acc[model, items, :] += lax.dot_general(
                    hi, u, backward, preferred_element_type=jnp.float32
                ) + lax.dot_general(lo, u, backward, preferred_element_type=jnp.float32)
    user_rows = user_out.shape[2]
    for dest in range(user_out.shape[0]):
        user_out[dest] = user_acc[:, pl.ds(dest * user_rows, user_rows), :]
    item_rows = item_out.shape[2]
    for dest in range(item_out.shape[0]):
        item_out[dest] = item_acc[:, pl.ds(dest * item_rows, item_rows), :]


def shards(
    user_pred,
    user_imp,
    item_pred,
    item_imp,
    uno_user,
    uno_item,
    obs_user,
    obs_item,
    obs_count,
    obs_label,
    obs_prop,
):
    item_ways = lax.axis_size("item")
    user_ways = lax.axis_size("user")
    tile = obs_label.shape[-1]
    rank = user_pred.shape[1]
    user_rows = user_pred.shape[0]
    shard_rows = item_pred.shape[0]
    user_blocks = user_rows // tile
    item_blocks = shard_rows // tile
    n_blocks = user_blocks * item_blocks
    obs_slots = obs_user.shape[-1] // item_ways

    labels = obs_label.reshape(item_ways, obs_slots * tile, tile).astype(jnp.bfloat16)
    propens = obs_prop.reshape(item_ways, obs_slots * tile, tile)
    indices = [x.reshape(x.shape[-1]) for x in (uno_user, uno_item, obs_user, obs_item, obs_count)]
    uno_grads, obs_grads, obs_hgrads, counts, tile_pos = exchange_tiles(
        labels, propens, indices, (user_pred, user_imp, item_pred, item_imp), tile, item_blocks, obs_slots
    )
    vmem = pl.BlockSpec(memory_space=pltpu.VMEM)
    smem = pl.BlockSpec(memory_space=pltpu.SMEM)
    user_chunks, item_chunks = pl.pallas_call(
        functools.partial(tile_kernel, tile, user_blocks, item_blocks),
        out_shape=[
            jax.ShapeDtypeStruct((item_ways, 2, user_rows // item_ways, rank), jnp.float32),
            jax.ShapeDtypeStruct((user_ways, 2, shard_rows // user_ways, rank), jnp.float32),
        ],
        in_specs=[smem] * 2 + [vmem] * 7,
        out_specs=[vmem, vmem],
        scratch_shapes=[
            pltpu.SMEM((n_blocks,), jnp.int32),
            pltpu.VMEM((n_blocks, tile, tile), jnp.float32),
            pltpu.VMEM((n_blocks, tile, tile), jnp.float32),
            pltpu.VMEM((2, user_rows, rank), jnp.float32),
            pltpu.VMEM((2, shard_rows, rank), jnp.float32),
        ],
    )(counts, tile_pos, uno_grads, obs_grads, obs_hgrads, user_pred, user_imp, item_pred, item_imp)
    user_share, item_share = reduce_exchange([(user_chunks, "item"), (item_chunks, "user")], 1)
    return (user_share[0], user_share[1], item_share[0], item_share[1])


def solution(mesh):
    in_specs = (
        P("user", None),
        P("user", None),
        P("item", None),
        P("item", None),
        P("user", "item", None),
        P("user", "item", None),
        P("user", "item", None),
        P("user", "item", None),
        P("user", "item", None),
        P("user", "item", None, None, None),
        P("user", "item", None, None, None),
    )
    out_specs = (
        P(("user", "item"), None),
        P(("user", "item"), None),
        P(("item", "user"), None),
        P(("item", "user"), None),
    )
    return jax.shard_map(shards, mesh=mesh, in_specs=in_specs, out_specs=out_specs, check_vma=False)
```

```python
import functools

import jax
import jax.numpy as jnp
from jax import lax
from jax.experimental import pallas as pl
from jax.experimental.pallas import tpu as pltpu
from jax.sharding import PartitionSpec as P

MESH = pl.DeviceIdType.MESH

loss_weight = 0.015625


def product(form, first, second):
    return jnp.einsum(form, first, second, preferred_element_type=jnp.float32)


def exchange_kernel(axes, whole, count, work_in, work, *refs):
    x_refs, y_refs = refs[:count], refs[count + work_in : 2 * count + work_in]
    send_sem, recv_sem, local_sem = refs[-3:]
    work_refs = refs[count : count + work_in] + refs[2 * count + work_in : -3]
    barrier = pltpu.get_barrier_semaphore()
    for axis in axes:
        n = lax.axis_size(axis)
        me = lax.axis_index(axis)
        for k in range(1, n):
            pl.semaphore_signal(barrier, inc=1, device_id={axis: lax.rem(me + k, n)}, device_id_type=MESH)
    pl.semaphore_wait(barrier, sum(lax.axis_size(axis) - 1 for axis in axes))
    copies = []
    slot = 0
    for which, axis in enumerate(axes):
        n = lax.axis_size(axis)
        me = lax.axis_index(axis)
        x_ref, y_ref = x_refs[which], y_refs[which]
        local = pltpu.make_async_copy(x_ref if whole[which] else x_ref.at[me], y_ref.at[me], local_sem.at[which])
        local.start()
        copies.append(local)
        for k in range(1, n):
            peer = lax.rem(me + k, n)
            copy = pltpu.make_async_remote_copy(
                src_ref=x_ref if whole[which] else x_ref.at[peer],
                dst_ref=y_ref.at[me],
                send_sem=send_sem.at[slot],
                recv_sem=recv_sem.at[slot],
                device_id={axis: peer},
                device_id_type=MESH,
            )
            copy.start()
            copies.append(copy)
            slot += 1
    if work is not None:
        work(*work_refs)
    for copy in copies:
        copy.wait()


def exchange(pairs, collective, work=None, work_inputs=(), work_outputs=(), whole=None):
    axes = tuple(axis for _, axis in pairs)
    arrays = [x for x, _ in pairs]
    whole = tuple(whole) if whole is not None else (False,) * len(arrays)
    shapes = [(lax.axis_size(axis),) + x.shape if w else x.shape for (x, axis), w in zip(pairs, whole)]
    slots = sum(lax.axis_size(axis) - 1 for axis in axes)
    vmem = pl.BlockSpec(memory_space=pltpu.VMEM)
    return pl.pallas_call(
        functools.partial(exchange_kernel, axes, whole, len(arrays), len(work_inputs), work),
        out_shape=[jax.ShapeDtypeStruct(shape, x.dtype) for shape, x in zip(shapes, arrays)] + list(work_outputs),
        in_specs=[pl.BlockSpec(memory_space=pl.ANY)] * len(arrays) + [vmem] * len(work_inputs),
        out_specs=[pl.BlockSpec(memory_space=pl.ANY)] * len(arrays) + [vmem] * len(work_outputs),
        scratch_shapes=[
            pltpu.SemaphoreType.DMA((slots,)),
            pltpu.SemaphoreType.DMA((slots,)),
            pltpu.SemaphoreType.DMA((len(arrays),)),
        ],
        compiler_params=pltpu.CompilerParams(collective_id=collective, has_side_effects=True),
    )(*arrays, *work_inputs)


def reduce_kernel(axes, *refs):
    count = len(axes)
    x_refs, out_refs = refs[:count], refs[count : 2 * count]
    land_refs = refs[2 * count : 3 * count]
    send_sem, recv_sem, local_sem = refs[3 * count :]
    barrier = pltpu.get_barrier_semaphore()
    for axis in axes:
        n = lax.axis_size(axis)
        me = lax.axis_index(axis)
        for k in range(1, n):
            pl.semaphore_signal(barrier, inc=1, device_id={axis: lax.rem(me + k, n)}, device_id_type=MESH)
    pl.semaphore_wait(barrier, sum(lax.axis_size(axis) - 1 for axis in axes))
    copies = []
    slot = 0
    for which, axis in enumerate(axes):
        n = lax.axis_size(axis)
        me = lax.axis_index(axis)
        x_ref, land = x_refs[which], land_refs[which]
        local = pltpu.make_async_copy(x_ref.at[me], land.at[me], local_sem.at[which])
        local.start()
        copies.append(local)
        for k in range(1, n):
            peer = lax.rem(me + k, n)
            copy = pltpu.make_async_remote_copy(
                src_ref=x_ref.at[peer],
                dst_ref=land.at[me],
                send_sem=send_sem.at[slot],
                recv_sem=recv_sem.at[slot],
                device_id={axis: peer},
                device_id_type=MESH,
            )
            copy.start()
            copies.append(copy)
            slot += 1
    for copy in copies:
        copy.wait()
    for which in range(count):
        land = land_refs[which]
        total = land[0]
        for source in range(1, land.shape[0]):
            total = total + land[source]
        out_refs[which][...] = total


def reduce_exchange(pairs, collective):
    axes = tuple(axis for _, axis in pairs)
    arrays = [x for x, _ in pairs]
    slots = sum(lax.axis_size(axis) - 1 for axis in axes)
    return pl.pallas_call(
        functools.partial(reduce_kernel, axes),
        out_shape=[jax.ShapeDtypeStruct(x.shape[1:], x.dtype) for x in arrays],
        in_specs=[pl.BlockSpec(memory_space=pl.ANY)] * len(arrays),
        out_specs=[pl.BlockSpec(memory_space=pltpu.VMEM)] * len(arrays),
        scratch_shapes=[pltpu.VMEM(x.shape, x.dtype) for x in arrays]
        + [
            pltpu.SemaphoreType.DMA((slots,)),
            pltpu.SemaphoreType.DMA((slots,)),
            pltpu.SemaphoreType.DMA((len(arrays),)),
        ],
        compiler_params=pltpu.CompilerParams(collective_id=collective, has_side_effects=True),
    )(*arrays)


def observed_grads(valid, ologits, imputed, labels, propens):
    predicted = jax.nn.sigmoid(ologits)
    imputes = jax.nn.sigmoid(imputed)
    seen = (labels > 0).astype(jnp.float32)
    clicks = (labels == 2).astype(jnp.float32)
    weight = valid * seen / propens
    ograds = ((valid * (predicted - imputes) + weight * (imputes - clicks)) * loss_weight).astype(jnp.bfloat16)
    ohgrads = (
        2.0 * weight * (imputes - clicks) * ologits * ologits * imputes * (1.0 - imputes) * loss_weight
    ).astype(jnp.bfloat16)
    return ograds, ohgrads


def gather_kernel(
    tile, item_blocks, obs_slots,
    lab_x, prop_x, uu_x, ui_x, ou_x, oi_x, oc_x, up_ref, uimp_ref, vp_ref, vi_ref,
    d_out, g_out, h_out, count_out, pos_out,
    lab_land, prop_land, uu_land, ui_land, ou_land, oi_land, oc_land, s_ref, m_ref,
    send_sem, recv_sem, local_sem,
):
    n = lax.axis_size("item")
    me = lax.axis_index("item")
    barrier = pltpu.get_barrier_semaphore()
    for k in range(1, n):
        pl.semaphore_signal(barrier, inc=1, device_id={"item": lax.rem(me + k, n)}, device_id_type=MESH)
    pl.semaphore_wait(barrier, n - 1)

    index_pairs = ((uu_x, uu_land), (ui_x, ui_land), (ou_x, ou_land), (oi_x, oi_land), (oc_x, oc_land))
    tile_pairs = ((lab_x, lab_land), (prop_x, prop_land))

    def send(which, src, dst, k):
        copy = pltpu.make_async_remote_copy(
            src_ref=src,
            dst_ref=dst,
            send_sem=send_sem.at[which, k - 1],
            recv_sem=recv_sem.at[which, k - 1],
            device_id={"item": lax.rem(me + k, n)},
            device_id_type=MESH,
        )
        copy.start()
        return copy

    index_copies = []
    for which, (x, land) in enumerate(index_pairs):
        local = pltpu.make_async_copy(x, land.at[me], local_sem.at[which])
        local.start()
        index_copies.append(local)
        for k in range(1, n):
            index_copies.append(send(which, x, land.at[me], k))
    tile_local = []
    tile_copies = [[] for _ in range(n)]
    for which, (x, land) in enumerate(tile_pairs):
        slot = len(index_pairs) + which
        local = pltpu.make_async_copy(x.at[me], land.at[me], local_sem.at[slot])
        local.start()
        tile_local.append(local)
        for k in range(1, n):
            tile_copies[k].append(send(slot, x.at[lax.rem(me + k, n)], land.at[me], k))

    dims = (((1,), (1,)), ((), ()))

    def block(k, carry):
        users = pl.ds(pl.multiple_of((k // item_blocks) * tile, tile), tile)
        items = pl.ds(pl.multiple_of((k % item_blocks) * tile, tile), tile)
        logits = lax.dot_general(up_ref[users, :], vp_ref[items, :], dims, preferred_element_type=jnp.float32)
        imputed = lax.dot_general(uimp_ref[users, :], vi_ref[items, :], dims, preferred_element_type=jnp.float32)
        s_ref[k] = logits
        m_ref[k] = imputed
        d_out[k] = ((jax.nn.sigmoid(logits) - jax.nn.sigmoid(imputed)) * loss_weight).astype(d_out.dtype)
        return carry

    lax.fori_loop(0, s_ref.shape[0], block, 0)

    for copy in index_copies:
        copy.wait()
    uno_slots = uu_land.shape[1] // n

    def tally(t, carry):
        origin = t // uno_slots
        slot = me * uno_slots + t % uno_slots
        count_out[t] = uu_land[origin, slot] * item_blocks + ui_land[origin, slot]
        return carry

    lax.fori_loop(0, n * uno_slots, tally, 0)

    def origin_tiles(origin):
        for place in range(obs_slots):
            slot = me * obs_slots + place
            t = origin * obs_slots + place
            pos = ou_land[origin, slot] * item_blocks + oi_land[origin, slot]
            pos_out[t] = pos
            valid = jnp.where(place < oc_land[origin, me], 1.0, 0.0).astype(jnp.float32)
            labels = lab_land[origin, pl.ds(place * tile, tile), :].astype(jnp.float32)
            propens = prop_land[origin, pl.ds(place * tile, tile), :].astype(jnp.float32)
            ograds, ohgrads = observed_grads(valid, s_ref[pos], m_ref[pos], labels, propens)
            g_out[t] = ograds
            h_out[t] = ohgrads

    for copy in tile_local:
        copy.wait()
    origin_tiles(me)
    for k in range(1, n):
        for copy in tile_copies[k]:
            copy.wait()
        origin_tiles(lax.rem(me + n - k, n))


def exchange_tiles(labels, propens, indices, factors, tile, item_blocks, obs_slots):
    n = lax.axis_size("item")
    n_blocks = (factors[0].shape[0] // tile) * item_blocks
    n_tiles = n * obs_slots
    vmem = pl.BlockSpec(memory_space=pltpu.VMEM)
    smem = pl.BlockSpec(memory_space=pltpu.SMEM)
    anyspace = pl.BlockSpec(memory_space=pl.ANY)
    return pl.pallas_call(
        functools.partial(gather_kernel, tile, item_blocks, obs_slots),
        out_shape=[
            jax.ShapeDtypeStruct((n_blocks, tile, tile), jnp.bfloat16),
            jax.ShapeDtypeStruct((n_tiles, tile, tile), jnp.bfloat16),
            jax.ShapeDtypeStruct((n_tiles, tile, tile), jnp.bfloat16),
            jax.ShapeDtypeStruct((indices[0].shape[0],), jnp.int32),
            jax.ShapeDtypeStruct((n_tiles,), jnp.int32),
        ],
        in_specs=[anyspace] * 7 + [vmem] * 4,
        out_specs=[vmem] * 3 + [smem] * 2,
        scratch_shapes=[
            pltpu.VMEM((n,) + labels.shape[1:], labels.dtype),
            pltpu.VMEM((n,) + propens.shape[1:], propens.dtype),
        ]
        + [pltpu.SMEM((n,) + x.shape, x.dtype) for x in indices]
        + [
            pltpu.VMEM((n_blocks, tile, tile), jnp.float32),
            pltpu.VMEM((n_blocks, tile, tile), jnp.float32),
            pltpu.SemaphoreType.DMA((7, n - 1)),
            pltpu.SemaphoreType.DMA((7, n - 1)),
            pltpu.SemaphoreType.DMA((7,)),
        ],
        compiler_params=pltpu.CompilerParams(collective_id=0, has_side_effects=True),
    )(labels, propens, *indices, *factors)


def tile_kernel(
    tile, user_blocks, item_blocks,
    slot_ref, pos_ref, d_ref, gt_ref, ht_ref, up_ref, ui_ref, vp_ref, vi_ref,
    user_out, item_out,
    count_ref, g_acc, h_acc, user_acc, item_acc,
):
    n_blocks = user_blocks * item_blocks
    for k in range(n_blocks):
        count_ref[k] = 0

    def tally(t, carry):
        k = slot_ref[t]
        count_ref[k] = count_ref[k] + 1
        return carry

    lax.fori_loop(0, slot_ref.shape[0], tally, 0)
    for k in range(n_blocks):
        g_acc[k] = count_ref[k].astype(jnp.float32) * d_ref[k].astype(jnp.float32)
        h_acc[k] = jnp.zeros((tile, tile), jnp.float32)

    def observed(t, carry):
        pos = pos_ref[t]
        g_acc[pos] += gt_ref[t].astype(jnp.float32)
        h_acc[pos] += ht_ref[t].astype(jnp.float32)
        return carry

    lax.fori_loop(0, gt_ref.shape[0], observed, 0)

    user_acc[...] = jnp.zeros(user_acc.shape, jnp.float32)
    item_acc[...] = jnp.zeros(item_acc.shape, jnp.float32)
    forward = (((1,), (0,)), ((), ()))
    backward = (((0,), (0,)), ((), ()))
    for ub in range(user_blocks):
        users = pl.ds(ub * tile, tile)
        for ib in range(item_blocks):
            items = pl.ds(ib * tile, tile)
            k = ub * item_blocks + ib
            for model, acc, u_ref, v_ref in ((0, g_acc, up_ref, vp_ref), (1, h_acc, ui_ref, vi_ref)):
                wide = acc[k]
                hi = wide.astype(jnp.bfloat16)
                lo = (wide - hi.astype(jnp.float32)).astype(jnp.bfloat16)
                v = v_ref[items, :]
                u = u_ref[users, :]
                user_acc[model, users, :] += lax.dot_general(
                    hi, v, forward, preferred_element_type=jnp.float32
                ) + lax.dot_general(lo, v, forward, preferred_element_type=jnp.float32)
                item_acc[model, items, :] += lax.dot_general(
                    hi, u, backward, preferred_element_type=jnp.float32
                ) + lax.dot_general(lo, u, backward, preferred_element_type=jnp.float32)
    user_rows = user_out.shape[2]
    for dest in range(user_out.shape[0]):
        user_out[dest] = user_acc[:, pl.ds(dest * user_rows, user_rows), :]
    item_rows = item_out.shape[2]
    for dest in range(item_out.shape[0]):
        item_out[dest] = item_acc[:, pl.ds(dest * item_rows, item_rows), :]


def convert_kernel(x_ref, y_ref):
    y_ref[...] = x_ref[...].astype(y_ref.dtype)


def to_bfloat16(x):
    block = (1,) + x.shape[1:]
    return pl.pallas_call(
        convert_kernel,
        grid=(x.shape[0],),
        out_shape=jax.ShapeDtypeStruct(x.shape, jnp.bfloat16),
        in_specs=[pl.BlockSpec(block, lambda i: (i, 0, 0))],
        out_specs=pl.BlockSpec(block, lambda i: (i, 0, 0)),
    )(x)


def shards(
    user_pred,
    user_imp,
    item_pred,
    item_imp,
    uno_user,
    uno_item,
    obs_user,
    obs_item,
    obs_count,
    obs_label,
    obs_prop,
):
    item_ways = lax.axis_size("item")
    user_ways = lax.axis_size("user")
    tile = obs_label.shape[-1]
    rank = user_pred.shape[1]
    user_rows = user_pred.shape[0]
    shard_rows = item_pred.shape[0]
    user_blocks = user_rows // tile
    item_blocks = shard_rows // tile
    n_blocks = user_blocks * item_blocks
    obs_slots = obs_user.shape[-1] // item_ways

    labels = to_bfloat16(obs_label.reshape(item_ways, obs_slots * tile, tile))
    propens = obs_prop.reshape(item_ways, obs_slots * tile, tile)
    indices = [x.reshape(x.shape[-1]) for x in (uno_user, uno_item, obs_user, obs_item, obs_count)]
    uno_grads, obs_grads, obs_hgrads, counts, tile_pos = exchange_tiles(
        labels, propens, indices, (user_pred, user_imp, item_pred, item_imp), tile, item_blocks, obs_slots
    )
    vmem = pl.BlockSpec(memory_space=pltpu.VMEM)
    smem = pl.BlockSpec(memory_space=pltpu.SMEM)
    user_chunks, item_chunks = pl.pallas_call(
        functools.partial(tile_kernel, tile, user_blocks, item_blocks),
        out_shape=[
            jax.ShapeDtypeStruct((item_ways, 2, user_rows // item_ways, rank), jnp.float32),
            jax.ShapeDtypeStruct((user_ways, 2, shard_rows // user_ways, rank), jnp.float32),
        ],
        in_specs=[smem] * 2 + [vmem] * 7,
        out_specs=[vmem, vmem],
        scratch_shapes=[
            pltpu.SMEM((n_blocks,), jnp.int32),
            pltpu.VMEM((n_blocks, tile, tile), jnp.float32),
            pltpu.VMEM((n_blocks, tile, tile), jnp.float32),
            pltpu.VMEM((2, user_rows, rank), jnp.float32),
            pltpu.VMEM((2, shard_rows, rank), jnp.float32),
        ],
    )(counts, tile_pos, uno_grads, obs_grads, obs_hgrads, user_pred, user_imp, item_pred, item_imp)
    user_share, item_share = reduce_exchange([(user_chunks, "item"), (item_chunks, "user")], 1)
    return (user_share[0], user_share[1], item_share[0], item_share[1])


def solution(mesh):
    in_specs = (
        P("user", None),
        P("user", None),
        P("item", None),
        P("item", None),
        P("user", "item", None),
        P("user", "item", None),
        P("user", "item", None),
        P("user", "item", None),
        P("user", "item", None),
        P("user", "item", None, None, None),
        P("user", "item", None, None, None),
    )
    out_specs = (
        P(("user", "item"), None),
        P(("user", "item"), None),
        P(("item", "user"), None),
        P(("item", "user"), None),
    )
    return jax.shard_map(shards, mesh=mesh, in_specs=in_specs, out_specs=out_specs, check_vma=False)
```

```python
import functools

import jax
import jax.numpy as jnp
from jax import lax
from jax.experimental import pallas as pl
from jax.experimental.pallas import tpu as pltpu
from jax.sharding import PartitionSpec as P

MESH = pl.DeviceIdType.MESH

loss_weight = 0.015625


def product(form, first, second):
    return jnp.einsum(form, first, second, preferred_element_type=jnp.float32)


def exchange_kernel(axes, whole, count, work_in, work, *refs):
    x_refs, y_refs = refs[:count], refs[count + work_in : 2 * count + work_in]
    send_sem, recv_sem, local_sem = refs[-3:]
    work_refs = refs[count : count + work_in] + refs[2 * count + work_in : -3]
    barrier = pltpu.get_barrier_semaphore()
    for axis in axes:
        n = lax.axis_size(axis)
        me = lax.axis_index(axis)
        for k in range(1, n):
            pl.semaphore_signal(barrier, inc=1, device_id={axis: lax.rem(me + k, n)}, device_id_type=MESH)
    pl.semaphore_wait(barrier, sum(lax.axis_size(axis) - 1 for axis in axes))
    copies = []
    slot = 0
    for which, axis in enumerate(axes):
        n = lax.axis_size(axis)
        me = lax.axis_index(axis)
        x_ref, y_ref = x_refs[which], y_refs[which]
        local = pltpu.make_async_copy(x_ref if whole[which] else x_ref.at[me], y_ref.at[me], local_sem.at[which])
        local.start()
        copies.append(local)
        for k in range(1, n):
            peer = lax.rem(me + k, n)
            copy = pltpu.make_async_remote_copy(
                src_ref=x_ref if whole[which] else x_ref.at[peer],
                dst_ref=y_ref.at[me],
                send_sem=send_sem.at[slot],
                recv_sem=recv_sem.at[slot],
                device_id={axis: peer},
                device_id_type=MESH,
            )
            copy.start()
            copies.append(copy)
            slot += 1
    if work is not None:
        work(*work_refs)
    for copy in copies:
        copy.wait()


def exchange(pairs, collective, work=None, work_inputs=(), work_outputs=(), whole=None):
    axes = tuple(axis for _, axis in pairs)
    arrays = [x for x, _ in pairs]
    whole = tuple(whole) if whole is not None else (False,) * len(arrays)
    shapes = [(lax.axis_size(axis),) + x.shape if w else x.shape for (x, axis), w in zip(pairs, whole)]
    slots = sum(lax.axis_size(axis) - 1 for axis in axes)
    vmem = pl.BlockSpec(memory_space=pltpu.VMEM)
    return pl.pallas_call(
        functools.partial(exchange_kernel, axes, whole, len(arrays), len(work_inputs), work),
        out_shape=[jax.ShapeDtypeStruct(shape, x.dtype) for shape, x in zip(shapes, arrays)] + list(work_outputs),
        in_specs=[pl.BlockSpec(memory_space=pl.ANY)] * len(arrays) + [vmem] * len(work_inputs),
        out_specs=[pl.BlockSpec(memory_space=pl.ANY)] * len(arrays) + [vmem] * len(work_outputs),
        scratch_shapes=[
            pltpu.SemaphoreType.DMA((slots,)),
            pltpu.SemaphoreType.DMA((slots,)),
            pltpu.SemaphoreType.DMA((len(arrays),)),
        ],
        compiler_params=pltpu.CompilerParams(collective_id=collective, has_side_effects=True),
    )(*arrays, *work_inputs)


def reduce_kernel(axes, *refs):
    count = len(axes)
    x_refs, out_refs = refs[:count], refs[count : 2 * count]
    land_refs = refs[2 * count : 3 * count]
    send_sem, recv_sem, local_sem = refs[3 * count :]
    barrier = pltpu.get_barrier_semaphore()
    for axis in axes:
        n = lax.axis_size(axis)
        me = lax.axis_index(axis)
        for k in range(1, n):
            pl.semaphore_signal(barrier, inc=1, device_id={axis: lax.rem(me + k, n)}, device_id_type=MESH)
    pl.semaphore_wait(barrier, sum(lax.axis_size(axis) - 1 for axis in axes))
    copies = [[] for _ in axes]
    slot = 0
    for which, axis in enumerate(axes):
        n = lax.axis_size(axis)
        me = lax.axis_index(axis)
        x_ref, land = x_refs[which], land_refs[which]
        local = pltpu.make_async_copy(x_ref.at[me], land.at[me], local_sem.at[which])
        local.start()
        copies[which].append(local)
        for k in range(1, n):
            peer = lax.rem(me + k, n)
            copy = pltpu.make_async_remote_copy(
                src_ref=x_ref.at[peer],
                dst_ref=land.at[me],
                send_sem=send_sem.at[slot],
                recv_sem=recv_sem.at[slot],
                device_id={axis: peer},
                device_id_type=MESH,
            )
            copy.start()
            copies[which].append(copy)
            slot += 1
    for which, axis in enumerate(axes):
        n = lax.axis_size(axis)
        me = lax.axis_index(axis)
        land = land_refs[which]
        copies[which][0].wait()
        total = land[me]
        for k in range(1, n):
            copies[which][k].wait()
            total = total + land[lax.rem(me + n - k, n)]
        out_refs[which][...] = total


def reduce_exchange(pairs, collective):
    axes = tuple(axis for _, axis in pairs)
    arrays = [x for x, _ in pairs]
    slots = sum(lax.axis_size(axis) - 1 for axis in axes)
    return pl.pallas_call(
        functools.partial(reduce_kernel, axes),
        out_shape=[jax.ShapeDtypeStruct(x.shape[1:], x.dtype) for x in arrays],
        in_specs=[pl.BlockSpec(memory_space=pl.ANY)] * len(arrays),
        out_specs=[pl.BlockSpec(memory_space=pltpu.VMEM)] * len(arrays),
        scratch_shapes=[pltpu.VMEM(x.shape, x.dtype) for x in arrays]
        + [
            pltpu.SemaphoreType.DMA((slots,)),
            pltpu.SemaphoreType.DMA((slots,)),
            pltpu.SemaphoreType.DMA((len(arrays),)),
        ],
        compiler_params=pltpu.CompilerParams(collective_id=collective, has_side_effects=True),
    )(*arrays)


def observed_grads(valid, ologits, imputed, labels, propens):
    predicted = jax.nn.sigmoid(ologits)
    imputes = jax.nn.sigmoid(imputed)
    seen = (labels > 0).astype(jnp.float32)
    clicks = (labels == 2).astype(jnp.float32)
    weight = valid * seen / propens
    ograds = ((valid * (predicted - imputes) + weight * (imputes - clicks)) * loss_weight).astype(jnp.bfloat16)
    ohgrads = (
        2.0 * weight * (imputes - clicks) * ologits * ologits * imputes * (1.0 - imputes) * loss_weight
    ).astype(jnp.bfloat16)
    return ograds, ohgrads


def gather_kernel(
    tile, item_blocks, obs_slots,
    lab_x, prop_x, uu_x, ui_x, ou_x, oi_x, oc_x, up_ref, uimp_ref, vp_ref, vi_ref,
    d_out, g_out, h_out, count_out, pos_out,
    lab_land, prop_land, uu_land, ui_land, ou_land, oi_land, oc_land, s_ref, m_ref,
    send_sem, recv_sem, local_sem,
):
    n = lax.axis_size("item")
    me = lax.axis_index("item")
    barrier = pltpu.get_barrier_semaphore()
    for k in range(1, n):
        pl.semaphore_signal(barrier, inc=1, device_id={"item": lax.rem(me + k, n)}, device_id_type=MESH)
    pl.semaphore_wait(barrier, n - 1)

    index_pairs = ((uu_x, uu_land), (ui_x, ui_land), (ou_x, ou_land), (oi_x, oi_land), (oc_x, oc_land))
    tile_pairs = ((lab_x, lab_land), (prop_x, prop_land))

    def send(which, src, dst, k):
        copy = pltpu.make_async_remote_copy(
            src_ref=src,
            dst_ref=dst,
            send_sem=send_sem.at[which, k - 1],
            recv_sem=recv_sem.at[which, k - 1],
            device_id={"item": lax.rem(me + k, n)},
            device_id_type=MESH,
        )
        copy.start()
        return copy

    index_copies = []
    for which, (x, land) in enumerate(index_pairs):
        local = pltpu.make_async_copy(x, land.at[me], local_sem.at[which])
        local.start()
        index_copies.append(local)
        for k in range(1, n):
            index_copies.append(send(which, x, land.at[me], k))
    tile_local = []
    tile_copies = [[] for _ in range(n)]
    for which, (x, land) in enumerate(tile_pairs):
        slot = len(index_pairs) + which
        local = pltpu.make_async_copy(x.at[me], land.at[me], local_sem.at[slot])
        local.start()
        tile_local.append(local)
        for k in range(1, n):
            tile_copies[k].append(send(slot, x.at[lax.rem(me + k, n)], land.at[me], k))

    dims = (((1,), (1,)), ((), ()))

    def block(k, carry):
        users = pl.ds(pl.multiple_of((k // item_blocks) * tile, tile), tile)
        items = pl.ds(pl.multiple_of((k % item_blocks) * tile, tile), tile)
        logits = lax.dot_general(up_ref[users, :], vp_ref[items, :], dims, preferred_element_type=jnp.float32)
        imputed = lax.dot_general(uimp_ref[users, :], vi_ref[items, :], dims, preferred_element_type=jnp.float32)
        s_ref[k] = logits
        m_ref[k] = imputed
        d_out[k] = ((jax.nn.sigmoid(logits) - jax.nn.sigmoid(imputed)) * loss_weight).astype(d_out.dtype)
        return carry

    lax.fori_loop(0, s_ref.shape[0], block, 0)

    for copy in index_copies:
        copy.wait()
    uno_slots = uu_land.shape[1] // n

    def tally(t, carry):
        origin = t // uno_slots
        slot = me * uno_slots + t % uno_slots
        count_out[t] = uu_land[origin, slot] * item_blocks + ui_land[origin, slot]
        return carry

    lax.fori_loop(0, n * uno_slots, tally, 0)

    def origin_tiles(origin):
        for place in range(obs_slots):
            slot = me * obs_slots + place
            t = origin * obs_slots + place
            pos = ou_land[origin, slot] * item_blocks + oi_land[origin, slot]
            pos_out[t] = pos
            valid = jnp.where(place < oc_land[origin, me], 1.0, 0.0).astype(jnp.float32)
            labels = lab_land[origin, pl.ds(place * tile, tile), :].astype(jnp.float32)
            propens = prop_land[origin, pl.ds(place * tile, tile), :].astype(jnp.float32)
            ograds, ohgrads = observed_grads(valid, s_ref[pos], m_ref[pos], labels, propens)
            g_out[t] = ograds
            h_out[t] = ohgrads

    for copy in tile_local:
        copy.wait()
    origin_tiles(me)
    for k in range(1, n):
        for copy in tile_copies[k]:
            copy.wait()
        origin_tiles(lax.rem(me + n - k, n))


def exchange_tiles(labels, propens, indices, factors, tile, item_blocks, obs_slots):
    n = lax.axis_size("item")
    n_blocks = (factors[0].shape[0] // tile) * item_blocks
    n_tiles = n * obs_slots
    vmem = pl.BlockSpec(memory_space=pltpu.VMEM)
    smem = pl.BlockSpec(memory_space=pltpu.SMEM)
    anyspace = pl.BlockSpec(memory_space=pl.ANY)
    return pl.pallas_call(
        functools.partial(gather_kernel, tile, item_blocks, obs_slots),
        out_shape=[
            jax.ShapeDtypeStruct((n_blocks, tile, tile), jnp.bfloat16),
            jax.ShapeDtypeStruct((n_tiles, tile, tile), jnp.bfloat16),
            jax.ShapeDtypeStruct((n_tiles, tile, tile), jnp.bfloat16),
            jax.ShapeDtypeStruct((indices[0].shape[0],), jnp.int32),
            jax.ShapeDtypeStruct((n_tiles,), jnp.int32),
        ],
        in_specs=[anyspace] * 7 + [vmem] * 4,
        out_specs=[vmem] * 3 + [smem] * 2,
        scratch_shapes=[
            pltpu.VMEM((n,) + labels.shape[1:], labels.dtype),
            pltpu.VMEM((n,) + propens.shape[1:], propens.dtype),
        ]
        + [pltpu.SMEM((n,) + x.shape, x.dtype) for x in indices]
        + [
            pltpu.VMEM((n_blocks, tile, tile), jnp.float32),
            pltpu.VMEM((n_blocks, tile, tile), jnp.float32),
            pltpu.SemaphoreType.DMA((7, n - 1)),
            pltpu.SemaphoreType.DMA((7, n - 1)),
            pltpu.SemaphoreType.DMA((7,)),
        ],
        compiler_params=pltpu.CompilerParams(collective_id=0, has_side_effects=True),
    )(labels, propens, *indices, *factors)


def tile_kernel(
    tile, user_blocks, item_blocks,
    slot_ref, pos_ref, d_ref, gt_ref, ht_ref, up_ref, ui_ref, vp_ref, vi_ref,
    user_out, item_out,
    count_ref, g_acc, h_acc, user_acc, item_acc,
):
    n_blocks = user_blocks * item_blocks
    for k in range(n_blocks):
        count_ref[k] = 0

    def tally(t, carry):
        k = slot_ref[t]
        count_ref[k] = count_ref[k] + 1
        return carry

    lax.fori_loop(0, slot_ref.shape[0], tally, 0)
    for k in range(n_blocks):
        g_acc[k] = count_ref[k].astype(jnp.float32) * d_ref[k].astype(jnp.float32)
        h_acc[k] = jnp.zeros((tile, tile), jnp.float32)

    def observed(t, carry):
        pos = pos_ref[t]
        g_acc[pos] += gt_ref[t].astype(jnp.float32)
        h_acc[pos] += ht_ref[t].astype(jnp.float32)
        return carry

    lax.fori_loop(0, gt_ref.shape[0], observed, 0)

    user_acc[...] = jnp.zeros(user_acc.shape, jnp.float32)
    item_acc[...] = jnp.zeros(item_acc.shape, jnp.float32)
    forward = (((1,), (0,)), ((), ()))
    backward = (((0,), (0,)), ((), ()))
    for ub in range(user_blocks):
        users = pl.ds(ub * tile, tile)
        for ib in range(item_blocks):
            items = pl.ds(ib * tile, tile)
            k = ub * item_blocks + ib
            for model, acc, u_ref, v_ref in ((0, g_acc, up_ref, vp_ref), (1, h_acc, ui_ref, vi_ref)):
                wide = acc[k]
                hi = wide.astype(jnp.bfloat16)
                lo = (wide - hi.astype(jnp.float32)).astype(jnp.bfloat16)
                v = v_ref[items, :]
                u = u_ref[users, :]
                user_acc[model, users, :] += lax.dot_general(
                    hi, v, forward, preferred_element_type=jnp.float32
                ) + lax.dot_general(lo, v, forward, preferred_element_type=jnp.float32)
                item_acc[model, items, :] += lax.dot_general(
                    hi, u, backward, preferred_element_type=jnp.float32
                ) + lax.dot_general(lo, u, backward, preferred_element_type=jnp.float32)
    user_rows = user_out.shape[2]
    for dest in range(user_out.shape[0]):
        user_out[dest] = user_acc[:, pl.ds(dest * user_rows, user_rows), :]
    item_rows = item_out.shape[2]
    for dest in range(item_out.shape[0]):
        item_out[dest] = item_acc[:, pl.ds(dest * item_rows, item_rows), :]


def shards(
    user_pred,
    user_imp,
    item_pred,
    item_imp,
    uno_user,
    uno_item,
    obs_user,
    obs_item,
    obs_count,
    obs_label,
    obs_prop,
):
    item_ways = lax.axis_size("item")
    user_ways = lax.axis_size("user")
    tile = obs_label.shape[-1]
    rank = user_pred.shape[1]
    user_rows = user_pred.shape[0]
    shard_rows = item_pred.shape[0]
    user_blocks = user_rows // tile
    item_blocks = shard_rows // tile
    n_blocks = user_blocks * item_blocks
    obs_slots = obs_user.shape[-1] // item_ways

    labels = obs_label.reshape(item_ways, obs_slots * tile, tile).astype(jnp.bfloat16)
    propens = obs_prop.reshape(item_ways, obs_slots * tile, tile)
    indices = [x.reshape(x.shape[-1]) for x in (uno_user, uno_item, obs_user, obs_item, obs_count)]
    uno_grads, obs_grads, obs_hgrads, counts, tile_pos = exchange_tiles(
        labels, propens, indices, (user_pred, user_imp, item_pred, item_imp), tile, item_blocks, obs_slots
    )
    vmem = pl.BlockSpec(memory_space=pltpu.VMEM)
    smem = pl.BlockSpec(memory_space=pltpu.SMEM)
    user_chunks, item_chunks = pl.pallas_call(
        functools.partial(tile_kernel, tile, user_blocks, item_blocks),
        out_shape=[
            jax.ShapeDtypeStruct((item_ways, 2, user_rows // item_ways, rank), jnp.float32),
            jax.ShapeDtypeStruct((user_ways, 2, shard_rows // user_ways, rank), jnp.float32),
        ],
        in_specs=[smem] * 2 + [vmem] * 7,
        out_specs=[vmem, vmem],
        scratch_shapes=[
            pltpu.SMEM((n_blocks,), jnp.int32),
            pltpu.VMEM((n_blocks, tile, tile), jnp.float32),
            pltpu.VMEM((n_blocks, tile, tile), jnp.float32),
            pltpu.VMEM((2, user_rows, rank), jnp.float32),
            pltpu.VMEM((2, shard_rows, rank), jnp.float32),
        ],
    )(counts, tile_pos, uno_grads, obs_grads, obs_hgrads, user_pred, user_imp, item_pred, item_imp)
    user_share, item_share = reduce_exchange([(user_chunks, "item"), (item_chunks, "user")], 1)
    return (user_share[0], user_share[1], item_share[0], item_share[1])


def solution(mesh):
    in_specs = (
        P("user", None),
        P("user", None),
        P("item", None),
        P("item", None),
        P("user", "item", None),
        P("user", "item", None),
        P("user", "item", None),
        P("user", "item", None),
        P("user", "item", None),
        P("user", "item", None, None, None),
        P("user", "item", None, None, None),
    )
    out_specs = (
        P(("user", "item"), None),
        P(("user", "item"), None),
        P(("item", "user"), None),
        P(("item", "user"), None),
    )
    return jax.shard_map(shards, mesh=mesh, in_specs=in_specs, out_specs=out_specs, check_vma=False)
```

```python
import functools

import jax
import jax.numpy as jnp
from jax import lax
from jax.experimental import pallas as pl
from jax.experimental.pallas import tpu as pltpu
from jax.sharding import PartitionSpec as P

MESH = pl.DeviceIdType.MESH

loss_weight = 0.015625


def product(form, first, second):
    return jnp.einsum(form, first, second, preferred_element_type=jnp.float32)


def exchange_kernel(axes, whole, count, work_in, work, *refs):
    x_refs, y_refs = refs[:count], refs[count + work_in : 2 * count + work_in]
    send_sem, recv_sem, local_sem = refs[-3:]
    work_refs = refs[count : count + work_in] + refs[2 * count + work_in : -3]
    barrier = pltpu.get_barrier_semaphore()
    for axis in axes:
        n = lax.axis_size(axis)
        me = lax.axis_index(axis)
        for k in range(1, n):
            pl.semaphore_signal(barrier, inc=1, device_id={axis: lax.rem(me + k, n)}, device_id_type=MESH)
    pl.semaphore_wait(barrier, sum(lax.axis_size(axis) - 1 for axis in axes))
    copies = []
    slot = 0
    for which, axis in enumerate(axes):
        n = lax.axis_size(axis)
        me = lax.axis_index(axis)
        x_ref, y_ref = x_refs[which], y_refs[which]
        local = pltpu.make_async_copy(x_ref if whole[which] else x_ref.at[me], y_ref.at[me], local_sem.at[which])
        local.start()
        copies.append(local)
        for k in range(1, n):
            peer = lax.rem(me + k, n)
            copy = pltpu.make_async_remote_copy(
                src_ref=x_ref if whole[which] else x_ref.at[peer],
                dst_ref=y_ref.at[me],
                send_sem=send_sem.at[slot],
                recv_sem=recv_sem.at[slot],
                device_id={axis: peer},
                device_id_type=MESH,
            )
            copy.start()
            copies.append(copy)
            slot += 1
    if work is not None:
        work(*work_refs)
    for copy in copies:
        copy.wait()


def exchange(pairs, collective, work=None, work_inputs=(), work_outputs=(), whole=None):
    axes = tuple(axis for _, axis in pairs)
    arrays = [x for x, _ in pairs]
    whole = tuple(whole) if whole is not None else (False,) * len(arrays)
    shapes = [(lax.axis_size(axis),) + x.shape if w else x.shape for (x, axis), w in zip(pairs, whole)]
    slots = sum(lax.axis_size(axis) - 1 for axis in axes)
    vmem = pl.BlockSpec(memory_space=pltpu.VMEM)
    return pl.pallas_call(
        functools.partial(exchange_kernel, axes, whole, len(arrays), len(work_inputs), work),
        out_shape=[jax.ShapeDtypeStruct(shape, x.dtype) for shape, x in zip(shapes, arrays)] + list(work_outputs),
        in_specs=[pl.BlockSpec(memory_space=pl.ANY)] * len(arrays) + [vmem] * len(work_inputs),
        out_specs=[pl.BlockSpec(memory_space=pl.ANY)] * len(arrays) + [vmem] * len(work_outputs),
        scratch_shapes=[
            pltpu.SemaphoreType.DMA((slots,)),
            pltpu.SemaphoreType.DMA((slots,)),
            pltpu.SemaphoreType.DMA((len(arrays),)),
        ],
        compiler_params=pltpu.CompilerParams(collective_id=collective, has_side_effects=True),
    )(*arrays, *work_inputs)


def reduce_kernel(axes, *refs):
    count = len(axes)
    x_refs, out_refs = refs[:count], refs[count : 2 * count]
    land_refs = refs[2 * count : 3 * count]
    send_sem, recv_sem, local_sem = refs[3 * count :]
    barrier = pltpu.get_barrier_semaphore()
    for axis in axes:
        n = lax.axis_size(axis)
        me = lax.axis_index(axis)
        for k in range(1, n):
            pl.semaphore_signal(barrier, inc=1, device_id={axis: lax.rem(me + k, n)}, device_id_type=MESH)
    pl.semaphore_wait(barrier, sum(lax.axis_size(axis) - 1 for axis in axes))
    copies = []
    slot = 0
    for which, axis in enumerate(axes):
        n = lax.axis_size(axis)
        me = lax.axis_index(axis)
        x_ref, land = x_refs[which], land_refs[which]
        local = pltpu.make_async_copy(x_ref.at[me], land.at[me], local_sem.at[which])
        local.start()
        copies.append(local)
        for k in range(1, n):
            peer = lax.rem(me + k, n)
            copy = pltpu.make_async_remote_copy(
                src_ref=x_ref.at[peer],
                dst_ref=land.at[me],
                send_sem=send_sem.at[slot],
                recv_sem=recv_sem.at[slot],
                device_id={axis: peer},
                device_id_type=MESH,
            )
            copy.start()
            copies.append(copy)
            slot += 1
    for copy in copies:
        copy.wait()
    for which in range(count):
        land = land_refs[which]
        total = land[0]
        for source in range(1, land.shape[0]):
            total = total + land[source]
        out_refs[which][...] = total


def reduce_exchange(pairs, collective):
    axes = tuple(axis for _, axis in pairs)
    arrays = [x for x, _ in pairs]
    slots = sum(lax.axis_size(axis) - 1 for axis in axes)
    return pl.pallas_call(
        functools.partial(reduce_kernel, axes),
        out_shape=[jax.ShapeDtypeStruct(x.shape[1:], x.dtype) for x in arrays],
        in_specs=[pl.BlockSpec(memory_space=pl.ANY)] * len(arrays),
        out_specs=[pl.BlockSpec(memory_space=pltpu.VMEM)] * len(arrays),
        scratch_shapes=[pltpu.VMEM(x.shape, x.dtype) for x in arrays]
        + [
            pltpu.SemaphoreType.DMA((slots,)),
            pltpu.SemaphoreType.DMA((slots,)),
            pltpu.SemaphoreType.DMA((len(arrays),)),
        ],
        compiler_params=pltpu.CompilerParams(collective_id=collective, has_side_effects=True),
    )(*arrays)


def observed_grads(valid, ologits, imputed, labels, propens):
    predicted = jax.nn.sigmoid(ologits)
    imputes = jax.nn.sigmoid(imputed)
    seen = (labels > 0).astype(jnp.float32)
    clicks = (labels == 2).astype(jnp.float32)
    weight = valid * seen / propens
    ograds = ((valid * (predicted - imputes) + weight * (imputes - clicks)) * loss_weight).astype(jnp.bfloat16)
    ohgrads = (
        2.0 * weight * (imputes - clicks) * ologits * ologits * imputes * (1.0 - imputes) * loss_weight
    ).astype(jnp.bfloat16)
    return ograds, ohgrads


def gather_kernel(
    tile, item_blocks, obs_slots,
    lab_x, prop_x, uu_x, ui_x, ou_x, oi_x, oc_x, up_ref, uimp_ref, vp_ref, vi_ref,
    user_out, item_out,
    lab_land, prop_land, uu_land, ui_land, ou_land, oi_land, oc_land, s_ref, m_ref, d_ref, user_acc, item_acc,
    send_sem, recv_sem, local_sem,
):
    n = lax.axis_size("item")
    me = lax.axis_index("item")
    barrier = pltpu.get_barrier_semaphore()
    for k in range(1, n):
        pl.semaphore_signal(barrier, inc=1, device_id={"item": lax.rem(me + k, n)}, device_id_type=MESH)
    pl.semaphore_wait(barrier, n - 1)

    index_pairs = ((uu_x, uu_land), (ui_x, ui_land), (ou_x, ou_land), (oi_x, oi_land), (oc_x, oc_land))
    tile_pairs = ((lab_x, lab_land), (prop_x, prop_land))

    def send(which, src, dst, k):
        copy = pltpu.make_async_remote_copy(
            src_ref=src,
            dst_ref=dst,
            send_sem=send_sem.at[which, k - 1],
            recv_sem=recv_sem.at[which, k - 1],
            device_id={"item": lax.rem(me + k, n)},
            device_id_type=MESH,
        )
        copy.start()
        return copy

    index_copies = []
    for which, (x, land) in enumerate(index_pairs):
        local = pltpu.make_async_copy(x, land.at[me], local_sem.at[which])
        local.start()
        index_copies.append(local)
        for k in range(1, n):
            index_copies.append(send(which, x, land.at[me], k))
    tile_local = []
    tile_copies = [[] for _ in range(n)]
    for which, (x, land) in enumerate(tile_pairs):
        slot = len(index_pairs) + which
        local = pltpu.make_async_copy(x.at[me], land.at[me], local_sem.at[slot])
        local.start()
        tile_local.append(local)
        for k in range(1, n):
            tile_copies[k].append(send(slot, x.at[lax.rem(me + k, n)], land.at[me], k))

    dims = (((1,), (1,)), ((), ()))

    def block(k, carry):
        ub = k // item_blocks
        ib = k % item_blocks
        logits = lax.dot_general(up_ref[ub], vp_ref[ib], dims, preferred_element_type=jnp.float32)
        imputed = lax.dot_general(uimp_ref[ub], vi_ref[ib], dims, preferred_element_type=jnp.float32)
        s_ref[k] = logits
        m_ref[k] = imputed
        d_ref[k] = ((jax.nn.sigmoid(logits) - jax.nn.sigmoid(imputed)) * loss_weight).astype(d_ref.dtype)
        return carry

    lax.fori_loop(0, s_ref.shape[0], block, 0)
    user_acc[...] = jnp.zeros(user_acc.shape, jnp.float32)
    item_acc[...] = jnp.zeros(item_acc.shape, jnp.float32)
    forward = (((1,), (0,)), ((), ()))
    backward = (((0,), (0,)), ((), ()))
    user_blocks = user_acc.shape[1] // tile

    for copy in index_copies:
        copy.wait()
    uno_slots = uu_land.shape[1] // n
    slots = []
    for t in range(n * uno_slots):
        origin = t // uno_slots
        slot = me * uno_slots + t % uno_slots
        slots.append(uu_land[origin, slot] * item_blocks + ui_land[origin, slot])
    for k in range(s_ref.shape[0]):
        count = jnp.where(slots[0] == k, 1.0, 0.0)
        for t in range(1, len(slots)):
            count = count + jnp.where(slots[t] == k, 1.0, 0.0)
        users = pl.ds((k // item_blocks) * tile, tile)
        items = pl.ds((k % item_blocks) * tile, tile)
        grads = d_ref[k]
        user_acc[0, users, :] += count * lax.dot_general(
            grads, vp_ref[k % item_blocks], forward, preferred_element_type=jnp.float32
        )
        item_acc[0, items, :] += count * lax.dot_general(
            grads, up_ref[k // item_blocks], backward, preferred_element_type=jnp.float32
        )

    def origin_tiles(origin):
        for place in range(obs_slots):
            slot = me * obs_slots + place
            ub = ou_land[origin, slot]
            ib = oi_land[origin, slot]
            pos = ub * item_blocks + ib
            valid = jnp.where(place < oc_land[origin, me], 1.0, 0.0).astype(jnp.float32)
            labels = lab_land[origin, pl.ds(place * tile, tile), :].astype(jnp.float32)
            propens = prop_land[origin, pl.ds(place * tile, tile), :].astype(jnp.float32)
            ograds, ohgrads = observed_grads(valid, s_ref[pos], m_ref[pos], labels, propens)
            terms = []
            for g, u_ref, v_ref in ((ograds, up_ref, vp_ref), (ohgrads, uimp_ref, vi_ref)):
                terms.append(
                    (
                        lax.dot_general(g, v_ref[ib], forward, preferred_element_type=jnp.float32),
                        lax.dot_general(g, u_ref[ub], backward, preferred_element_type=jnp.float32),
                    )
                )
            for b in range(user_blocks):
                hit = jnp.where(ub == b, 1.0, 0.0)
                for model in range(2):
                    user_acc[model, pl.ds(b * tile, tile), :] += hit * terms[model][0]
            for c in range(item_blocks):
                hit = jnp.where(ib == c, 1.0, 0.0)
                for model in range(2):
                    item_acc[model, pl.ds(c * tile, tile), :] += hit * terms[model][1]

    for copy in tile_local:
        copy.wait()
    origin_tiles(me)
    for k in range(1, n):
        for copy in tile_copies[k]:
            copy.wait()
        origin_tiles(lax.rem(me + n - k, n))
    user_rows = user_out.shape[2]
    for dest in range(user_out.shape[0]):
        user_out[dest] = user_acc[:, pl.ds(dest * user_rows, user_rows), :]
    item_rows = item_out.shape[2]
    for dest in range(item_out.shape[0]):
        item_out[dest] = item_acc[:, pl.ds(dest * item_rows, item_rows), :]


def exchange_tiles(labels, propens, indices, factors, tile, item_blocks, obs_slots, user_ways):
    n = lax.axis_size("item")
    user_rows, rank = factors[0].shape
    shard_rows = factors[2].shape[0]
    factors = [x.reshape(x.shape[0] // tile, tile, rank) for x in factors]
    n_blocks = factors[0].shape[0] * item_blocks
    n_tiles = n * obs_slots
    vmem = pl.BlockSpec(memory_space=pltpu.VMEM)
    smem = pl.BlockSpec(memory_space=pltpu.SMEM)
    anyspace = pl.BlockSpec(memory_space=pl.ANY)
    return pl.pallas_call(
        functools.partial(gather_kernel, tile, item_blocks, obs_slots),
        out_shape=[
            jax.ShapeDtypeStruct((n, 2, user_rows // n, rank), jnp.float32),
            jax.ShapeDtypeStruct((user_ways, 2, shard_rows // user_ways, rank), jnp.float32),
        ],
        in_specs=[anyspace] * 7 + [vmem] * 4,
        out_specs=[vmem] * 2,
        scratch_shapes=[
            pltpu.VMEM((n,) + labels.shape[1:], labels.dtype),
            pltpu.VMEM((n,) + propens.shape[1:], propens.dtype),
        ]
        + [pltpu.SMEM((n,) + x.shape, x.dtype) for x in indices]
        + [
            pltpu.VMEM((n_blocks, tile, tile), jnp.float32),
            pltpu.VMEM((n_blocks, tile, tile), jnp.float32),
            pltpu.VMEM((n_blocks, tile, tile), jnp.bfloat16),
            pltpu.VMEM((2, user_rows, rank), jnp.float32),
            pltpu.VMEM((2, shard_rows, rank), jnp.float32),
            pltpu.SemaphoreType.DMA((7, n - 1)),
            pltpu.SemaphoreType.DMA((7, n - 1)),
            pltpu.SemaphoreType.DMA((7,)),
        ],
        compiler_params=pltpu.CompilerParams(collective_id=0, has_side_effects=True),
    )(labels, propens, *indices, *factors)


def tile_kernel(
    tile, user_blocks, item_blocks,
    slot_ref, pos_ref, d_ref, gt_ref, ht_ref, up_ref, ui_ref, vp_ref, vi_ref,
    user_out, item_out,
    count_ref, g_acc, h_acc, user_acc, item_acc,
):
    n_blocks = user_blocks * item_blocks
    for k in range(n_blocks):
        count_ref[k] = 0

    def tally(t, carry):
        k = slot_ref[t]
        count_ref[k] = count_ref[k] + 1
        return carry

    lax.fori_loop(0, slot_ref.shape[0], tally, 0)
    for k in range(n_blocks):
        g_acc[k] = count_ref[k].astype(jnp.float32) * d_ref[k].astype(jnp.float32)
        h_acc[k] = jnp.zeros((tile, tile), jnp.float32)

    def observed(t, carry):
        pos = pos_ref[t]
        g_acc[pos] += gt_ref[t].astype(jnp.float32)
        h_acc[pos] += ht_ref[t].astype(jnp.float32)
        return carry

    lax.fori_loop(0, gt_ref.shape[0], observed, 0)

    user_acc[...] = jnp.zeros(user_acc.shape, jnp.float32)
    item_acc[...] = jnp.zeros(item_acc.shape, jnp.float32)
    forward = (((1,), (0,)), ((), ()))
    backward = (((0,), (0,)), ((), ()))
    for ub in range(user_blocks):
        users = pl.ds(ub * tile, tile)
        for ib in range(item_blocks):
            items = pl.ds(ib * tile, tile)
            k = ub * item_blocks + ib
            for model, acc, u_ref, v_ref in ((0, g_acc, up_ref, vp_ref), (1, h_acc, ui_ref, vi_ref)):
                wide = acc[k]
                hi = wide.astype(jnp.bfloat16)
                lo = (wide - hi.astype(jnp.float32)).astype(jnp.bfloat16)
                v = v_ref[items, :]
                u = u_ref[users, :]
                user_acc[model, users, :] += lax.dot_general(
                    hi, v, forward, preferred_element_type=jnp.float32
                ) + lax.dot_general(lo, v, forward, preferred_element_type=jnp.float32)
                item_acc[model, items, :] += lax.dot_general(
                    hi, u, backward, preferred_element_type=jnp.float32
                ) + lax.dot_general(lo, u, backward, preferred_element_type=jnp.float32)
    user_rows = user_out.shape[2]
    for dest in range(user_out.shape[0]):
        user_out[dest] = user_acc[:, pl.ds(dest * user_rows, user_rows), :]
    item_rows = item_out.shape[2]
    for dest in range(item_out.shape[0]):
        item_out[dest] = item_acc[:, pl.ds(dest * item_rows, item_rows), :]


def shards(
    user_pred,
    user_imp,
    item_pred,
    item_imp,
    uno_user,
    uno_item,
    obs_user,
    obs_item,
    obs_count,
    obs_label,
    obs_prop,
):
    item_ways = lax.axis_size("item")
    user_ways = lax.axis_size("user")
    tile = obs_label.shape[-1]
    rank = user_pred.shape[1]
    user_rows = user_pred.shape[0]
    shard_rows = item_pred.shape[0]
    user_blocks = user_rows // tile
    item_blocks = shard_rows // tile
    n_blocks = user_blocks * item_blocks
    obs_slots = obs_user.shape[-1] // item_ways

    labels = obs_label.reshape(item_ways, obs_slots * tile, tile).astype(jnp.bfloat16)
    propens = obs_prop.reshape(item_ways, obs_slots * tile, tile)
    indices = [x.reshape(x.shape[-1]) for x in (uno_user, uno_item, obs_user, obs_item, obs_count)]
    user_chunks, item_chunks = exchange_tiles(
        labels, propens, indices, (user_pred, user_imp, item_pred, item_imp), tile, item_blocks, obs_slots, user_ways
    )
    user_share, item_share = reduce_exchange([(user_chunks, "item"), (item_chunks, "user")], 1)
    return (user_share[0], user_share[1], item_share[0], item_share[1])


def solution(mesh):
    in_specs = (
        P("user", None),
        P("user", None),
        P("item", None),
        P("item", None),
        P("user", "item", None),
        P("user", "item", None),
        P("user", "item", None),
        P("user", "item", None),
        P("user", "item", None),
        P("user", "item", None, None, None),
        P("user", "item", None, None, None),
    )
    out_specs = (
        P(("user", "item"), None),
        P(("user", "item"), None),
        P(("item", "user"), None),
        P(("item", "user"), None),
    )
    return jax.shard_map(shards, mesh=mesh, in_specs=in_specs, out_specs=out_specs, check_vma=False)
```

```python
import functools

import jax
import jax.numpy as jnp
from jax import lax
from jax.experimental import pallas as pl
from jax.experimental.pallas import tpu as pltpu
from jax.sharding import PartitionSpec as P

MESH = pl.DeviceIdType.MESH

loss_weight = 0.015625


def product(form, first, second):
    return jnp.einsum(form, first, second, preferred_element_type=jnp.float32)


def exchange_kernel(axes, whole, count, work_in, work, *refs):
    x_refs, y_refs = refs[:count], refs[count + work_in : 2 * count + work_in]
    send_sem, recv_sem, local_sem = refs[-3:]
    work_refs = refs[count : count + work_in] + refs[2 * count + work_in : -3]
    barrier = pltpu.get_barrier_semaphore()
    for axis in axes:
        n = lax.axis_size(axis)
        me = lax.axis_index(axis)
        for k in range(1, n):
            pl.semaphore_signal(barrier, inc=1, device_id={axis: lax.rem(me + k, n)}, device_id_type=MESH)
    pl.semaphore_wait(barrier, sum(lax.axis_size(axis) - 1 for axis in axes))
    copies = []
    slot = 0
    for which, axis in enumerate(axes):
        n = lax.axis_size(axis)
        me = lax.axis_index(axis)
        x_ref, y_ref = x_refs[which], y_refs[which]
        local = pltpu.make_async_copy(x_ref if whole[which] else x_ref.at[me], y_ref.at[me], local_sem.at[which])
        local.start()
        copies.append(local)
        for k in range(1, n):
            peer = lax.rem(me + k, n)
            copy = pltpu.make_async_remote_copy(
                src_ref=x_ref if whole[which] else x_ref.at[peer],
                dst_ref=y_ref.at[me],
                send_sem=send_sem.at[slot],
                recv_sem=recv_sem.at[slot],
                device_id={axis: peer},
                device_id_type=MESH,
            )
            copy.start()
            copies.append(copy)
            slot += 1
    if work is not None:
        work(*work_refs)
    for copy in copies:
        copy.wait()


def exchange(pairs, collective, work=None, work_inputs=(), work_outputs=(), whole=None):
    axes = tuple(axis for _, axis in pairs)
    arrays = [x for x, _ in pairs]
    whole = tuple(whole) if whole is not None else (False,) * len(arrays)
    shapes = [(lax.axis_size(axis),) + x.shape if w else x.shape for (x, axis), w in zip(pairs, whole)]
    slots = sum(lax.axis_size(axis) - 1 for axis in axes)
    vmem = pl.BlockSpec(memory_space=pltpu.VMEM)
    return pl.pallas_call(
        functools.partial(exchange_kernel, axes, whole, len(arrays), len(work_inputs), work),
        out_shape=[jax.ShapeDtypeStruct(shape, x.dtype) for shape, x in zip(shapes, arrays)] + list(work_outputs),
        in_specs=[pl.BlockSpec(memory_space=pl.ANY)] * len(arrays) + [vmem] * len(work_inputs),
        out_specs=[pl.BlockSpec(memory_space=pl.ANY)] * len(arrays) + [vmem] * len(work_outputs),
        scratch_shapes=[
            pltpu.SemaphoreType.DMA((slots,)),
            pltpu.SemaphoreType.DMA((slots,)),
            pltpu.SemaphoreType.DMA((len(arrays),)),
        ],
        compiler_params=pltpu.CompilerParams(collective_id=collective, has_side_effects=True),
    )(*arrays, *work_inputs)


def reduce_kernel(axes, *refs):
    count = len(axes)
    x_refs, out_refs = refs[:count], refs[count : 2 * count]
    land_refs = refs[2 * count : 3 * count]
    send_sem, recv_sem, local_sem = refs[3 * count :]
    barrier = pltpu.get_barrier_semaphore()
    for axis in axes:
        n = lax.axis_size(axis)
        me = lax.axis_index(axis)
        for k in range(1, n):
            pl.semaphore_signal(barrier, inc=1, device_id={axis: lax.rem(me + k, n)}, device_id_type=MESH)
    pl.semaphore_wait(barrier, sum(lax.axis_size(axis) - 1 for axis in axes))
    copies = []
    slot = 0
    for which, axis in enumerate(axes):
        n = lax.axis_size(axis)
        me = lax.axis_index(axis)
        x_ref, land = x_refs[which], land_refs[which]
        local = pltpu.make_async_copy(x_ref.at[me], land.at[me], local_sem.at[which])
        local.start()
        copies.append(local)
        for k in range(1, n):
            peer = lax.rem(me + k, n)
            copy = pltpu.make_async_remote_copy(
                src_ref=x_ref.at[peer],
                dst_ref=land.at[me],
                send_sem=send_sem.at[slot],
                recv_sem=recv_sem.at[slot],
                device_id={axis: peer},
                device_id_type=MESH,
            )
            copy.start()
            copies.append(copy)
            slot += 1
    for copy in copies:
        copy.wait()
    for which in range(count):
        land = land_refs[which]
        total = land[0]
        for source in range(1, land.shape[0]):
            total = total + land[source]
        out_refs[which][...] = total


def reduce_exchange(pairs, collective):
    axes = tuple(axis for _, axis in pairs)
    arrays = [x for x, _ in pairs]
    slots = sum(lax.axis_size(axis) - 1 for axis in axes)
    return pl.pallas_call(
        functools.partial(reduce_kernel, axes),
        out_shape=[jax.ShapeDtypeStruct(x.shape[1:], x.dtype) for x in arrays],
        in_specs=[pl.BlockSpec(memory_space=pl.ANY)] * len(arrays),
        out_specs=[pl.BlockSpec(memory_space=pltpu.VMEM)] * len(arrays),
        scratch_shapes=[pltpu.VMEM(x.shape, x.dtype) for x in arrays]
        + [
            pltpu.SemaphoreType.DMA((slots,)),
            pltpu.SemaphoreType.DMA((slots,)),
            pltpu.SemaphoreType.DMA((len(arrays),)),
        ],
        compiler_params=pltpu.CompilerParams(collective_id=collective, has_side_effects=True),
    )(*arrays)


def observed_grads(valid, ologits, imputed, labels, propens):
    predicted = jax.nn.sigmoid(ologits)
    imputes = jax.nn.sigmoid(imputed)
    seen = (labels > 0).astype(jnp.float32)
    clicks = (labels == 2).astype(jnp.float32)
    weight = valid * seen / propens
    ograds = ((valid * (predicted - imputes) + weight * (imputes - clicks)) * loss_weight).astype(jnp.bfloat16)
    ohgrads = (
        2.0 * weight * (imputes - clicks) * ologits * ologits * imputes * (1.0 - imputes) * loss_weight
    ).astype(jnp.bfloat16)
    return ograds, ohgrads


def gather_kernel(
    tile, item_blocks, obs_slots,
    lab_x, prop_x, uu_x, ui_x, ou_x, oi_x, oc_x, up_ref, uimp_ref, vp_ref, vi_ref,
    user_pred_out, user_imp_out, item_pred_out, item_imp_out,
    lab_land, prop_land, uu_land, ui_land, ou_land, oi_land, oc_land, s_ref, m_ref, d_ref, user_acc, item_acc,
    user_land, item_land, send_sem, recv_sem, local_sem, sum_send, sum_recv, sum_local,
):
    n = lax.axis_size("item")
    me = lax.axis_index("item")
    barrier = pltpu.get_barrier_semaphore()
    user_n = lax.axis_size("user")
    me_user = lax.axis_index("user")
    for k in range(1, n):
        pl.semaphore_signal(barrier, inc=1, device_id={"item": lax.rem(me + k, n)}, device_id_type=MESH)
    for k in range(1, user_n):
        pl.semaphore_signal(barrier, inc=1, device_id={"user": lax.rem(me_user + k, user_n)}, device_id_type=MESH)
    pl.semaphore_wait(barrier, (n - 1) + (user_n - 1))

    index_pairs = ((uu_x, uu_land), (ui_x, ui_land), (ou_x, ou_land), (oi_x, oi_land), (oc_x, oc_land))
    tile_pairs = ((lab_x, lab_land), (prop_x, prop_land))

    def send(which, src, dst, k):
        copy = pltpu.make_async_remote_copy(
            src_ref=src,
            dst_ref=dst,
            send_sem=send_sem.at[which, k - 1],
            recv_sem=recv_sem.at[which, k - 1],
            device_id={"item": lax.rem(me + k, n)},
            device_id_type=MESH,
        )
        copy.start()
        return copy

    index_copies = []
    for which, (x, land) in enumerate(index_pairs):
        local = pltpu.make_async_copy(x, land.at[me], local_sem.at[which])
        local.start()
        index_copies.append(local)
        for k in range(1, n):
            index_copies.append(send(which, x, land.at[me], k))
    tile_local = []
    tile_copies = [[] for _ in range(n)]
    for which, (x, land) in enumerate(tile_pairs):
        slot = len(index_pairs) + which
        local = pltpu.make_async_copy(x.at[me], land.at[me], local_sem.at[slot])
        local.start()
        tile_local.append(local)
        for k in range(1, n):
            tile_copies[k].append(send(slot, x.at[lax.rem(me + k, n)], land.at[me], k))

    dims = (((1,), (1,)), ((), ()))

    def block(k, carry):
        ub = k // item_blocks
        ib = k % item_blocks
        logits = lax.dot_general(up_ref[ub], vp_ref[ib], dims, preferred_element_type=jnp.float32)
        imputed = lax.dot_general(uimp_ref[ub], vi_ref[ib], dims, preferred_element_type=jnp.float32)
        s_ref[k] = logits
        m_ref[k] = imputed
        d_ref[k] = ((jax.nn.sigmoid(logits) - jax.nn.sigmoid(imputed)) * loss_weight).astype(d_ref.dtype)
        return carry

    lax.fori_loop(0, s_ref.shape[0], block, 0)
    user_acc[...] = jnp.zeros(user_acc.shape, jnp.float32)
    item_acc[...] = jnp.zeros(item_acc.shape, jnp.float32)
    forward = (((1,), (0,)), ((), ()))
    backward = (((0,), (0,)), ((), ()))
    user_blocks = user_acc.shape[1] // tile

    for copy in index_copies:
        copy.wait()
    uno_slots = uu_land.shape[1] // n
    slots = []
    for t in range(n * uno_slots):
        origin = t // uno_slots
        slot = me * uno_slots + t % uno_slots
        slots.append(uu_land[origin, slot] * item_blocks + ui_land[origin, slot])
    for k in range(s_ref.shape[0]):
        count = jnp.where(slots[0] == k, 1.0, 0.0)
        for t in range(1, len(slots)):
            count = count + jnp.where(slots[t] == k, 1.0, 0.0)
        users = pl.ds((k // item_blocks) * tile, tile)
        items = pl.ds((k % item_blocks) * tile, tile)
        grads = d_ref[k]
        user_acc[0, users, :] += count * lax.dot_general(
            grads, vp_ref[k % item_blocks], forward, preferred_element_type=jnp.float32
        )
        item_acc[0, items, :] += count * lax.dot_general(
            grads, up_ref[k // item_blocks], backward, preferred_element_type=jnp.float32
        )

    def origin_tiles(origin):
        for place in range(obs_slots):
            slot = me * obs_slots + place
            ub = ou_land[origin, slot]
            ib = oi_land[origin, slot]
            pos = ub * item_blocks + ib
            valid = jnp.where(place < oc_land[origin, me], 1.0, 0.0).astype(jnp.float32)
            labels = lab_land[origin, pl.ds(place * tile, tile), :].astype(jnp.float32)
            propens = prop_land[origin, pl.ds(place * tile, tile), :].astype(jnp.float32)
            ograds, ohgrads = observed_grads(valid, s_ref[pos], m_ref[pos], labels, propens)
            terms = []
            for g, u_ref, v_ref in ((ograds, up_ref, vp_ref), (ohgrads, uimp_ref, vi_ref)):
                terms.append(
                    (
                        lax.dot_general(g, v_ref[ib], forward, preferred_element_type=jnp.float32),
                        lax.dot_general(g, u_ref[ub], backward, preferred_element_type=jnp.float32),
                    )
                )
            for b in range(user_blocks):
                hit = jnp.where(ub == b, 1.0, 0.0)
                for model in range(2):
                    user_acc[model, pl.ds(b * tile, tile), :] += hit * terms[model][0]
            for c in range(item_blocks):
                hit = jnp.where(ib == c, 1.0, 0.0)
                for model in range(2):
                    item_acc[model, pl.ds(c * tile, tile), :] += hit * terms[model][1]

    for copy in tile_local:
        copy.wait()
    origin_tiles(me)
    for k in range(1, n):
        for copy in tile_copies[k]:
            copy.wait()
        origin_tiles(lax.rem(me + n - k, n))
    sums = []
    for which, (acc, land, axis, me_at, size) in enumerate(
        ((user_acc, user_land, "item", me, n), (item_acc, item_land, "user", me_user, user_n))
    ):
        rows = land.shape[2]
        local = pltpu.make_async_copy(acc.at[:, pl.ds(me_at * rows, rows), :], land.at[me_at], sum_local.at[which])
        local.start()
        copies = [local]
        for k in range(1, size):
            peer = lax.rem(me_at + k, size)
            copy = pltpu.make_async_remote_copy(
                src_ref=acc.at[:, pl.ds(peer * rows, rows), :],
                dst_ref=land.at[me_at],
                send_sem=sum_send.at[which, k - 1],
                recv_sem=sum_recv.at[which, k - 1],
                device_id={axis: peer},
                device_id_type=MESH,
            )
            copy.start()
            copies.append(copy)
        sums.append(copies)
    for copies in sums:
        for copy in copies:
            copy.wait()
    for land, outs in ((user_land, (user_pred_out, user_imp_out)), (item_land, (item_pred_out, item_imp_out))):
        total = land[0]
        for source in range(1, land.shape[0]):
            total = total + land[source]
        outs[0][...] = total[0]
        outs[1][...] = total[1]


def exchange_tiles(labels, propens, indices, factors, tile, item_blocks, obs_slots, user_ways):
    n = lax.axis_size("item")
    user_rows, rank = factors[0].shape
    shard_rows = factors[2].shape[0]
    factors = [x.reshape(x.shape[0] // tile, tile, rank) for x in factors]
    n_blocks = factors[0].shape[0] * item_blocks
    n_tiles = n * obs_slots
    vmem = pl.BlockSpec(memory_space=pltpu.VMEM)
    smem = pl.BlockSpec(memory_space=pltpu.SMEM)
    anyspace = pl.BlockSpec(memory_space=pl.ANY)
    return pl.pallas_call(
        functools.partial(gather_kernel, tile, item_blocks, obs_slots),
        out_shape=[jax.ShapeDtypeStruct((user_rows // n, rank), jnp.float32)] * 2
        + [jax.ShapeDtypeStruct((shard_rows // user_ways, rank), jnp.float32)] * 2,
        in_specs=[anyspace] * 7 + [vmem] * 4,
        out_specs=[vmem] * 4,
        scratch_shapes=[
            pltpu.VMEM((n,) + labels.shape[1:], labels.dtype),
            pltpu.VMEM((n,) + propens.shape[1:], propens.dtype),
        ]
        + [pltpu.SMEM((n,) + x.shape, x.dtype) for x in indices]
        + [
            pltpu.VMEM((n_blocks, tile, tile), jnp.float32),
            pltpu.VMEM((n_blocks, tile, tile), jnp.float32),
            pltpu.VMEM((n_blocks, tile, tile), jnp.bfloat16),
            pltpu.VMEM((2, user_rows, rank), jnp.float32),
            pltpu.VMEM((2, shard_rows, rank), jnp.float32),
            pltpu.VMEM((n, 2, user_rows // n, rank), jnp.float32),
            pltpu.VMEM((user_ways, 2, shard_rows // user_ways, rank), jnp.float32),
            pltpu.SemaphoreType.DMA((7, n - 1)),
            pltpu.SemaphoreType.DMA((7, n - 1)),
            pltpu.SemaphoreType.DMA((7,)),
            pltpu.SemaphoreType.DMA((2, max(n, user_ways) - 1)),
            pltpu.SemaphoreType.DMA((2, max(n, user_ways) - 1)),
            pltpu.SemaphoreType.DMA((2,)),
        ],
        compiler_params=pltpu.CompilerParams(collective_id=0, has_side_effects=True),
    )(labels, propens, *indices, *factors)


def tile_kernel(
    tile, user_blocks, item_blocks,
    slot_ref, pos_ref, d_ref, gt_ref, ht_ref, up_ref, ui_ref, vp_ref, vi_ref,
    user_out, item_out,
    count_ref, g_acc, h_acc, user_acc, item_acc,
):
    n_blocks = user_blocks * item_blocks
    for k in range(n_blocks):
        count_ref[k] = 0

    def tally(t, carry):
        k = slot_ref[t]
        count_ref[k] = count_ref[k] + 1
        return carry

    lax.fori_loop(0, slot_ref.shape[0], tally, 0)
    for k in range(n_blocks):
        g_acc[k] = count_ref[k].astype(jnp.float32) * d_ref[k].astype(jnp.float32)
        h_acc[k] = jnp.zeros((tile, tile), jnp.float32)

    def observed(t, carry):
        pos = pos_ref[t]
        g_acc[pos] += gt_ref[t].astype(jnp.float32)
        h_acc[pos] += ht_ref[t].astype(jnp.float32)
        return carry

    lax.fori_loop(0, gt_ref.shape[0], observed, 0)

    user_acc[...] = jnp.zeros(user_acc.shape, jnp.float32)
    item_acc[...] = jnp.zeros(item_acc.shape, jnp.float32)
    forward = (((1,), (0,)), ((), ()))
    backward = (((0,), (0,)), ((), ()))
    for ub in range(user_blocks):
        users = pl.ds(ub * tile, tile)
        for ib in range(item_blocks):
            items = pl.ds(ib * tile, tile)
            k = ub * item_blocks + ib
            for model, acc, u_ref, v_ref in ((0, g_acc, up_ref, vp_ref), (1, h_acc, ui_ref, vi_ref)):
                wide = acc[k]
                hi = wide.astype(jnp.bfloat16)
                lo = (wide - hi.astype(jnp.float32)).astype(jnp.bfloat16)
                v = v_ref[items, :]
                u = u_ref[users, :]
                user_acc[model, users, :] += lax.dot_general(
                    hi, v, forward, preferred_element_type=jnp.float32
                ) + lax.dot_general(lo, v, forward, preferred_element_type=jnp.float32)
                item_acc[model, items, :] += lax.dot_general(
                    hi, u, backward, preferred_element_type=jnp.float32
                ) + lax.dot_general(lo, u, backward, preferred_element_type=jnp.float32)
    user_rows = user_out.shape[2]
    for dest in range(user_out.shape[0]):
        user_out[dest] = user_acc[:, pl.ds(dest * user_rows, user_rows), :]
    item_rows = item_out.shape[2]
    for dest in range(item_out.shape[0]):
        item_out[dest] = item_acc[:, pl.ds(dest * item_rows, item_rows), :]


def shards(
    user_pred,
    user_imp,
    item_pred,
    item_imp,
    uno_user,
    uno_item,
    obs_user,
    obs_item,
    obs_count,
    obs_label,
    obs_prop,
):
    item_ways = lax.axis_size("item")
    user_ways = lax.axis_size("user")
    tile = obs_label.shape[-1]
    rank = user_pred.shape[1]
    user_rows = user_pred.shape[0]
    shard_rows = item_pred.shape[0]
    user_blocks = user_rows // tile
    item_blocks = shard_rows // tile
    n_blocks = user_blocks * item_blocks
    obs_slots = obs_user.shape[-1] // item_ways

    labels = obs_label.reshape(item_ways, obs_slots * tile, tile).astype(jnp.bfloat16)
    propens = obs_prop.reshape(item_ways, obs_slots * tile, tile)
    indices = [x.reshape(x.shape[-1]) for x in (uno_user, uno_item, obs_user, obs_item, obs_count)]
    return tuple(
        exchange_tiles(
            labels, propens, indices, (user_pred, user_imp, item_pred, item_imp), tile, item_blocks, obs_slots,
            user_ways,
        )
    )


def solution(mesh):
    in_specs = (
        P("user", None),
        P("user", None),
        P("item", None),
        P("item", None),
        P("user", "item", None),
        P("user", "item", None),
        P("user", "item", None),
        P("user", "item", None),
        P("user", "item", None),
        P("user", "item", None, None, None),
        P("user", "item", None, None, None),
    )
    out_specs = (
        P(("user", "item"), None),
        P(("user", "item"), None),
        P(("item", "user"), None),
        P(("item", "user"), None),
    )
    return jax.shard_map(shards, mesh=mesh, in_specs=in_specs, out_specs=out_specs, check_vma=False)
```

```python
import functools

import jax
import jax.numpy as jnp
from jax import lax
from jax.experimental import pallas as pl
from jax.experimental.pallas import tpu as pltpu
from jax.sharding import PartitionSpec as P

MESH = pl.DeviceIdType.MESH

loss_weight = 0.015625


def product(form, first, second):
    return jnp.einsum(form, first, second, preferred_element_type=jnp.float32)


def exchange_kernel(axes, whole, count, work_in, work, *refs):
    x_refs, y_refs = refs[:count], refs[count + work_in : 2 * count + work_in]
    send_sem, recv_sem, local_sem = refs[-3:]
    work_refs = refs[count : count + work_in] + refs[2 * count + work_in : -3]
    barrier = pltpu.get_barrier_semaphore()
    for axis in axes:
        n = lax.axis_size(axis)
        me = lax.axis_index(axis)
        for k in range(1, n):
            pl.semaphore_signal(barrier, inc=1, device_id={axis: lax.rem(me + k, n)}, device_id_type=MESH)
    pl.semaphore_wait(barrier, sum(lax.axis_size(axis) - 1 for axis in axes))
    copies = []
    slot = 0
    for which, axis in enumerate(axes):
        n = lax.axis_size(axis)
        me = lax.axis_index(axis)
        x_ref, y_ref = x_refs[which], y_refs[which]
        local = pltpu.make_async_copy(x_ref if whole[which] else x_ref.at[me], y_ref.at[me], local_sem.at[which])
        local.start()
        copies.append(local)
        for k in range(1, n):
            peer = lax.rem(me + k, n)
            copy = pltpu.make_async_remote_copy(
                src_ref=x_ref if whole[which] else x_ref.at[peer],
                dst_ref=y_ref.at[me],
                send_sem=send_sem.at[slot],
                recv_sem=recv_sem.at[slot],
                device_id={axis: peer},
                device_id_type=MESH,
            )
            copy.start()
            copies.append(copy)
            slot += 1
    if work is not None:
        work(*work_refs)
    for copy in copies:
        copy.wait()


def exchange(pairs, collective, work=None, work_inputs=(), work_outputs=(), whole=None):
    axes = tuple(axis for _, axis in pairs)
    arrays = [x for x, _ in pairs]
    whole = tuple(whole) if whole is not None else (False,) * len(arrays)
    shapes = [(lax.axis_size(axis),) + x.shape if w else x.shape for (x, axis), w in zip(pairs, whole)]
    slots = sum(lax.axis_size(axis) - 1 for axis in axes)
    vmem = pl.BlockSpec(memory_space=pltpu.VMEM)
    return pl.pallas_call(
        functools.partial(exchange_kernel, axes, whole, len(arrays), len(work_inputs), work),
        out_shape=[jax.ShapeDtypeStruct(shape, x.dtype) for shape, x in zip(shapes, arrays)] + list(work_outputs),
        in_specs=[pl.BlockSpec(memory_space=pl.ANY)] * len(arrays) + [vmem] * len(work_inputs),
        out_specs=[pl.BlockSpec(memory_space=pl.ANY)] * len(arrays) + [vmem] * len(work_outputs),
        scratch_shapes=[
            pltpu.SemaphoreType.DMA((slots,)),
            pltpu.SemaphoreType.DMA((slots,)),
            pltpu.SemaphoreType.DMA((len(arrays),)),
        ],
        compiler_params=pltpu.CompilerParams(collective_id=collective, has_side_effects=True),
    )(*arrays, *work_inputs)


def reduce_kernel(axes, *refs):
    count = len(axes)
    x_refs, out_refs = refs[:count], refs[count : 2 * count]
    land_refs = refs[2 * count : 3 * count]
    send_sem, recv_sem, local_sem = refs[3 * count :]
    barrier = pltpu.get_barrier_semaphore()
    for axis in axes:
        n = lax.axis_size(axis)
        me = lax.axis_index(axis)
        for k in range(1, n):
            pl.semaphore_signal(barrier, inc=1, device_id={axis: lax.rem(me + k, n)}, device_id_type=MESH)
    pl.semaphore_wait(barrier, sum(lax.axis_size(axis) - 1 for axis in axes))
    copies = []
    slot = 0
    for which, axis in enumerate(axes):
        n = lax.axis_size(axis)
        me = lax.axis_index(axis)
        x_ref, land = x_refs[which], land_refs[which]
        local = pltpu.make_async_copy(x_ref.at[me], land.at[me], local_sem.at[which])
        local.start()
        copies.append(local)
        for k in range(1, n):
            peer = lax.rem(me + k, n)
            copy = pltpu.make_async_remote_copy(
                src_ref=x_ref.at[peer],
                dst_ref=land.at[me],
                send_sem=send_sem.at[slot],
                recv_sem=recv_sem.at[slot],
                device_id={axis: peer},
                device_id_type=MESH,
            )
            copy.start()
            copies.append(copy)
            slot += 1
    for copy in copies:
        copy.wait()
    for which in range(count):
        land = land_refs[which]
        total = land[0]
        for source in range(1, land.shape[0]):
            total = total + land[source]
        out_refs[which][...] = total


def reduce_exchange(pairs, collective):
    axes = tuple(axis for _, axis in pairs)
    arrays = [x for x, _ in pairs]
    slots = sum(lax.axis_size(axis) - 1 for axis in axes)
    return pl.pallas_call(
        functools.partial(reduce_kernel, axes),
        out_shape=[jax.ShapeDtypeStruct(x.shape[1:], x.dtype) for x in arrays],
        in_specs=[pl.BlockSpec(memory_space=pl.ANY)] * len(arrays),
        out_specs=[pl.BlockSpec(memory_space=pltpu.VMEM)] * len(arrays),
        scratch_shapes=[pltpu.VMEM(x.shape, x.dtype) for x in arrays]
        + [
            pltpu.SemaphoreType.DMA((slots,)),
            pltpu.SemaphoreType.DMA((slots,)),
            pltpu.SemaphoreType.DMA((len(arrays),)),
        ],
        compiler_params=pltpu.CompilerParams(collective_id=collective, has_side_effects=True),
    )(*arrays)


def observed_grads(valid, ologits, imputed, labels, propens):
    predicted = jax.nn.sigmoid(ologits)
    imputes = jax.nn.sigmoid(imputed)
    seen = (labels > 0).astype(jnp.float32)
    clicks = (labels == 2).astype(jnp.float32)
    weight = valid * seen / propens
    ograds = ((valid * (predicted - imputes) + weight * (imputes - clicks)) * loss_weight).astype(jnp.bfloat16)
    ohgrads = (
        2.0 * weight * (imputes - clicks) * ologits * ologits * imputes * (1.0 - imputes) * loss_weight
    ).astype(jnp.bfloat16)
    return ograds, ohgrads


def gather_kernel(
    tile, item_blocks, obs_slots,
    lab_x, prop_x, uu_x, ui_x, ou_x, oi_x, oc_x, up_ref, uimp_ref, vp_ref, vi_ref,
    user_out, item_out,
    lab_land, prop_land, uu_land, ui_land, ou_land, oi_land, oc_land, s_ref, m_ref, d_ref, user_acc, item_acc,
    user_land, item_land, send_sem, recv_sem, local_sem, sum_send, sum_recv, sum_local,
):
    n = lax.axis_size("item")
    me = lax.axis_index("item")
    barrier = pltpu.get_barrier_semaphore()
    user_n = lax.axis_size("user")
    me_user = lax.axis_index("user")
    for k in range(1, n):
        pl.semaphore_signal(barrier, inc=1, device_id={"item": lax.rem(me + k, n)}, device_id_type=MESH)
    for k in range(1, user_n):
        pl.semaphore_signal(barrier, inc=1, device_id={"user": lax.rem(me_user + k, user_n)}, device_id_type=MESH)
    pl.semaphore_wait(barrier, (n - 1) + (user_n - 1))

    index_pairs = ((uu_x, uu_land), (ui_x, ui_land), (ou_x, ou_land), (oi_x, oi_land), (oc_x, oc_land))
    tile_pairs = ((lab_x, lab_land), (prop_x, prop_land))

    def send(which, src, dst, k):
        copy = pltpu.make_async_remote_copy(
            src_ref=src,
            dst_ref=dst,
            send_sem=send_sem.at[which, k - 1],
            recv_sem=recv_sem.at[which, k - 1],
            device_id={"item": lax.rem(me + k, n)},
            device_id_type=MESH,
        )
        copy.start()
        return copy

    index_copies = []
    for which, (x, land) in enumerate(index_pairs):
        local = pltpu.make_async_copy(x, land.at[me], local_sem.at[which])
        local.start()
        index_copies.append(local)
        for k in range(1, n):
            index_copies.append(send(which, x, land.at[me], k))
    tile_local = []
    tile_copies = [[] for _ in range(n)]
    for which, (x, land) in enumerate(tile_pairs):
        slot = len(index_pairs) + which
        local = pltpu.make_async_copy(x.at[me], land.at[me], local_sem.at[slot])
        local.start()
        tile_local.append(local)
        for k in range(1, n):
            tile_copies[k].append(send(slot, x.at[lax.rem(me + k, n)], land.at[me], k))

    dims = (((1,), (1,)), ((), ()))

    def block(k, carry):
        ub = k // item_blocks
        ib = k % item_blocks
        logits = lax.dot_general(up_ref[ub], vp_ref[ib], dims, preferred_element_type=jnp.float32)
        imputed = lax.dot_general(uimp_ref[ub], vi_ref[ib], dims, preferred_element_type=jnp.float32)
        s_ref[k] = logits
        m_ref[k] = imputed
        d_ref[k] = ((jax.nn.sigmoid(logits) - jax.nn.sigmoid(imputed)) * loss_weight).astype(d_ref.dtype)
        return carry

    lax.fori_loop(0, s_ref.shape[0], block, 0)
    user_acc[...] = jnp.zeros(user_acc.shape, jnp.float32)
    item_acc[...] = jnp.zeros(item_acc.shape, jnp.float32)
    forward = (((1,), (0,)), ((), ()))
    backward = (((0,), (0,)), ((), ()))
    user_blocks = user_acc.shape[1] // tile

    for copy in index_copies:
        copy.wait()
    uno_slots = uu_land.shape[1] // n
    slots = []
    for t in range(n * uno_slots):
        origin = t // uno_slots
        slot = me * uno_slots + t % uno_slots
        slots.append(uu_land[origin, slot] * item_blocks + ui_land[origin, slot])
    for k in range(s_ref.shape[0]):
        count = jnp.where(slots[0] == k, 1.0, 0.0)
        for t in range(1, len(slots)):
            count = count + jnp.where(slots[t] == k, 1.0, 0.0)
        users = pl.ds((k // item_blocks) * tile, tile)
        items = pl.ds((k % item_blocks) * tile, tile)
        grads = d_ref[k]
        user_acc[0, users, :] += count * lax.dot_general(
            grads, vp_ref[k % item_blocks], forward, preferred_element_type=jnp.float32
        )
        item_acc[0, items, :] += count * lax.dot_general(
            grads, up_ref[k // item_blocks], backward, preferred_element_type=jnp.float32
        )

    def origin_tiles(origin):
        for place in range(obs_slots):
            slot = me * obs_slots + place
            ub = ou_land[origin, slot]
            ib = oi_land[origin, slot]
            pos = ub * item_blocks + ib
            valid = jnp.where(place < oc_land[origin, me], 1.0, 0.0).astype(jnp.float32)
            labels = lab_land[origin, pl.ds(place * tile, tile), :].astype(jnp.float32)
            propens = prop_land[origin, pl.ds(place * tile, tile), :].astype(jnp.float32)
            ograds, ohgrads = observed_grads(valid, s_ref[pos], m_ref[pos], labels, propens)
            terms = []
            for g, u_ref, v_ref in ((ograds, up_ref, vp_ref), (ohgrads, uimp_ref, vi_ref)):
                terms.append(
                    (
                        lax.dot_general(g, v_ref[ib], forward, preferred_element_type=jnp.float32),
                        lax.dot_general(g, u_ref[ub], backward, preferred_element_type=jnp.float32),
                    )
                )
            for b in range(user_blocks):
                hit = jnp.where(ub == b, 1.0, 0.0)
                for model in range(2):
                    user_acc[model, pl.ds(b * tile, tile), :] += hit * terms[model][0]
            for c in range(item_blocks):
                hit = jnp.where(ib == c, 1.0, 0.0)
                for model in range(2):
                    item_acc[model, pl.ds(c * tile, tile), :] += hit * terms[model][1]

    for copy in tile_local:
        copy.wait()
    origin_tiles(me)
    for k in range(1, n):
        for copy in tile_copies[k]:
            copy.wait()
        origin_tiles(lax.rem(me + n - k, n))
    sums = []
    for which, (acc, land, axis, me_at, size) in enumerate(
        ((user_acc, user_land, "item", me, n), (item_acc, item_land, "user", me_user, user_n))
    ):
        rows = land.shape[2]
        local = pltpu.make_async_copy(acc.at[:, pl.ds(me_at * rows, rows), :], land.at[me_at], sum_local.at[which])
        local.start()
        copies = [local]
        for k in range(1, size):
            peer = lax.rem(me_at + k, size)
            copy = pltpu.make_async_remote_copy(
                src_ref=acc.at[:, pl.ds(peer * rows, rows), :],
                dst_ref=land.at[me_at],
                send_sem=sum_send.at[which, k - 1],
                recv_sem=sum_recv.at[which, k - 1],
                device_id={axis: peer},
                device_id_type=MESH,
            )
            copy.start()
            copies.append(copy)
        sums.append(copies)
    for copies in sums:
        for copy in copies:
            copy.wait()
    for land, out in ((user_land, user_out), (item_land, item_out)):
        total = land[0]
        for source in range(1, land.shape[0]):
            total = total + land[source]
        out[...] = total


def exchange_tiles(labels, propens, indices, factors, tile, item_blocks, obs_slots, user_ways):
    n = lax.axis_size("item")
    user_rows, rank = factors[0].shape
    shard_rows = factors[2].shape[0]
    factors = [x.reshape(x.shape[0] // tile, tile, rank) for x in factors]
    n_blocks = factors[0].shape[0] * item_blocks
    n_tiles = n * obs_slots
    vmem = pl.BlockSpec(memory_space=pltpu.VMEM)
    smem = pl.BlockSpec(memory_space=pltpu.SMEM)
    anyspace = pl.BlockSpec(memory_space=pl.ANY)
    return pl.pallas_call(
        functools.partial(gather_kernel, tile, item_blocks, obs_slots),
        out_shape=[
            jax.ShapeDtypeStruct((2, user_rows // n, rank), jnp.float32),
            jax.ShapeDtypeStruct((2, shard_rows // user_ways, rank), jnp.float32),
        ],
        in_specs=[anyspace] * 7 + [vmem] * 4,
        out_specs=[vmem] * 2,
        scratch_shapes=[
            pltpu.VMEM((n,) + labels.shape[1:], labels.dtype),
            pltpu.VMEM((n,) + propens.shape[1:], propens.dtype),
        ]
        + [pltpu.SMEM((n,) + x.shape, x.dtype) for x in indices]
        + [
            pltpu.VMEM((n_blocks, tile, tile), jnp.float32),
            pltpu.VMEM((n_blocks, tile, tile), jnp.float32),
            pltpu.VMEM((n_blocks, tile, tile), jnp.bfloat16),
            pltpu.VMEM((2, user_rows, rank), jnp.float32),
            pltpu.VMEM((2, shard_rows, rank), jnp.float32),
            pltpu.VMEM((n, 2, user_rows // n, rank), jnp.float32),
            pltpu.VMEM((user_ways, 2, shard_rows // user_ways, rank), jnp.float32),
            pltpu.SemaphoreType.DMA((7, n - 1)),
            pltpu.SemaphoreType.DMA((7, n - 1)),
            pltpu.SemaphoreType.DMA((7,)),
            pltpu.SemaphoreType.DMA((2, max(n, user_ways) - 1)),
            pltpu.SemaphoreType.DMA((2, max(n, user_ways) - 1)),
            pltpu.SemaphoreType.DMA((2,)),
        ],
        compiler_params=pltpu.CompilerParams(collective_id=0, has_side_effects=True),
    )(labels, propens, *indices, *factors)


def tile_kernel(
    tile, user_blocks, item_blocks,
    slot_ref, pos_ref, d_ref, gt_ref, ht_ref, up_ref, ui_ref, vp_ref, vi_ref,
    user_out, item_out,
    count_ref, g_acc, h_acc, user_acc, item_acc,
):
    n_blocks = user_blocks * item_blocks
    for k in range(n_blocks):
        count_ref[k] = 0

    def tally(t, carry):
        k = slot_ref[t]
        count_ref[k] = count_ref[k] + 1
        return carry

    lax.fori_loop(0, slot_ref.shape[0], tally, 0)
    for k in range(n_blocks):
        g_acc[k] = count_ref[k].astype(jnp.float32) * d_ref[k].astype(jnp.float32)
        h_acc[k] = jnp.zeros((tile, tile), jnp.float32)

    def observed(t, carry):
        pos = pos_ref[t]
        g_acc[pos] += gt_ref[t].astype(jnp.float32)
        h_acc[pos] += ht_ref[t].astype(jnp.float32)
        return carry

    lax.fori_loop(0, gt_ref.shape[0], observed, 0)

    user_acc[...] = jnp.zeros(user_acc.shape, jnp.float32)
    item_acc[...] = jnp.zeros(item_acc.shape, jnp.float32)
    forward = (((1,), (0,)), ((), ()))
    backward = (((0,), (0,)), ((), ()))
    for ub in range(user_blocks):
        users = pl.ds(ub * tile, tile)
        for ib in range(item_blocks):
            items = pl.ds(ib * tile, tile)
            k = ub * item_blocks + ib
            for model, acc, u_ref, v_ref in ((0, g_acc, up_ref, vp_ref), (1, h_acc, ui_ref, vi_ref)):
                wide = acc[k]
                hi = wide.astype(jnp.bfloat16)
                lo = (wide - hi.astype(jnp.float32)).astype(jnp.bfloat16)
                v = v_ref[items, :]
                u = u_ref[users, :]
                user_acc[model, users, :] += lax.dot_general(
                    hi, v, forward, preferred_element_type=jnp.float32
                ) + lax.dot_general(lo, v, forward, preferred_element_type=jnp.float32)
                item_acc[model, items, :] += lax.dot_general(
                    hi, u, backward, preferred_element_type=jnp.float32
                ) + lax.dot_general(lo, u, backward, preferred_element_type=jnp.float32)
    user_rows = user_out.shape[2]
    for dest in range(user_out.shape[0]):
        user_out[dest] = user_acc[:, pl.ds(dest * user_rows, user_rows), :]
    item_rows = item_out.shape[2]
    for dest in range(item_out.shape[0]):
        item_out[dest] = item_acc[:, pl.ds(dest * item_rows, item_rows), :]


def shards(
    user_pred,
    user_imp,
    item_pred,
    item_imp,
    uno_user,
    uno_item,
    obs_user,
    obs_item,
    obs_count,
    obs_label,
    obs_prop,
):
    item_ways = lax.axis_size("item")
    user_ways = lax.axis_size("user")
    tile = obs_label.shape[-1]
    rank = user_pred.shape[1]
    user_rows = user_pred.shape[0]
    shard_rows = item_pred.shape[0]
    user_blocks = user_rows // tile
    item_blocks = shard_rows // tile
    n_blocks = user_blocks * item_blocks
    obs_slots = obs_user.shape[-1] // item_ways

    labels = obs_label.reshape(item_ways, obs_slots * tile, tile).astype(jnp.bfloat16)
    propens = obs_prop.reshape(item_ways, obs_slots * tile, tile)
    indices = [x.reshape(x.shape[-1]) for x in (uno_user, uno_item, obs_user, obs_item, obs_count)]
    user_share, item_share = exchange_tiles(
        labels, propens, indices, (user_pred, user_imp, item_pred, item_imp), tile, item_blocks, obs_slots, user_ways
    )
    return (user_share[0], user_share[1], item_share[0], item_share[1])


def solution(mesh):
    in_specs = (
        P("user", None),
        P("user", None),
        P("item", None),
        P("item", None),
        P("user", "item", None),
        P("user", "item", None),
        P("user", "item", None),
        P("user", "item", None),
        P("user", "item", None),
        P("user", "item", None, None, None),
        P("user", "item", None, None, None),
    )
    out_specs = (
        P(("user", "item"), None),
        P(("user", "item"), None),
        P(("item", "user"), None),
        P(("item", "user"), None),
    )
    return jax.shard_map(shards, mesh=mesh, in_specs=in_specs, out_specs=out_specs, check_vma=False)
```

```python
import functools

import jax
import jax.numpy as jnp
from jax import lax
from jax.experimental import pallas as pl
from jax.experimental.pallas import tpu as pltpu
from jax.sharding import PartitionSpec as P

MESH = pl.DeviceIdType.MESH

loss_weight = 0.015625


def product(form, first, second):
    return jnp.einsum(form, first, second, preferred_element_type=jnp.float32)


def exchange_kernel(axes, whole, count, work_in, work, *refs):
    x_refs, y_refs = refs[:count], refs[count + work_in : 2 * count + work_in]
    send_sem, recv_sem, local_sem = refs[-3:]
    work_refs = refs[count : count + work_in] + refs[2 * count + work_in : -3]
    barrier = pltpu.get_barrier_semaphore()
    for axis in axes:
        n = lax.axis_size(axis)
        me = lax.axis_index(axis)
        for k in range(1, n):
            pl.semaphore_signal(barrier, inc=1, device_id={axis: lax.rem(me + k, n)}, device_id_type=MESH)
    pl.semaphore_wait(barrier, sum(lax.axis_size(axis) - 1 for axis in axes))
    copies = []
    slot = 0
    for which, axis in enumerate(axes):
        n = lax.axis_size(axis)
        me = lax.axis_index(axis)
        x_ref, y_ref = x_refs[which], y_refs[which]
        local = pltpu.make_async_copy(x_ref if whole[which] else x_ref.at[me], y_ref.at[me], local_sem.at[which])
        local.start()
        copies.append(local)
        for k in range(1, n):
            peer = lax.rem(me + k, n)
            copy = pltpu.make_async_remote_copy(
                src_ref=x_ref if whole[which] else x_ref.at[peer],
                dst_ref=y_ref.at[me],
                send_sem=send_sem.at[slot],
                recv_sem=recv_sem.at[slot],
                device_id={axis: peer},
                device_id_type=MESH,
            )
            copy.start()
            copies.append(copy)
            slot += 1
    if work is not None:
        work(*work_refs)
    for copy in copies:
        copy.wait()


def exchange(pairs, collective, work=None, work_inputs=(), work_outputs=(), whole=None):
    axes = tuple(axis for _, axis in pairs)
    arrays = [x for x, _ in pairs]
    whole = tuple(whole) if whole is not None else (False,) * len(arrays)
    shapes = [(lax.axis_size(axis),) + x.shape if w else x.shape for (x, axis), w in zip(pairs, whole)]
    slots = sum(lax.axis_size(axis) - 1 for axis in axes)
    vmem = pl.BlockSpec(memory_space=pltpu.VMEM)
    return pl.pallas_call(
        functools.partial(exchange_kernel, axes, whole, len(arrays), len(work_inputs), work),
        out_shape=[jax.ShapeDtypeStruct(shape, x.dtype) for shape, x in zip(shapes, arrays)] + list(work_outputs),
        in_specs=[pl.BlockSpec(memory_space=pl.ANY)] * len(arrays) + [vmem] * len(work_inputs),
        out_specs=[pl.BlockSpec(memory_space=pl.ANY)] * len(arrays) + [vmem] * len(work_outputs),
        scratch_shapes=[
            pltpu.SemaphoreType.DMA((slots,)),
            pltpu.SemaphoreType.DMA((slots,)),
            pltpu.SemaphoreType.DMA((len(arrays),)),
        ],
        compiler_params=pltpu.CompilerParams(collective_id=collective, has_side_effects=True),
    )(*arrays, *work_inputs)


def reduce_kernel(axes, *refs):
    count = len(axes)
    x_refs, out_refs = refs[:count], refs[count : 2 * count]
    land_refs = refs[2 * count : 3 * count]
    send_sem, recv_sem, local_sem = refs[3 * count :]
    barrier = pltpu.get_barrier_semaphore()
    for axis in axes:
        n = lax.axis_size(axis)
        me = lax.axis_index(axis)
        for k in range(1, n):
            pl.semaphore_signal(barrier, inc=1, device_id={axis: lax.rem(me + k, n)}, device_id_type=MESH)
    pl.semaphore_wait(barrier, sum(lax.axis_size(axis) - 1 for axis in axes))
    copies = []
    slot = 0
    for which, axis in enumerate(axes):
        n = lax.axis_size(axis)
        me = lax.axis_index(axis)
        x_ref, land = x_refs[which], land_refs[which]
        local = pltpu.make_async_copy(x_ref.at[me], land.at[me], local_sem.at[which])
        local.start()
        copies.append(local)
        for k in range(1, n):
            peer = lax.rem(me + k, n)
            copy = pltpu.make_async_remote_copy(
                src_ref=x_ref.at[peer],
                dst_ref=land.at[me],
                send_sem=send_sem.at[slot],
                recv_sem=recv_sem.at[slot],
                device_id={axis: peer},
                device_id_type=MESH,
            )
            copy.start()
            copies.append(copy)
            slot += 1
    for copy in copies:
        copy.wait()
    for which in range(count):
        land = land_refs[which]
        total = land[0]
        for source in range(1, land.shape[0]):
            total = total + land[source]
        out_refs[which][...] = total


def reduce_exchange(pairs, collective):
    axes = tuple(axis for _, axis in pairs)
    arrays = [x for x, _ in pairs]
    slots = sum(lax.axis_size(axis) - 1 for axis in axes)
    return pl.pallas_call(
        functools.partial(reduce_kernel, axes),
        out_shape=[jax.ShapeDtypeStruct(x.shape[1:], x.dtype) for x in arrays],
        in_specs=[pl.BlockSpec(memory_space=pl.ANY)] * len(arrays),
        out_specs=[pl.BlockSpec(memory_space=pltpu.VMEM)] * len(arrays),
        scratch_shapes=[pltpu.VMEM(x.shape, x.dtype) for x in arrays]
        + [
            pltpu.SemaphoreType.DMA((slots,)),
            pltpu.SemaphoreType.DMA((slots,)),
            pltpu.SemaphoreType.DMA((len(arrays),)),
        ],
        compiler_params=pltpu.CompilerParams(collective_id=collective, has_side_effects=True),
    )(*arrays)


def observed_grads(valid, ologits, imputed, labels, propens):
    predicted = jax.nn.sigmoid(ologits)
    imputes = jax.nn.sigmoid(imputed)
    seen = (labels > 0).astype(jnp.float32)
    clicks = (labels == 2).astype(jnp.float32)
    weight = valid * seen / propens
    ograds = ((valid * (predicted - imputes) + weight * (imputes - clicks)) * loss_weight).astype(jnp.bfloat16)
    ohgrads = (
        2.0 * weight * (imputes - clicks) * ologits * ologits * imputes * (1.0 - imputes) * loss_weight
    ).astype(jnp.bfloat16)
    return ograds, ohgrads


def gather_kernel(
    tile, item_blocks, obs_slots,
    lab_x, prop_x, uu_x, ui_x, ou_x, oi_x, oc_x, up_ref, uimp_ref, vp_ref, vi_ref,
    user_out, item_out,
    lab_land, prop_land, uu_land, ui_land, ou_land, oi_land, oc_land, s_ref, m_ref, d_ref, user_acc, item_acc,
    user_land, item_land, lab_wide, lab_narrow, send_sem, recv_sem, local_sem, sum_send, sum_recv, sum_local,
):
    n = lax.axis_size("item")
    me = lax.axis_index("item")
    barrier = pltpu.get_barrier_semaphore()
    user_n = lax.axis_size("user")
    me_user = lax.axis_index("user")
    for k in range(1, n):
        pl.semaphore_signal(barrier, inc=1, device_id={"item": lax.rem(me + k, n)}, device_id_type=MESH)
    for k in range(1, user_n):
        pl.semaphore_signal(barrier, inc=1, device_id={"user": lax.rem(me_user + k, user_n)}, device_id_type=MESH)
    pl.semaphore_wait(barrier, (n - 1) + (user_n - 1))

    index_pairs = ((uu_x, uu_land), (ui_x, ui_land), (ou_x, ou_land), (oi_x, oi_land), (oc_x, oc_land))
    tile_pairs = ((lab_x, lab_land), (prop_x, prop_land))

    def send(which, src, dst, k):
        copy = pltpu.make_async_remote_copy(
            src_ref=src,
            dst_ref=dst,
            send_sem=send_sem.at[which, k - 1],
            recv_sem=recv_sem.at[which, k - 1],
            device_id={"item": lax.rem(me + k, n)},
            device_id_type=MESH,
        )
        copy.start()
        return copy

    index_copies = []
    for which, (x, land) in enumerate(index_pairs):
        local = pltpu.make_async_copy(x, land.at[me], local_sem.at[which])
        local.start()
        index_copies.append(local)
        for k in range(1, n):
            index_copies.append(send(which, x, land.at[me], k))
    tile_local = []
    tile_copies = [[] for _ in range(n)]
    staging = pltpu.make_async_copy(lab_x, lab_wide, local_sem.at[len(index_pairs) + len(tile_pairs)])
    staging.start()

    def send_tiles(which, x, land):
        slot = len(index_pairs) + which
        local = pltpu.make_async_copy(x.at[me], land.at[me], local_sem.at[slot])
        local.start()
        tile_local.append(local)
        for k in range(1, n):
            tile_copies[k].append(send(slot, x.at[lax.rem(me + k, n)], land.at[me], k))

    send_tiles(1, prop_x, prop_land)
    staging.wait()
    for row in range(lab_wide.shape[0]):
        lab_narrow[row] = lab_wide[row].astype(lab_narrow.dtype)
    send_tiles(0, lab_narrow, lab_land)

    dims = (((1,), (1,)), ((), ()))

    def block(k, carry):
        ub = k // item_blocks
        ib = k % item_blocks
        logits = lax.dot_general(up_ref[ub], vp_ref[ib], dims, preferred_element_type=jnp.float32)
        imputed = lax.dot_general(uimp_ref[ub], vi_ref[ib], dims, preferred_element_type=jnp.float32)
        s_ref[k] = logits
        m_ref[k] = imputed
        d_ref[k] = ((jax.nn.sigmoid(logits) - jax.nn.sigmoid(imputed)) * loss_weight).astype(d_ref.dtype)
        return carry

    lax.fori_loop(0, s_ref.shape[0], block, 0)
    user_acc[...] = jnp.zeros(user_acc.shape, jnp.float32)
    item_acc[...] = jnp.zeros(item_acc.shape, jnp.float32)
    forward = (((1,), (0,)), ((), ()))
    backward = (((0,), (0,)), ((), ()))
    user_blocks = user_acc.shape[1] // tile

    for copy in index_copies:
        copy.wait()
    uno_slots = uu_land.shape[1] // n
    slots = []
    for t in range(n * uno_slots):
        origin = t // uno_slots
        slot = me * uno_slots + t % uno_slots
        slots.append(uu_land[origin, slot] * item_blocks + ui_land[origin, slot])
    for k in range(s_ref.shape[0]):
        count = jnp.where(slots[0] == k, 1.0, 0.0)
        for t in range(1, len(slots)):
            count = count + jnp.where(slots[t] == k, 1.0, 0.0)
        users = pl.ds((k // item_blocks) * tile, tile)
        items = pl.ds((k % item_blocks) * tile, tile)
        grads = d_ref[k]
        user_acc[0, users, :] += count * lax.dot_general(
            grads, vp_ref[k % item_blocks], forward, preferred_element_type=jnp.float32
        )
        item_acc[0, items, :] += count * lax.dot_general(
            grads, up_ref[k // item_blocks], backward, preferred_element_type=jnp.float32
        )

    def origin_tiles(origin):
        for place in range(obs_slots):
            slot = me * obs_slots + place
            ub = ou_land[origin, slot]
            ib = oi_land[origin, slot]
            pos = ub * item_blocks + ib
            valid = jnp.where(place < oc_land[origin, me], 1.0, 0.0).astype(jnp.float32)
            labels = lab_land[origin, pl.ds(place * tile, tile), :].astype(jnp.float32)
            propens = prop_land[origin, pl.ds(place * tile, tile), :].astype(jnp.float32)
            ograds, ohgrads = observed_grads(valid, s_ref[pos], m_ref[pos], labels, propens)
            terms = []
            for g, u_ref, v_ref in ((ograds, up_ref, vp_ref), (ohgrads, uimp_ref, vi_ref)):
                terms.append(
                    (
                        lax.dot_general(g, v_ref[ib], forward, preferred_element_type=jnp.float32),
                        lax.dot_general(g, u_ref[ub], backward, preferred_element_type=jnp.float32),
                    )
                )
            for b in range(user_blocks):
                hit = jnp.where(ub == b, 1.0, 0.0)
                for model in range(2):
                    user_acc[model, pl.ds(b * tile, tile), :] += hit * terms[model][0]
            for c in range(item_blocks):
                hit = jnp.where(ib == c, 1.0, 0.0)
                for model in range(2):
                    item_acc[model, pl.ds(c * tile, tile), :] += hit * terms[model][1]

    for copy in tile_local:
        copy.wait()
    origin_tiles(me)
    for k in range(1, n):
        for copy in tile_copies[k]:
            copy.wait()
        origin_tiles(lax.rem(me + n - k, n))
    sums = []
    for which, (acc, land, axis, me_at, size) in enumerate(
        ((user_acc, user_land, "item", me, n), (item_acc, item_land, "user", me_user, user_n))
    ):
        rows = land.shape[2]
        local = pltpu.make_async_copy(acc.at[:, pl.ds(me_at * rows, rows), :], land.at[me_at], sum_local.at[which])
        local.start()
        copies = [local]
        for k in range(1, size):
            peer = lax.rem(me_at + k, size)
            copy = pltpu.make_async_remote_copy(
                src_ref=acc.at[:, pl.ds(peer * rows, rows), :],
                dst_ref=land.at[me_at],
                send_sem=sum_send.at[which, k - 1],
                recv_sem=sum_recv.at[which, k - 1],
                device_id={axis: peer},
                device_id_type=MESH,
            )
            copy.start()
            copies.append(copy)
        sums.append(copies)
    for copies in sums:
        for copy in copies:
            copy.wait()
    for land, out in ((user_land, user_out), (item_land, item_out)):
        total = land[0]
        for source in range(1, land.shape[0]):
            total = total + land[source]
        out[...] = total


def exchange_tiles(labels, propens, indices, factors, tile, item_blocks, obs_slots, user_ways):
    n = lax.axis_size("item")
    user_rows, rank = factors[0].shape
    shard_rows = factors[2].shape[0]
    factors = [x.reshape(x.shape[0] // tile, tile, rank) for x in factors]
    n_blocks = factors[0].shape[0] * item_blocks
    n_tiles = n * obs_slots
    vmem = pl.BlockSpec(memory_space=pltpu.VMEM)
    smem = pl.BlockSpec(memory_space=pltpu.SMEM)
    anyspace = pl.BlockSpec(memory_space=pl.ANY)
    return pl.pallas_call(
        functools.partial(gather_kernel, tile, item_blocks, obs_slots),
        out_shape=[
            jax.ShapeDtypeStruct((2, user_rows // n, rank), jnp.float32),
            jax.ShapeDtypeStruct((2, shard_rows // user_ways, rank), jnp.float32),
        ],
        in_specs=[anyspace] * 7 + [vmem] * 4,
        out_specs=[vmem] * 2,
        scratch_shapes=[
            pltpu.VMEM((n,) + labels.shape[1:], jnp.bfloat16),
            pltpu.VMEM((n,) + propens.shape[1:], propens.dtype),
        ]
        + [pltpu.SMEM((n,) + x.shape, x.dtype) for x in indices]
        + [
            pltpu.VMEM((n_blocks, tile, tile), jnp.float32),
            pltpu.VMEM((n_blocks, tile, tile), jnp.float32),
            pltpu.VMEM((n_blocks, tile, tile), jnp.bfloat16),
            pltpu.VMEM((2, user_rows, rank), jnp.float32),
            pltpu.VMEM((2, shard_rows, rank), jnp.float32),
            pltpu.VMEM((n, 2, user_rows // n, rank), jnp.float32),
            pltpu.VMEM((user_ways, 2, shard_rows // user_ways, rank), jnp.float32),
            pltpu.VMEM(labels.shape, labels.dtype),
            pltpu.VMEM(labels.shape, jnp.bfloat16),
            pltpu.SemaphoreType.DMA((7, n - 1)),
            pltpu.SemaphoreType.DMA((7, n - 1)),
            pltpu.SemaphoreType.DMA((8,)),
            pltpu.SemaphoreType.DMA((2, max(n, user_ways) - 1)),
            pltpu.SemaphoreType.DMA((2, max(n, user_ways) - 1)),
            pltpu.SemaphoreType.DMA((2,)),
        ],
        compiler_params=pltpu.CompilerParams(collective_id=0, has_side_effects=True),
    )(labels, propens, *indices, *factors)


def tile_kernel(
    tile, user_blocks, item_blocks,
    slot_ref, pos_ref, d_ref, gt_ref, ht_ref, up_ref, ui_ref, vp_ref, vi_ref,
    user_out, item_out,
    count_ref, g_acc, h_acc, user_acc, item_acc,
):
    n_blocks = user_blocks * item_blocks
    for k in range(n_blocks):
        count_ref[k] = 0

    def tally(t, carry):
        k = slot_ref[t]
        count_ref[k] = count_ref[k] + 1
        return carry

    lax.fori_loop(0, slot_ref.shape[0], tally, 0)
    for k in range(n_blocks):
        g_acc[k] = count_ref[k].astype(jnp.float32) * d_ref[k].astype(jnp.float32)
        h_acc[k] = jnp.zeros((tile, tile), jnp.float32)

    def observed(t, carry):
        pos = pos_ref[t]
        g_acc[pos] += gt_ref[t].astype(jnp.float32)
        h_acc[pos] += ht_ref[t].astype(jnp.float32)
        return carry

    lax.fori_loop(0, gt_ref.shape[0], observed, 0)

    user_acc[...] = jnp.zeros(user_acc.shape, jnp.float32)
    item_acc[...] = jnp.zeros(item_acc.shape, jnp.float32)
    forward = (((1,), (0,)), ((), ()))
    backward = (((0,), (0,)), ((), ()))
    for ub in range(user_blocks):
        users = pl.ds(ub * tile, tile)
        for ib in range(item_blocks):
            items = pl.ds(ib * tile, tile)
            k = ub * item_blocks + ib
            for model, acc, u_ref, v_ref in ((0, g_acc, up_ref, vp_ref), (1, h_acc, ui_ref, vi_ref)):
                wide = acc[k]
                hi = wide.astype(jnp.bfloat16)
                lo = (wide - hi.astype(jnp.float32)).astype(jnp.bfloat16)
                v = v_ref[items, :]
                u = u_ref[users, :]
                user_acc[model, users, :] += lax.dot_general(
                    hi, v, forward, preferred_element_type=jnp.float32
                ) + lax.dot_general(lo, v, forward, preferred_element_type=jnp.float32)
                item_acc[model, items, :] += lax.dot_general(
                    hi, u, backward, preferred_element_type=jnp.float32
                ) + lax.dot_general(lo, u, backward, preferred_element_type=jnp.float32)
    user_rows = user_out.shape[2]
    for dest in range(user_out.shape[0]):
        user_out[dest] = user_acc[:, pl.ds(dest * user_rows, user_rows), :]
    item_rows = item_out.shape[2]
    for dest in range(item_out.shape[0]):
        item_out[dest] = item_acc[:, pl.ds(dest * item_rows, item_rows), :]


def shards(
    user_pred,
    user_imp,
    item_pred,
    item_imp,
    uno_user,
    uno_item,
    obs_user,
    obs_item,
    obs_count,
    obs_label,
    obs_prop,
):
    item_ways = lax.axis_size("item")
    user_ways = lax.axis_size("user")
    tile = obs_label.shape[-1]
    rank = user_pred.shape[1]
    user_rows = user_pred.shape[0]
    shard_rows = item_pred.shape[0]
    user_blocks = user_rows // tile
    item_blocks = shard_rows // tile
    n_blocks = user_blocks * item_blocks
    obs_slots = obs_user.shape[-1] // item_ways

    labels = obs_label.reshape(item_ways, obs_slots * tile, tile)
    propens = obs_prop.reshape(item_ways, obs_slots * tile, tile)
    indices = [x.reshape(x.shape[-1]) for x in (uno_user, uno_item, obs_user, obs_item, obs_count)]
    user_share, item_share = exchange_tiles(
        labels, propens, indices, (user_pred, user_imp, item_pred, item_imp), tile, item_blocks, obs_slots, user_ways
    )
    return (user_share[0], user_share[1], item_share[0], item_share[1])


def solution(mesh):
    in_specs = (
        P("user", None),
        P("user", None),
        P("item", None),
        P("item", None),
        P("user", "item", None),
        P("user", "item", None),
        P("user", "item", None),
        P("user", "item", None),
        P("user", "item", None),
        P("user", "item", None, None, None),
        P("user", "item", None, None, None),
    )
    out_specs = (
        P(("user", "item"), None),
        P(("user", "item"), None),
        P(("item", "user"), None),
        P(("item", "user"), None),
    )
    return jax.shard_map(shards, mesh=mesh, in_specs=in_specs, out_specs=out_specs, check_vma=False)
```

```python
import functools

import jax
import jax.numpy as jnp
from jax import lax
from jax.experimental import pallas as pl
from jax.experimental.pallas import tpu as pltpu
from jax.sharding import PartitionSpec as P

MESH = pl.DeviceIdType.MESH

loss_weight = 0.015625


def product(form, first, second):
    return jnp.einsum(form, first, second, preferred_element_type=jnp.float32)


def exchange_kernel(axes, whole, count, work_in, work, *refs):
    x_refs, y_refs = refs[:count], refs[count + work_in : 2 * count + work_in]
    send_sem, recv_sem, local_sem = refs[-3:]
    work_refs = refs[count : count + work_in] + refs[2 * count + work_in : -3]
    barrier = pltpu.get_barrier_semaphore()
    for axis in axes:
        n = lax.axis_size(axis)
        me = lax.axis_index(axis)
        for k in range(1, n):
            pl.semaphore_signal(barrier, inc=1, device_id={axis: lax.rem(me + k, n)}, device_id_type=MESH)
    pl.semaphore_wait(barrier, sum(lax.axis_size(axis) - 1 for axis in axes))
    copies = []
    slot = 0
    for which, axis in enumerate(axes):
        n = lax.axis_size(axis)
        me = lax.axis_index(axis)
        x_ref, y_ref = x_refs[which], y_refs[which]
        local = pltpu.make_async_copy(x_ref if whole[which] else x_ref.at[me], y_ref.at[me], local_sem.at[which])
        local.start()
        copies.append(local)
        for k in range(1, n):
            peer = lax.rem(me + k, n)
            copy = pltpu.make_async_remote_copy(
                src_ref=x_ref if whole[which] else x_ref.at[peer],
                dst_ref=y_ref.at[me],
                send_sem=send_sem.at[slot],
                recv_sem=recv_sem.at[slot],
                device_id={axis: peer},
                device_id_type=MESH,
            )
            copy.start()
            copies.append(copy)
            slot += 1
    if work is not None:
        work(*work_refs)
    for copy in copies:
        copy.wait()


def exchange(pairs, collective, work=None, work_inputs=(), work_outputs=(), whole=None):
    axes = tuple(axis for _, axis in pairs)
    arrays = [x for x, _ in pairs]
    whole = tuple(whole) if whole is not None else (False,) * len(arrays)
    shapes = [(lax.axis_size(axis),) + x.shape if w else x.shape for (x, axis), w in zip(pairs, whole)]
    slots = sum(lax.axis_size(axis) - 1 for axis in axes)
    vmem = pl.BlockSpec(memory_space=pltpu.VMEM)
    return pl.pallas_call(
        functools.partial(exchange_kernel, axes, whole, len(arrays), len(work_inputs), work),
        out_shape=[jax.ShapeDtypeStruct(shape, x.dtype) for shape, x in zip(shapes, arrays)] + list(work_outputs),
        in_specs=[pl.BlockSpec(memory_space=pl.ANY)] * len(arrays) + [vmem] * len(work_inputs),
        out_specs=[pl.BlockSpec(memory_space=pl.ANY)] * len(arrays) + [vmem] * len(work_outputs),
        scratch_shapes=[
            pltpu.SemaphoreType.DMA((slots,)),
            pltpu.SemaphoreType.DMA((slots,)),
            pltpu.SemaphoreType.DMA((len(arrays),)),
        ],
        compiler_params=pltpu.CompilerParams(collective_id=collective, has_side_effects=True),
    )(*arrays, *work_inputs)


def reduce_kernel(axes, *refs):
    count = len(axes)
    x_refs, out_refs = refs[:count], refs[count : 2 * count]
    land_refs = refs[2 * count : 3 * count]
    send_sem, recv_sem, local_sem = refs[3 * count :]
    barrier = pltpu.get_barrier_semaphore()
    for axis in axes:
        n = lax.axis_size(axis)
        me = lax.axis_index(axis)
        for k in range(1, n):
            pl.semaphore_signal(barrier, inc=1, device_id={axis: lax.rem(me + k, n)}, device_id_type=MESH)
    pl.semaphore_wait(barrier, sum(lax.axis_size(axis) - 1 for axis in axes))
    copies = []
    slot = 0
    for which, axis in enumerate(axes):
        n = lax.axis_size(axis)
        me = lax.axis_index(axis)
        x_ref, land = x_refs[which], land_refs[which]
        local = pltpu.make_async_copy(x_ref.at[me], land.at[me], local_sem.at[which])
        local.start()
        copies.append(local)
        for k in range(1, n):
            peer = lax.rem(me + k, n)
            copy = pltpu.make_async_remote_copy(
                src_ref=x_ref.at[peer],
                dst_ref=land.at[me],
                send_sem=send_sem.at[slot],
                recv_sem=recv_sem.at[slot],
                device_id={axis: peer},
                device_id_type=MESH,
            )
            copy.start()
            copies.append(copy)
            slot += 1
    for copy in copies:
        copy.wait()
    for which in range(count):
        land = land_refs[which]
        total = land[0]
        for source in range(1, land.shape[0]):
            total = total + land[source]
        out_refs[which][...] = total


def reduce_exchange(pairs, collective):
    axes = tuple(axis for _, axis in pairs)
    arrays = [x for x, _ in pairs]
    slots = sum(lax.axis_size(axis) - 1 for axis in axes)
    return pl.pallas_call(
        functools.partial(reduce_kernel, axes),
        out_shape=[jax.ShapeDtypeStruct(x.shape[1:], x.dtype) for x in arrays],
        in_specs=[pl.BlockSpec(memory_space=pl.ANY)] * len(arrays),
        out_specs=[pl.BlockSpec(memory_space=pltpu.VMEM)] * len(arrays),
        scratch_shapes=[pltpu.VMEM(x.shape, x.dtype) for x in arrays]
        + [
            pltpu.SemaphoreType.DMA((slots,)),
            pltpu.SemaphoreType.DMA((slots,)),
            pltpu.SemaphoreType.DMA((len(arrays),)),
        ],
        compiler_params=pltpu.CompilerParams(collective_id=collective, has_side_effects=True),
    )(*arrays)


def observed_grads(valid, ologits, imputed, labels, propens):
    predicted = jax.nn.sigmoid(ologits)
    imputes = jax.nn.sigmoid(imputed)
    seen = (labels > 0).astype(jnp.float32)
    clicks = (labels == 2).astype(jnp.float32)
    weight = valid * seen / propens
    ograds = ((valid * (predicted - imputes) + weight * (imputes - clicks)) * loss_weight).astype(jnp.bfloat16)
    ohgrads = (
        2.0 * weight * (imputes - clicks) * ologits * ologits * imputes * (1.0 - imputes) * loss_weight
    ).astype(jnp.bfloat16)
    return ograds, ohgrads


def gather_kernel(
    tile, item_blocks, obs_slots,
    lab_x, prop_x, uu_x, ui_x, ou_x, oi_x, oc_x, up_ref, uimp_ref, vp_ref, vi_ref,
    shares,
    lab_land, prop_land, uu_land, ui_land, ou_land, oi_land, oc_land, s_ref, m_ref, d_ref, user_acc, item_acc,
    user_land, item_land, lab_wide, lab_narrow, send_sem, recv_sem, local_sem, sum_send, sum_recv, sum_local,
):
    n = lax.axis_size("item")
    me = lax.axis_index("item")
    barrier = pltpu.get_barrier_semaphore()
    user_n = lax.axis_size("user")
    me_user = lax.axis_index("user")
    for k in range(1, n):
        pl.semaphore_signal(barrier, inc=1, device_id={"item": lax.rem(me + k, n)}, device_id_type=MESH)
    for k in range(1, user_n):
        pl.semaphore_signal(barrier, inc=1, device_id={"user": lax.rem(me_user + k, user_n)}, device_id_type=MESH)
    pl.semaphore_wait(barrier, (n - 1) + (user_n - 1))

    index_pairs = ((uu_x, uu_land), (ui_x, ui_land), (ou_x, ou_land), (oi_x, oi_land), (oc_x, oc_land))
    tile_pairs = ((lab_x, lab_land), (prop_x, prop_land))

    def send(which, src, dst, k):
        copy = pltpu.make_async_remote_copy(
            src_ref=src,
            dst_ref=dst,
            send_sem=send_sem.at[which, k - 1],
            recv_sem=recv_sem.at[which, k - 1],
            device_id={"item": lax.rem(me + k, n)},
            device_id_type=MESH,
        )
        copy.start()
        return copy

    index_copies = []
    for which, (x, land) in enumerate(index_pairs):
        local = pltpu.make_async_copy(x, land.at[me], local_sem.at[which])
        local.start()
        index_copies.append(local)
        for k in range(1, n):
            index_copies.append(send(which, x, land.at[me], k))
    tile_local = []
    tile_copies = [[] for _ in range(n)]
    staging = pltpu.make_async_copy(lab_x, lab_wide, local_sem.at[len(index_pairs) + len(tile_pairs)])
    staging.start()

    def send_tiles(which, x, land):
        slot = len(index_pairs) + which
        local = pltpu.make_async_copy(x.at[me], land.at[me], local_sem.at[slot])
        local.start()
        tile_local.append(local)
        for k in range(1, n):
            tile_copies[k].append(send(slot, x.at[lax.rem(me + k, n)], land.at[me], k))

    send_tiles(1, prop_x, prop_land)
    staging.wait()
    for row in range(lab_wide.shape[0]):
        lab_narrow[row] = lab_wide[row].astype(lab_narrow.dtype)
    send_tiles(0, lab_narrow, lab_land)

    dims = (((1,), (1,)), ((), ()))

    def block(k, carry):
        ub = k // item_blocks
        ib = k % item_blocks
        logits = lax.dot_general(up_ref[ub], vp_ref[ib], dims, preferred_element_type=jnp.float32)
        imputed = lax.dot_general(uimp_ref[ub], vi_ref[ib], dims, preferred_element_type=jnp.float32)
        s_ref[k] = logits
        m_ref[k] = imputed
        d_ref[k] = ((jax.nn.sigmoid(logits) - jax.nn.sigmoid(imputed)) * loss_weight).astype(d_ref.dtype)
        return carry

    lax.fori_loop(0, s_ref.shape[0], block, 0)
    user_acc[...] = jnp.zeros(user_acc.shape, jnp.float32)
    item_acc[...] = jnp.zeros(item_acc.shape, jnp.float32)
    forward = (((1,), (0,)), ((), ()))
    backward = (((0,), (0,)), ((), ()))
    user_blocks = user_acc.shape[1] // tile

    for copy in index_copies:
        copy.wait()
    uno_slots = uu_land.shape[1] // n
    slots = []
    for t in range(n * uno_slots):
        origin = t // uno_slots
        slot = me * uno_slots + t % uno_slots
        slots.append(uu_land[origin, slot] * item_blocks + ui_land[origin, slot])
    for k in range(s_ref.shape[0]):
        count = jnp.where(slots[0] == k, 1.0, 0.0)
        for t in range(1, len(slots)):
            count = count + jnp.where(slots[t] == k, 1.0, 0.0)
        users = pl.ds((k // item_blocks) * tile, tile)
        items = pl.ds((k % item_blocks) * tile, tile)
        grads = d_ref[k]
        user_acc[0, users, :] += count * lax.dot_general(
            grads, vp_ref[k % item_blocks], forward, preferred_element_type=jnp.float32
        )
        item_acc[0, items, :] += count * lax.dot_general(
            grads, up_ref[k // item_blocks], backward, preferred_element_type=jnp.float32
        )

    def origin_tiles(origin):
        for place in range(obs_slots):
            slot = me * obs_slots + place
            ub = ou_land[origin, slot]
            ib = oi_land[origin, slot]
            pos = ub * item_blocks + ib
            valid = jnp.where(place < oc_land[origin, me], 1.0, 0.0).astype(jnp.float32)
            labels = lab_land[origin, pl.ds(place * tile, tile), :].astype(jnp.float32)
            propens = prop_land[origin, pl.ds(place * tile, tile), :].astype(jnp.float32)
            ograds, ohgrads = observed_grads(valid, s_ref[pos], m_ref[pos], labels, propens)
            terms = []
            for g, u_ref, v_ref in ((ograds, up_ref, vp_ref), (ohgrads, uimp_ref, vi_ref)):
                terms.append(
                    (
                        lax.dot_general(g, v_ref[ib], forward, preferred_element_type=jnp.float32),
                        lax.dot_general(g, u_ref[ub], backward, preferred_element_type=jnp.float32),
                    )
                )
            for b in range(user_blocks):
                hit = jnp.where(ub == b, 1.0, 0.0)
                for model in range(2):
                    user_acc[model, pl.ds(b * tile, tile), :] += hit * terms[model][0]
            for c in range(item_blocks):
                hit = jnp.where(ib == c, 1.0, 0.0)
                for model in range(2):
                    item_acc[model, pl.ds(c * tile, tile), :] += hit * terms[model][1]

    for copy in tile_local:
        copy.wait()
    origin_tiles(me)
    for k in range(1, n):
        for copy in tile_copies[k]:
            copy.wait()
        origin_tiles(lax.rem(me + n - k, n))
    sums = []
    for which, (acc, land, axis, me_at, size) in enumerate(
        ((user_acc, user_land, "item", me, n), (item_acc, item_land, "user", me_user, user_n))
    ):
        rows = land.shape[2]
        local = pltpu.make_async_copy(acc.at[:, pl.ds(me_at * rows, rows), :], land.at[me_at], sum_local.at[which])
        local.start()
        copies = [local]
        for k in range(1, size):
            peer = lax.rem(me_at + k, size)
            copy = pltpu.make_async_remote_copy(
                src_ref=acc.at[:, pl.ds(peer * rows, rows), :],
                dst_ref=land.at[me_at],
                send_sem=sum_send.at[which, k - 1],
                recv_sem=sum_recv.at[which, k - 1],
                device_id={axis: peer},
                device_id_type=MESH,
            )
            copy.start()
            copies.append(copy)
        sums.append(copies)
    for copies in sums:
        for copy in copies:
            copy.wait()
    rows = 0
    for land in (user_land, item_land):
        total = land[0]
        for source in range(1, land.shape[0]):
            total = total + land[source]
        shares[:, pl.ds(rows, land.shape[2]), :] = total
        rows += land.shape[2]


def exchange_tiles(labels, propens, indices, factors, tile, item_blocks, obs_slots, user_ways):
    n = lax.axis_size("item")
    user_rows, rank = factors[0].shape
    shard_rows = factors[2].shape[0]
    factors = [x.reshape(x.shape[0] // tile, tile, rank) for x in factors]
    n_blocks = factors[0].shape[0] * item_blocks
    n_tiles = n * obs_slots
    vmem = pl.BlockSpec(memory_space=pltpu.VMEM)
    smem = pl.BlockSpec(memory_space=pltpu.SMEM)
    anyspace = pl.BlockSpec(memory_space=pl.ANY)
    return pl.pallas_call(
        functools.partial(gather_kernel, tile, item_blocks, obs_slots),
        out_shape=jax.ShapeDtypeStruct((2, user_rows // n + shard_rows // user_ways, rank), jnp.float32),
        in_specs=[anyspace] * 7 + [vmem] * 4,
        out_specs=vmem,
        scratch_shapes=[
            pltpu.VMEM((n,) + labels.shape[1:], jnp.bfloat16),
            pltpu.VMEM((n,) + propens.shape[1:], propens.dtype),
        ]
        + [pltpu.SMEM((n,) + x.shape, x.dtype) for x in indices]
        + [
            pltpu.VMEM((n_blocks, tile, tile), jnp.float32),
            pltpu.VMEM((n_blocks, tile, tile), jnp.float32),
            pltpu.VMEM((n_blocks, tile, tile), jnp.bfloat16),
            pltpu.VMEM((2, user_rows, rank), jnp.float32),
            pltpu.VMEM((2, shard_rows, rank), jnp.float32),
            pltpu.VMEM((n, 2, user_rows // n, rank), jnp.float32),
            pltpu.VMEM((user_ways, 2, shard_rows // user_ways, rank), jnp.float32),
            pltpu.VMEM(labels.shape, labels.dtype),
            pltpu.VMEM(labels.shape, jnp.bfloat16),
            pltpu.SemaphoreType.DMA((7, n - 1)),
            pltpu.SemaphoreType.DMA((7, n - 1)),
            pltpu.SemaphoreType.DMA((8,)),
            pltpu.SemaphoreType.DMA((2, max(n, user_ways) - 1)),
            pltpu.SemaphoreType.DMA((2, max(n, user_ways) - 1)),
            pltpu.SemaphoreType.DMA((2,)),
        ],
        compiler_params=pltpu.CompilerParams(collective_id=0, has_side_effects=True),
    )(labels, propens, *indices, *factors)


def tile_kernel(
    tile, user_blocks, item_blocks,
    slot_ref, pos_ref, d_ref, gt_ref, ht_ref, up_ref, ui_ref, vp_ref, vi_ref,
    user_out, item_out,
    count_ref, g_acc, h_acc, user_acc, item_acc,
):
    n_blocks = user_blocks * item_blocks
    for k in range(n_blocks):
        count_ref[k] = 0

    def tally(t, carry):
        k = slot_ref[t]
        count_ref[k] = count_ref[k] + 1
        return carry

    lax.fori_loop(0, slot_ref.shape[0], tally, 0)
    for k in range(n_blocks):
        g_acc[k] = count_ref[k].astype(jnp.float32) * d_ref[k].astype(jnp.float32)
        h_acc[k] = jnp.zeros((tile, tile), jnp.float32)

    def observed(t, carry):
        pos = pos_ref[t]
        g_acc[pos] += gt_ref[t].astype(jnp.float32)
        h_acc[pos] += ht_ref[t].astype(jnp.float32)
        return carry

    lax.fori_loop(0, gt_ref.shape[0], observed, 0)

    user_acc[...] = jnp.zeros(user_acc.shape, jnp.float32)
    item_acc[...] = jnp.zeros(item_acc.shape, jnp.float32)
    forward = (((1,), (0,)), ((), ()))
    backward = (((0,), (0,)), ((), ()))
    for ub in range(user_blocks):
        users = pl.ds(ub * tile, tile)
        for ib in range(item_blocks):
            items = pl.ds(ib * tile, tile)
            k = ub * item_blocks + ib
            for model, acc, u_ref, v_ref in ((0, g_acc, up_ref, vp_ref), (1, h_acc, ui_ref, vi_ref)):
                wide = acc[k]
                hi = wide.astype(jnp.bfloat16)
                lo = (wide - hi.astype(jnp.float32)).astype(jnp.bfloat16)
                v = v_ref[items, :]
                u = u_ref[users, :]
                user_acc[model, users, :] += lax.dot_general(
                    hi, v, forward, preferred_element_type=jnp.float32
                ) + lax.dot_general(lo, v, forward, preferred_element_type=jnp.float32)
                item_acc[model, items, :] += lax.dot_general(
                    hi, u, backward, preferred_element_type=jnp.float32
                ) + lax.dot_general(lo, u, backward, preferred_element_type=jnp.float32)
    user_rows = user_out.shape[2]
    for dest in range(user_out.shape[0]):
        user_out[dest] = user_acc[:, pl.ds(dest * user_rows, user_rows), :]
    item_rows = item_out.shape[2]
    for dest in range(item_out.shape[0]):
        item_out[dest] = item_acc[:, pl.ds(dest * item_rows, item_rows), :]


def shards(
    user_pred,
    user_imp,
    item_pred,
    item_imp,
    uno_user,
    uno_item,
    obs_user,
    obs_item,
    obs_count,
    obs_label,
    obs_prop,
):
    item_ways = lax.axis_size("item")
    user_ways = lax.axis_size("user")
    tile = obs_label.shape[-1]
    rank = user_pred.shape[1]
    user_rows = user_pred.shape[0]
    shard_rows = item_pred.shape[0]
    user_blocks = user_rows // tile
    item_blocks = shard_rows // tile
    n_blocks = user_blocks * item_blocks
    obs_slots = obs_user.shape[-1] // item_ways

    labels = obs_label.reshape(item_ways, obs_slots * tile, tile)
    propens = obs_prop.reshape(item_ways, obs_slots * tile, tile)
    indices = [x.reshape(x.shape[-1]) for x in (uno_user, uno_item, obs_user, obs_item, obs_count)]
    shares = exchange_tiles(
        labels, propens, indices, (user_pred, user_imp, item_pred, item_imp), tile, item_blocks, obs_slots, user_ways
    )
    user_part = user_rows // item_ways
    return (shares[0, :user_part], shares[1, :user_part], shares[0, user_part:], shares[1, user_part:])


def solution(mesh):
    in_specs = (
        P("user", None),
        P("user", None),
        P("item", None),
        P("item", None),
        P("user", "item", None),
        P("user", "item", None),
        P("user", "item", None),
        P("user", "item", None),
        P("user", "item", None),
        P("user", "item", None, None, None),
        P("user", "item", None, None, None),
    )
    out_specs = (
        P(("user", "item"), None),
        P(("user", "item"), None),
        P(("item", "user"), None),
        P(("item", "user"), None),
    )
    return jax.shard_map(shards, mesh=mesh, in_specs=in_specs, out_specs=out_specs, check_vma=False)
```

```python
import functools

import jax
import jax.numpy as jnp
from jax import lax
from jax.experimental import pallas as pl
from jax.experimental.pallas import tpu as pltpu
from jax.sharding import PartitionSpec as P

MESH = pl.DeviceIdType.MESH

loss_weight = 0.015625


def product(form, first, second):
    return jnp.einsum(form, first, second, preferred_element_type=jnp.float32)


def exchange_kernel(axes, whole, count, work_in, work, *refs):
    x_refs, y_refs = refs[:count], refs[count + work_in : 2 * count + work_in]
    send_sem, recv_sem, local_sem = refs[-3:]
    work_refs = refs[count : count + work_in] + refs[2 * count + work_in : -3]
    barrier = pltpu.get_barrier_semaphore()
    for axis in axes:
        n = lax.axis_size(axis)
        me = lax.axis_index(axis)
        for k in range(1, n):
            pl.semaphore_signal(barrier, inc=1, device_id={axis: lax.rem(me + k, n)}, device_id_type=MESH)
    pl.semaphore_wait(barrier, sum(lax.axis_size(axis) - 1 for axis in axes))
    copies = []
    slot = 0
    for which, axis in enumerate(axes):
        n = lax.axis_size(axis)
        me = lax.axis_index(axis)
        x_ref, y_ref = x_refs[which], y_refs[which]
        local = pltpu.make_async_copy(x_ref if whole[which] else x_ref.at[me], y_ref.at[me], local_sem.at[which])
        local.start()
        copies.append(local)
        for k in range(1, n):
            peer = lax.rem(me + k, n)
            copy = pltpu.make_async_remote_copy(
                src_ref=x_ref if whole[which] else x_ref.at[peer],
                dst_ref=y_ref.at[me],
                send_sem=send_sem.at[slot],
                recv_sem=recv_sem.at[slot],
                device_id={axis: peer},
                device_id_type=MESH,
            )
            copy.start()
            copies.append(copy)
            slot += 1
    if work is not None:
        work(*work_refs)
    for copy in copies:
        copy.wait()


def exchange(pairs, collective, work=None, work_inputs=(), work_outputs=(), whole=None):
    axes = tuple(axis for _, axis in pairs)
    arrays = [x for x, _ in pairs]
    whole = tuple(whole) if whole is not None else (False,) * len(arrays)
    shapes = [(lax.axis_size(axis),) + x.shape if w else x.shape for (x, axis), w in zip(pairs, whole)]
    slots = sum(lax.axis_size(axis) - 1 for axis in axes)
    vmem = pl.BlockSpec(memory_space=pltpu.VMEM)
    return pl.pallas_call(
        functools.partial(exchange_kernel, axes, whole, len(arrays), len(work_inputs), work),
        out_shape=[jax.ShapeDtypeStruct(shape, x.dtype) for shape, x in zip(shapes, arrays)] + list(work_outputs),
        in_specs=[pl.BlockSpec(memory_space=pl.ANY)] * len(arrays) + [vmem] * len(work_inputs),
        out_specs=[pl.BlockSpec(memory_space=pl.ANY)] * len(arrays) + [vmem] * len(work_outputs),
        scratch_shapes=[
            pltpu.SemaphoreType.DMA((slots,)),
            pltpu.SemaphoreType.DMA((slots,)),
            pltpu.SemaphoreType.DMA((len(arrays),)),
        ],
        compiler_params=pltpu.CompilerParams(collective_id=collective, has_side_effects=True),
    )(*arrays, *work_inputs)


def reduce_kernel(axes, *refs):
    count = len(axes)
    x_refs, out_refs = refs[:count], refs[count : 2 * count]
    land_refs = refs[2 * count : 3 * count]
    send_sem, recv_sem, local_sem = refs[3 * count :]
    barrier = pltpu.get_barrier_semaphore()
    for axis in axes:
        n = lax.axis_size(axis)
        me = lax.axis_index(axis)
        for k in range(1, n):
            pl.semaphore_signal(barrier, inc=1, device_id={axis: lax.rem(me + k, n)}, device_id_type=MESH)
    pl.semaphore_wait(barrier, sum(lax.axis_size(axis) - 1 for axis in axes))
    copies = []
    slot = 0
    for which, axis in enumerate(axes):
        n = lax.axis_size(axis)
        me = lax.axis_index(axis)
        x_ref, land = x_refs[which], land_refs[which]
        local = pltpu.make_async_copy(x_ref.at[me], land.at[me], local_sem.at[which])
        local.start()
        copies.append(local)
        for k in range(1, n):
            peer = lax.rem(me + k, n)
            copy = pltpu.make_async_remote_copy(
                src_ref=x_ref.at[peer],
                dst_ref=land.at[me],
                send_sem=send_sem.at[slot],
                recv_sem=recv_sem.at[slot],
                device_id={axis: peer},
                device_id_type=MESH,
            )
            copy.start()
            copies.append(copy)
            slot += 1
    for copy in copies:
        copy.wait()
    for which in range(count):
        land = land_refs[which]
        total = land[0]
        for source in range(1, land.shape[0]):
            total = total + land[source]
        out_refs[which][...] = total


def reduce_exchange(pairs, collective):
    axes = tuple(axis for _, axis in pairs)
    arrays = [x for x, _ in pairs]
    slots = sum(lax.axis_size(axis) - 1 for axis in axes)
    return pl.pallas_call(
        functools.partial(reduce_kernel, axes),
        out_shape=[jax.ShapeDtypeStruct(x.shape[1:], x.dtype) for x in arrays],
        in_specs=[pl.BlockSpec(memory_space=pl.ANY)] * len(arrays),
        out_specs=[pl.BlockSpec(memory_space=pltpu.VMEM)] * len(arrays),
        scratch_shapes=[pltpu.VMEM(x.shape, x.dtype) for x in arrays]
        + [
            pltpu.SemaphoreType.DMA((slots,)),
            pltpu.SemaphoreType.DMA((slots,)),
            pltpu.SemaphoreType.DMA((len(arrays),)),
        ],
        compiler_params=pltpu.CompilerParams(collective_id=collective, has_side_effects=True),
    )(*arrays)


def observed_grads(valid, ologits, imputed, labels, propens):
    predicted = jax.nn.sigmoid(ologits)
    imputes = jax.nn.sigmoid(imputed)
    seen = (labels > 0).astype(jnp.float32)
    clicks = (labels == 2).astype(jnp.float32)
    weight = valid * seen / propens
    ograds = ((valid * (predicted - imputes) + weight * (imputes - clicks)) * loss_weight).astype(jnp.bfloat16)
    ohgrads = (
        2.0 * weight * (imputes - clicks) * ologits * ologits * imputes * (1.0 - imputes) * loss_weight
    ).astype(jnp.bfloat16)
    return ograds, ohgrads


def gather_kernel(
    tile, item_blocks, obs_slots,
    lab_x, prop_x, uu_x, ui_x, ou_x, oi_x, oc_x, up_ref, uimp_ref, vp_ref, vi_ref,
    user_out, item_out,
    lab_land, prop_land, uu_land, ui_land, ou_land, oi_land, oc_land, s_ref, m_ref, d_ref, user_acc, item_acc,
    user_land, item_land, lab_wide, lab_narrow, send_sem, recv_sem, local_sem, sum_send, sum_recv, sum_local,
):
    n = lax.axis_size("item")
    me = lax.axis_index("item")
    barrier = pltpu.get_barrier_semaphore()
    user_n = lax.axis_size("user")
    me_user = lax.axis_index("user")
    for k in range(1, n):
        pl.semaphore_signal(barrier, inc=1, device_id={"item": lax.rem(me + k, n)}, device_id_type=MESH)
    for k in range(1, user_n):
        pl.semaphore_signal(barrier, inc=1, device_id={"user": lax.rem(me_user + k, user_n)}, device_id_type=MESH)
    pl.semaphore_wait(barrier, (n - 1) + (user_n - 1))

    index_pairs = ((uu_x, uu_land), (ui_x, ui_land), (ou_x, ou_land), (oi_x, oi_land), (oc_x, oc_land))
    tile_pairs = ((lab_x, lab_land), (prop_x, prop_land))

    def send(which, src, dst, k):
        copy = pltpu.make_async_remote_copy(
            src_ref=src,
            dst_ref=dst,
            send_sem=send_sem.at[which, k - 1],
            recv_sem=recv_sem.at[which, k - 1],
            device_id={"item": lax.rem(me + k, n)},
            device_id_type=MESH,
        )
        copy.start()
        return copy

    tile_local = []
    tile_copies = [[] for _ in range(n)]
    staging = pltpu.make_async_copy(lab_x, lab_wide, local_sem.at[len(index_pairs) + len(tile_pairs)])
    staging.start()

    def send_tiles(which, x, land):
        slot = len(index_pairs) + which
        local = pltpu.make_async_copy(x.at[me], land.at[me], local_sem.at[slot])
        local.start()
        tile_local.append(local)
        for k in range(1, n):
            tile_copies[k].append(send(slot, x.at[lax.rem(me + k, n)], land.at[me], k))

    send_tiles(1, prop_x, prop_land)
    index_copies = []
    for which, (x, land) in enumerate(index_pairs):
        local = pltpu.make_async_copy(x, land.at[me], local_sem.at[which])
        local.start()
        index_copies.append(local)
        for k in range(1, n):
            index_copies.append(send(which, x, land.at[me], k))
    staging.wait()
    for row in range(lab_wide.shape[0]):
        lab_narrow[row] = lab_wide[row].astype(lab_narrow.dtype)
    send_tiles(0, lab_narrow, lab_land)

    dims = (((1,), (1,)), ((), ()))

    def block(k, carry):
        ub = k // item_blocks
        ib = k % item_blocks
        logits = lax.dot_general(up_ref[ub], vp_ref[ib], dims, preferred_element_type=jnp.float32)
        imputed = lax.dot_general(uimp_ref[ub], vi_ref[ib], dims, preferred_element_type=jnp.float32)
        s_ref[k] = logits
        m_ref[k] = imputed
        d_ref[k] = ((jax.nn.sigmoid(logits) - jax.nn.sigmoid(imputed)) * loss_weight).astype(d_ref.dtype)
        return carry

    lax.fori_loop(0, s_ref.shape[0], block, 0)
    user_acc[...] = jnp.zeros(user_acc.shape, jnp.float32)
    item_acc[...] = jnp.zeros(item_acc.shape, jnp.float32)
    forward = (((1,), (0,)), ((), ()))
    backward = (((0,), (0,)), ((), ()))
    user_blocks = user_acc.shape[1] // tile

    for copy in index_copies:
        copy.wait()
    uno_slots = uu_land.shape[1] // n
    slots = []
    for t in range(n * uno_slots):
        origin = t // uno_slots
        slot = me * uno_slots + t % uno_slots
        slots.append(uu_land[origin, slot] * item_blocks + ui_land[origin, slot])
    for k in range(s_ref.shape[0]):
        count = jnp.where(slots[0] == k, 1.0, 0.0)
        for t in range(1, len(slots)):
            count = count + jnp.where(slots[t] == k, 1.0, 0.0)
        users = pl.ds((k // item_blocks) * tile, tile)
        items = pl.ds((k % item_blocks) * tile, tile)
        grads = d_ref[k]
        user_acc[0, users, :] += count * lax.dot_general(
            grads, vp_ref[k % item_blocks], forward, preferred_element_type=jnp.float32
        )
        item_acc[0, items, :] += count * lax.dot_general(
            grads, up_ref[k // item_blocks], backward, preferred_element_type=jnp.float32
        )

    def origin_tiles(origin):
        for place in range(obs_slots):
            slot = me * obs_slots + place
            ub = ou_land[origin, slot]
            ib = oi_land[origin, slot]
            pos = ub * item_blocks + ib
            valid = jnp.where(place < oc_land[origin, me], 1.0, 0.0).astype(jnp.float32)
            labels = lab_land[origin, pl.ds(place * tile, tile), :].astype(jnp.float32)
            propens = prop_land[origin, pl.ds(place * tile, tile), :].astype(jnp.float32)
            ograds, ohgrads = observed_grads(valid, s_ref[pos], m_ref[pos], labels, propens)
            terms = []
            for g, u_ref, v_ref in ((ograds, up_ref, vp_ref), (ohgrads, uimp_ref, vi_ref)):
                terms.append(
                    (
                        lax.dot_general(g, v_ref[ib], forward, preferred_element_type=jnp.float32),
                        lax.dot_general(g, u_ref[ub], backward, preferred_element_type=jnp.float32),
                    )
                )
            for b in range(user_blocks):
                hit = jnp.where(ub == b, 1.0, 0.0)
                for model in range(2):
                    user_acc[model, pl.ds(b * tile, tile), :] += hit * terms[model][0]
            for c in range(item_blocks):
                hit = jnp.where(ib == c, 1.0, 0.0)
                for model in range(2):
                    item_acc[model, pl.ds(c * tile, tile), :] += hit * terms[model][1]

    for copy in tile_local:
        copy.wait()
    origin_tiles(me)
    for k in range(1, n):
        for copy in tile_copies[k]:
            copy.wait()
        origin_tiles(lax.rem(me + n - k, n))
    sums = []
    for which, (acc, land, axis, me_at, size) in enumerate(
        ((user_acc, user_land, "item", me, n), (item_acc, item_land, "user", me_user, user_n))
    ):
        rows = land.shape[2]
        local = pltpu.make_async_copy(acc.at[:, pl.ds(me_at * rows, rows), :], land.at[me_at], sum_local.at[which])
        local.start()
        copies = [local]
        for k in range(1, size):
            peer = lax.rem(me_at + k, size)
            copy = pltpu.make_async_remote_copy(
                src_ref=acc.at[:, pl.ds(peer * rows, rows), :],
                dst_ref=land.at[me_at],
                send_sem=sum_send.at[which, k - 1],
                recv_sem=sum_recv.at[which, k - 1],
                device_id={axis: peer},
                device_id_type=MESH,
            )
            copy.start()
            copies.append(copy)
        sums.append(copies)
    for copies in sums:
        for copy in copies:
            copy.wait()
    for land, out in ((user_land, user_out), (item_land, item_out)):
        total = land[0]
        for source in range(1, land.shape[0]):
            total = total + land[source]
        out[...] = total


def exchange_tiles(labels, propens, indices, factors, tile, item_blocks, obs_slots, user_ways):
    n = lax.axis_size("item")
    user_rows, rank = factors[0].shape
    shard_rows = factors[2].shape[0]
    factors = [x.reshape(x.shape[0] // tile, tile, rank) for x in factors]
    n_blocks = factors[0].shape[0] * item_blocks
    n_tiles = n * obs_slots
    vmem = pl.BlockSpec(memory_space=pltpu.VMEM)
    smem = pl.BlockSpec(memory_space=pltpu.SMEM)
    anyspace = pl.BlockSpec(memory_space=pl.ANY)
    return pl.pallas_call(
        functools.partial(gather_kernel, tile, item_blocks, obs_slots),
        out_shape=[
            jax.ShapeDtypeStruct((2, user_rows // n, rank), jnp.float32),
            jax.ShapeDtypeStruct((2, shard_rows // user_ways, rank), jnp.float32),
        ],
        in_specs=[anyspace] * 7 + [vmem] * 4,
        out_specs=[vmem] * 2,
        scratch_shapes=[
            pltpu.VMEM((n,) + labels.shape[1:], jnp.bfloat16),
            pltpu.VMEM((n,) + propens.shape[1:], propens.dtype),
        ]
        + [pltpu.SMEM((n,) + x.shape, x.dtype) for x in indices]
        + [
            pltpu.VMEM((n_blocks, tile, tile), jnp.float32),
            pltpu.VMEM((n_blocks, tile, tile), jnp.float32),
            pltpu.VMEM((n_blocks, tile, tile), jnp.bfloat16),
            pltpu.VMEM((2, user_rows, rank), jnp.float32),
            pltpu.VMEM((2, shard_rows, rank), jnp.float32),
            pltpu.VMEM((n, 2, user_rows // n, rank), jnp.float32),
            pltpu.VMEM((user_ways, 2, shard_rows // user_ways, rank), jnp.float32),
            pltpu.VMEM(labels.shape, labels.dtype),
            pltpu.VMEM(labels.shape, jnp.bfloat16),
            pltpu.SemaphoreType.DMA((7, n - 1)),
            pltpu.SemaphoreType.DMA((7, n - 1)),
            pltpu.SemaphoreType.DMA((8,)),
            pltpu.SemaphoreType.DMA((2, max(n, user_ways) - 1)),
            pltpu.SemaphoreType.DMA((2, max(n, user_ways) - 1)),
            pltpu.SemaphoreType.DMA((2,)),
        ],
        compiler_params=pltpu.CompilerParams(collective_id=0, has_side_effects=True),
    )(labels, propens, *indices, *factors)


def tile_kernel(
    tile, user_blocks, item_blocks,
    slot_ref, pos_ref, d_ref, gt_ref, ht_ref, up_ref, ui_ref, vp_ref, vi_ref,
    user_out, item_out,
    count_ref, g_acc, h_acc, user_acc, item_acc,
):
    n_blocks = user_blocks * item_blocks
    for k in range(n_blocks):
        count_ref[k] = 0

    def tally(t, carry):
        k = slot_ref[t]
        count_ref[k] = count_ref[k] + 1
        return carry

    lax.fori_loop(0, slot_ref.shape[0], tally, 0)
    for k in range(n_blocks):
        g_acc[k] = count_ref[k].astype(jnp.float32) * d_ref[k].astype(jnp.float32)
        h_acc[k] = jnp.zeros((tile, tile), jnp.float32)

    def observed(t, carry):
        pos = pos_ref[t]
        g_acc[pos] += gt_ref[t].astype(jnp.float32)
        h_acc[pos] += ht_ref[t].astype(jnp.float32)
        return carry

    lax.fori_loop(0, gt_ref.shape[0], observed, 0)

    user_acc[...] = jnp.zeros(user_acc.shape, jnp.float32)
    item_acc[...] = jnp.zeros(item_acc.shape, jnp.float32)
    forward = (((1,), (0,)), ((), ()))
    backward = (((0,), (0,)), ((), ()))
    for ub in range(user_blocks):
        users = pl.ds(ub * tile, tile)
        for ib in range(item_blocks):
            items = pl.ds(ib * tile, tile)
            k = ub * item_blocks + ib
            for model, acc, u_ref, v_ref in ((0, g_acc, up_ref, vp_ref), (1, h_acc, ui_ref, vi_ref)):
                wide = acc[k]
                hi = wide.astype(jnp.bfloat16)
                lo = (wide - hi.astype(jnp.float32)).astype(jnp.bfloat16)
                v = v_ref[items, :]
                u = u_ref[users, :]
                user_acc[model, users, :] += lax.dot_general(
                    hi, v, forward, preferred_element_type=jnp.float32
                ) + lax.dot_general(lo, v, forward, preferred_element_type=jnp.float32)
                item_acc[model, items, :] += lax.dot_general(
                    hi, u, backward, preferred_element_type=jnp.float32
                ) + lax.dot_general(lo, u, backward, preferred_element_type=jnp.float32)
    user_rows = user_out.shape[2]
    for dest in range(user_out.shape[0]):
        user_out[dest] = user_acc[:, pl.ds(dest * user_rows, user_rows), :]
    item_rows = item_out.shape[2]
    for dest in range(item_out.shape[0]):
        item_out[dest] = item_acc[:, pl.ds(dest * item_rows, item_rows), :]


def shards(
    user_pred,
    user_imp,
    item_pred,
    item_imp,
    uno_user,
    uno_item,
    obs_user,
    obs_item,
    obs_count,
    obs_label,
    obs_prop,
):
    item_ways = lax.axis_size("item")
    user_ways = lax.axis_size("user")
    tile = obs_label.shape[-1]
    rank = user_pred.shape[1]
    user_rows = user_pred.shape[0]
    shard_rows = item_pred.shape[0]
    user_blocks = user_rows // tile
    item_blocks = shard_rows // tile
    n_blocks = user_blocks * item_blocks
    obs_slots = obs_user.shape[-1] // item_ways

    labels = obs_label.reshape(item_ways, obs_slots * tile, tile)
    propens = obs_prop.reshape(item_ways, obs_slots * tile, tile)
    indices = [x.reshape(x.shape[-1]) for x in (uno_user, uno_item, obs_user, obs_item, obs_count)]
    user_share, item_share = exchange_tiles(
        labels, propens, indices, (user_pred, user_imp, item_pred, item_imp), tile, item_blocks, obs_slots, user_ways
    )
    return (user_share[0], user_share[1], item_share[0], item_share[1])


def solution(mesh):
    in_specs = (
        P("user", None),
        P("user", None),
        P("item", None),
        P("item", None),
        P("user", "item", None),
        P("user", "item", None),
        P("user", "item", None),
        P("user", "item", None),
        P("user", "item", None),
        P("user", "item", None, None, None),
        P("user", "item", None, None, None),
    )
    out_specs = (
        P(("user", "item"), None),
        P(("user", "item"), None),
        P(("item", "user"), None),
        P(("item", "user"), None),
    )
    return jax.shard_map(shards, mesh=mesh, in_specs=in_specs, out_specs=out_specs, check_vma=False)
```

```python
import functools

import jax
import jax.numpy as jnp
from jax import lax
from jax.experimental import pallas as pl
from jax.experimental.pallas import tpu as pltpu
from jax.sharding import PartitionSpec as P

MESH = pl.DeviceIdType.MESH

loss_weight = 0.015625


def product(form, first, second):
    return jnp.einsum(form, first, second, preferred_element_type=jnp.float32)


def exchange_kernel(axes, whole, count, work_in, work, *refs):
    x_refs, y_refs = refs[:count], refs[count + work_in : 2 * count + work_in]
    send_sem, recv_sem, local_sem = refs[-3:]
    work_refs = refs[count : count + work_in] + refs[2 * count + work_in : -3]
    barrier = pltpu.get_barrier_semaphore()
    for axis in axes:
        n = lax.axis_size(axis)
        me = lax.axis_index(axis)
        for k in range(1, n):
            pl.semaphore_signal(barrier, inc=1, device_id={axis: lax.rem(me + k, n)}, device_id_type=MESH)
    pl.semaphore_wait(barrier, sum(lax.axis_size(axis) - 1 for axis in axes))
    copies = []
    slot = 0
    for which, axis in enumerate(axes):
        n = lax.axis_size(axis)
        me = lax.axis_index(axis)
        x_ref, y_ref = x_refs[which], y_refs[which]
        local = pltpu.make_async_copy(x_ref if whole[which] else x_ref.at[me], y_ref.at[me], local_sem.at[which])
        local.start()
        copies.append(local)
        for k in range(1, n):
            peer = lax.rem(me + k, n)
            copy = pltpu.make_async_remote_copy(
                src_ref=x_ref if whole[which] else x_ref.at[peer],
                dst_ref=y_ref.at[me],
                send_sem=send_sem.at[slot],
                recv_sem=recv_sem.at[slot],
                device_id={axis: peer},
                device_id_type=MESH,
            )
            copy.start()
            copies.append(copy)
            slot += 1
    if work is not None:
        work(*work_refs)
    for copy in copies:
        copy.wait()


def exchange(pairs, collective, work=None, work_inputs=(), work_outputs=(), whole=None):
    axes = tuple(axis for _, axis in pairs)
    arrays = [x for x, _ in pairs]
    whole = tuple(whole) if whole is not None else (False,) * len(arrays)
    shapes = [(lax.axis_size(axis),) + x.shape if w else x.shape for (x, axis), w in zip(pairs, whole)]
    slots = sum(lax.axis_size(axis) - 1 for axis in axes)
    vmem = pl.BlockSpec(memory_space=pltpu.VMEM)
    return pl.pallas_call(
        functools.partial(exchange_kernel, axes, whole, len(arrays), len(work_inputs), work),
        out_shape=[jax.ShapeDtypeStruct(shape, x.dtype) for shape, x in zip(shapes, arrays)] + list(work_outputs),
        in_specs=[pl.BlockSpec(memory_space=pl.ANY)] * len(arrays) + [vmem] * len(work_inputs),
        out_specs=[pl.BlockSpec(memory_space=pl.ANY)] * len(arrays) + [vmem] * len(work_outputs),
        scratch_shapes=[
            pltpu.SemaphoreType.DMA((slots,)),
            pltpu.SemaphoreType.DMA((slots,)),
            pltpu.SemaphoreType.DMA((len(arrays),)),
        ],
        compiler_params=pltpu.CompilerParams(collective_id=collective, has_side_effects=True),
    )(*arrays, *work_inputs)


def reduce_kernel(axes, *refs):
    count = len(axes)
    x_refs, out_refs = refs[:count], refs[count : 2 * count]
    land_refs = refs[2 * count : 3 * count]
    send_sem, recv_sem, local_sem = refs[3 * count :]
    barrier = pltpu.get_barrier_semaphore()
    for axis in axes:
        n = lax.axis_size(axis)
        me = lax.axis_index(axis)
        for k in range(1, n):
            pl.semaphore_signal(barrier, inc=1, device_id={axis: lax.rem(me + k, n)}, device_id_type=MESH)
    pl.semaphore_wait(barrier, sum(lax.axis_size(axis) - 1 for axis in axes))
    copies = []
    slot = 0
    for which, axis in enumerate(axes):
        n = lax.axis_size(axis)
        me = lax.axis_index(axis)
        x_ref, land = x_refs[which], land_refs[which]
        local = pltpu.make_async_copy(x_ref.at[me], land.at[me], local_sem.at[which])
        local.start()
        copies.append(local)
        for k in range(1, n):
            peer = lax.rem(me + k, n)
            copy = pltpu.make_async_remote_copy(
                src_ref=x_ref.at[peer],
                dst_ref=land.at[me],
                send_sem=send_sem.at[slot],
                recv_sem=recv_sem.at[slot],
                device_id={axis: peer},
                device_id_type=MESH,
            )
            copy.start()
            copies.append(copy)
            slot += 1
    for copy in copies:
        copy.wait()
    for which in range(count):
        land = land_refs[which]
        total = land[0]
        for source in range(1, land.shape[0]):
            total = total + land[source]
        out_refs[which][...] = total


def reduce_exchange(pairs, collective):
    axes = tuple(axis for _, axis in pairs)
    arrays = [x for x, _ in pairs]
    slots = sum(lax.axis_size(axis) - 1 for axis in axes)
    return pl.pallas_call(
        functools.partial(reduce_kernel, axes),
        out_shape=[jax.ShapeDtypeStruct(x.shape[1:], x.dtype) for x in arrays],
        in_specs=[pl.BlockSpec(memory_space=pl.ANY)] * len(arrays),
        out_specs=[pl.BlockSpec(memory_space=pltpu.VMEM)] * len(arrays),
        scratch_shapes=[pltpu.VMEM(x.shape, x.dtype) for x in arrays]
        + [
            pltpu.SemaphoreType.DMA((slots,)),
            pltpu.SemaphoreType.DMA((slots,)),
            pltpu.SemaphoreType.DMA((len(arrays),)),
        ],
        compiler_params=pltpu.CompilerParams(collective_id=collective, has_side_effects=True),
    )(*arrays)


def observed_grads(valid, ologits, imputed, labels, propens):
    predicted = jax.nn.sigmoid(ologits)
    imputes = jax.nn.sigmoid(imputed)
    seen = (labels > 0).astype(jnp.float32)
    clicks = (labels == 2).astype(jnp.float32)
    weight = valid * seen / propens
    ograds = ((valid * (predicted - imputes) + weight * (imputes - clicks)) * loss_weight).astype(jnp.bfloat16)
    ohgrads = (
        2.0 * weight * (imputes - clicks) * ologits * ologits * imputes * (1.0 - imputes) * loss_weight
    ).astype(jnp.bfloat16)
    return ograds, ohgrads


def gather_kernel(
    tile, item_blocks, obs_slots,
    lab_x, prop_x, uu_x, ui_x, ou_x, oi_x, oc_x, up_ref, uimp_ref, vp_ref, vi_ref,
    user_out, item_out,
    lab_land, prop_land, uu_land, ui_land, ou_land, oi_land, oc_land, s_ref, m_ref, d_ref, user_acc, item_acc,
    user_land, item_land, lab_wide, lab_narrow, send_sem, recv_sem, local_sem, sum_send, sum_recv, sum_local,
):
    n = lax.axis_size("item")
    me = lax.axis_index("item")
    barrier = pltpu.get_barrier_semaphore()
    user_n = lax.axis_size("user")
    me_user = lax.axis_index("user")
    for k in range(1, n):
        pl.semaphore_signal(barrier, inc=1, device_id={"item": lax.rem(me + k, n)}, device_id_type=MESH)
    for k in range(1, user_n):
        pl.semaphore_signal(barrier, inc=1, device_id={"user": lax.rem(me_user + k, user_n)}, device_id_type=MESH)
    pl.semaphore_wait(barrier, (n - 1) + (user_n - 1))

    index_pairs = ((uu_x, uu_land), (ui_x, ui_land), (ou_x, ou_land), (oi_x, oi_land), (oc_x, oc_land))
    tile_pairs = ((lab_x, lab_land), (prop_x, prop_land))

    def send(which, src, dst, k):
        copy = pltpu.make_async_remote_copy(
            src_ref=src,
            dst_ref=dst,
            send_sem=send_sem.at[which, k - 1],
            recv_sem=recv_sem.at[which, k - 1],
            device_id={"item": lax.rem(me + k, n)},
            device_id_type=MESH,
        )
        copy.start()
        return copy

    tile_local = []
    tile_copies = [[] for _ in range(n)]
    staging = pltpu.make_async_copy(lab_x, lab_wide, local_sem.at[len(index_pairs) + len(tile_pairs)])
    staging.start()

    def send_tiles(which, x, land):
        slot = len(index_pairs) + which
        local = pltpu.make_async_copy(x.at[me], land.at[me], local_sem.at[slot])
        local.start()
        tile_local.append(local)
        for k in range(1, n):
            tile_copies[k].append(send(slot, x.at[lax.rem(me + k, n)], land.at[me], k))

    send_tiles(1, prop_x, prop_land)
    index_copies = []
    for which, (x, land) in enumerate(index_pairs):
        local = pltpu.make_async_copy(x, land.at[me], local_sem.at[which])
        local.start()
        index_copies.append(local)
        for k in range(1, n):
            index_copies.append(send(which, x, land.at[me], k))
    staging.wait()
    for row in range(lab_wide.shape[0]):
        lab_narrow[row] = lab_wide[row].astype(lab_narrow.dtype)
    send_tiles(0, lab_narrow, lab_land)

    dims = (((1,), (1,)), ((), ()))

    def block(k, carry):
        ub = k // item_blocks
        ib = k % item_blocks
        logits = lax.dot_general(up_ref[ub], vp_ref[ib], dims, preferred_element_type=jnp.float32)
        imputed = lax.dot_general(uimp_ref[ub], vi_ref[ib], dims, preferred_element_type=jnp.float32)
        s_ref[k] = logits
        m_ref[k] = imputed
        d_ref[k] = ((jax.nn.sigmoid(logits) - jax.nn.sigmoid(imputed)) * loss_weight).astype(d_ref.dtype)
        return carry

    lax.fori_loop(0, s_ref.shape[0], block, 0)
    user_acc[...] = jnp.zeros(user_acc.shape, jnp.float32)
    item_acc[...] = jnp.zeros(item_acc.shape, jnp.float32)
    forward = (((1,), (0,)), ((), ()))
    backward = (((0,), (0,)), ((), ()))
    user_blocks = user_acc.shape[1] // tile

    for copy in index_copies:
        copy.wait()
    uno_slots = uu_land.shape[1] // n
    slots = []
    for t in range(n * uno_slots):
        origin = t // uno_slots
        slot = me * uno_slots + t % uno_slots
        slots.append(uu_land[origin, slot] * item_blocks + ui_land[origin, slot])
    for k in range(s_ref.shape[0]):
        count = jnp.where(slots[0] == k, 1.0, 0.0)
        for t in range(1, len(slots)):
            count = count + jnp.where(slots[t] == k, 1.0, 0.0)
        users = pl.ds((k // item_blocks) * tile, tile)
        items = pl.ds((k % item_blocks) * tile, tile)
        grads = d_ref[k]
        user_acc[0, users, :] += count * lax.dot_general(
            grads, vp_ref[k % item_blocks], forward, preferred_element_type=jnp.float32
        )
        item_acc[0, items, :] += count * lax.dot_general(
            grads, up_ref[k // item_blocks], backward, preferred_element_type=jnp.float32
        )

    def origin_tiles(origin):
        for place in range(obs_slots):
            slot = me * obs_slots + place
            ub = ou_land[origin, slot]
            ib = oi_land[origin, slot]
            pos = ub * item_blocks + ib
            valid = jnp.where(place < oc_land[origin, me], 1.0, 0.0).astype(jnp.float32)
            labels = lab_land[origin, pl.ds(place * tile, tile), :].astype(jnp.float32)
            propens = prop_land[origin, pl.ds(place * tile, tile), :].astype(jnp.float32)
            ograds, ohgrads = observed_grads(valid, s_ref[pos], m_ref[pos], labels, propens)
            terms = []
            for g, u_ref, v_ref in ((ograds, up_ref, vp_ref), (ohgrads, uimp_ref, vi_ref)):
                terms.append(
                    (
                        lax.dot_general(g, v_ref[ib], forward, preferred_element_type=jnp.float32),
                        lax.dot_general(g, u_ref[ub], backward, preferred_element_type=jnp.float32),
                    )
                )
            for b in range(user_blocks):
                hit = jnp.where(ub == b, 1.0, 0.0)
                for model in range(2):
                    user_acc[model, pl.ds(b * tile, tile), :] += hit * terms[model][0]
            for c in range(item_blocks):
                hit = jnp.where(ib == c, 1.0, 0.0)
                for model in range(2):
                    item_acc[model, pl.ds(c * tile, tile), :] += hit * terms[model][1]

    for copy in tile_local:
        copy.wait()
    origin_tiles(me)
    order = [k for pair in zip(range(1, n), range(n - 1, 0, -1)) for k in pair]
    order = list(dict.fromkeys(order))
    for k in order:
        for copy in tile_copies[k]:
            copy.wait()
        origin_tiles(lax.rem(me + n - k, n))
    sums = []
    for which, (acc, land, axis, me_at, size) in enumerate(
        ((user_acc, user_land, "item", me, n), (item_acc, item_land, "user", me_user, user_n))
    ):
        rows = land.shape[2]
        local = pltpu.make_async_copy(acc.at[:, pl.ds(me_at * rows, rows), :], land.at[me_at], sum_local.at[which])
        local.start()
        copies = [local]
        for k in range(1, size):
            peer = lax.rem(me_at + k, size)
            copy = pltpu.make_async_remote_copy(
                src_ref=acc.at[:, pl.ds(peer * rows, rows), :],
                dst_ref=land.at[me_at],
                send_sem=sum_send.at[which, k - 1],
                recv_sem=sum_recv.at[which, k - 1],
                device_id={axis: peer},
                device_id_type=MESH,
            )
            copy.start()
            copies.append(copy)
        sums.append(copies)
    for copies in sums:
        for copy in copies:
            copy.wait()
    for land, out in ((user_land, user_out), (item_land, item_out)):
        total = land[0]
        for source in range(1, land.shape[0]):
            total = total + land[source]
        out[...] = total


def exchange_tiles(labels, propens, indices, factors, tile, item_blocks, obs_slots, user_ways):
    n = lax.axis_size("item")
    user_rows, rank = factors[0].shape
    shard_rows = factors[2].shape[0]
    factors = [x.reshape(x.shape[0] // tile, tile, rank) for x in factors]
    n_blocks = factors[0].shape[0] * item_blocks
    n_tiles = n * obs_slots
    vmem = pl.BlockSpec(memory_space=pltpu.VMEM)
    smem = pl.BlockSpec(memory_space=pltpu.SMEM)
    anyspace = pl.BlockSpec(memory_space=pl.ANY)
    return pl.pallas_call(
        functools.partial(gather_kernel, tile, item_blocks, obs_slots),
        out_shape=[
            jax.ShapeDtypeStruct((2, user_rows // n, rank), jnp.float32),
            jax.ShapeDtypeStruct((2, shard_rows // user_ways, rank), jnp.float32),
        ],
        in_specs=[anyspace] * 7 + [vmem] * 4,
        out_specs=[vmem] * 2,
        scratch_shapes=[
            pltpu.VMEM((n,) + labels.shape[1:], jnp.bfloat16),
            pltpu.VMEM((n,) + propens.shape[1:], propens.dtype),
        ]
        + [pltpu.SMEM((n,) + x.shape, x.dtype) for x in indices]
        + [
            pltpu.VMEM((n_blocks, tile, tile), jnp.float32),
            pltpu.VMEM((n_blocks, tile, tile), jnp.float32),
            pltpu.VMEM((n_blocks, tile, tile), jnp.bfloat16),
            pltpu.VMEM((2, user_rows, rank), jnp.float32),
            pltpu.VMEM((2, shard_rows, rank), jnp.float32),
            pltpu.VMEM((n, 2, user_rows // n, rank), jnp.float32),
            pltpu.VMEM((user_ways, 2, shard_rows // user_ways, rank), jnp.float32),
            pltpu.VMEM(labels.shape, labels.dtype),
            pltpu.VMEM(labels.shape, jnp.bfloat16),
            pltpu.SemaphoreType.DMA((7, n - 1)),
            pltpu.SemaphoreType.DMA((7, n - 1)),
            pltpu.SemaphoreType.DMA((8,)),
            pltpu.SemaphoreType.DMA((2, max(n, user_ways) - 1)),
            pltpu.SemaphoreType.DMA((2, max(n, user_ways) - 1)),
            pltpu.SemaphoreType.DMA((2,)),
        ],
        compiler_params=pltpu.CompilerParams(collective_id=0, has_side_effects=True),
    )(labels, propens, *indices, *factors)


def tile_kernel(
    tile, user_blocks, item_blocks,
    slot_ref, pos_ref, d_ref, gt_ref, ht_ref, up_ref, ui_ref, vp_ref, vi_ref,
    user_out, item_out,
    count_ref, g_acc, h_acc, user_acc, item_acc,
):
    n_blocks = user_blocks * item_blocks
    for k in range(n_blocks):
        count_ref[k] = 0

    def tally(t, carry):
        k = slot_ref[t]
        count_ref[k] = count_ref[k] + 1
        return carry

    lax.fori_loop(0, slot_ref.shape[0], tally, 0)
    for k in range(n_blocks):
        g_acc[k] = count_ref[k].astype(jnp.float32) * d_ref[k].astype(jnp.float32)
        h_acc[k] = jnp.zeros((tile, tile), jnp.float32)

    def observed(t, carry):
        pos = pos_ref[t]
        g_acc[pos] += gt_ref[t].astype(jnp.float32)
        h_acc[pos] += ht_ref[t].astype(jnp.float32)
        return carry

    lax.fori_loop(0, gt_ref.shape[0], observed, 0)

    user_acc[...] = jnp.zeros(user_acc.shape, jnp.float32)
    item_acc[...] = jnp.zeros(item_acc.shape, jnp.float32)
    forward = (((1,), (0,)), ((), ()))
    backward = (((0,), (0,)), ((), ()))
    for ub in range(user_blocks):
        users = pl.ds(ub * tile, tile)
        for ib in range(item_blocks):
            items = pl.ds(ib * tile, tile)
            k = ub * item_blocks + ib
            for model, acc, u_ref, v_ref in ((0, g_acc, up_ref, vp_ref), (1, h_acc, ui_ref, vi_ref)):
                wide = acc[k]
                hi = wide.astype(jnp.bfloat16)
                lo = (wide - hi.astype(jnp.float32)).astype(jnp.bfloat16)
                v = v_ref[items, :]
                u = u_ref[users, :]
                user_acc[model, users, :] += lax.dot_general(
                    hi, v, forward, preferred_element_type=jnp.float32
                ) + lax.dot_general(lo, v, forward, preferred_element_type=jnp.float32)
                item_acc[model, items, :] += lax.dot_general(
                    hi, u, backward, preferred_element_type=jnp.float32
                ) + lax.dot_general(lo, u, backward, preferred_element_type=jnp.float32)
    user_rows = user_out.shape[2]
    for dest in range(user_out.shape[0]):
        user_out[dest] = user_acc[:, pl.ds(dest * user_rows, user_rows), :]
    item_rows = item_out.shape[2]
    for dest in range(item_out.shape[0]):
        item_out[dest] = item_acc[:, pl.ds(dest * item_rows, item_rows), :]


def shards(
    user_pred,
    user_imp,
    item_pred,
    item_imp,
    uno_user,
    uno_item,
    obs_user,
    obs_item,
    obs_count,
    obs_label,
    obs_prop,
):
    item_ways = lax.axis_size("item")
    user_ways = lax.axis_size("user")
    tile = obs_label.shape[-1]
    rank = user_pred.shape[1]
    user_rows = user_pred.shape[0]
    shard_rows = item_pred.shape[0]
    user_blocks = user_rows // tile
    item_blocks = shard_rows // tile
    n_blocks = user_blocks * item_blocks
    obs_slots = obs_user.shape[-1] // item_ways

    labels = obs_label.reshape(item_ways, obs_slots * tile, tile)
    propens = obs_prop.reshape(item_ways, obs_slots * tile, tile)
    indices = [x.reshape(x.shape[-1]) for x in (uno_user, uno_item, obs_user, obs_item, obs_count)]
    user_share, item_share = exchange_tiles(
        labels, propens, indices, (user_pred, user_imp, item_pred, item_imp), tile, item_blocks, obs_slots, user_ways
    )
    return (user_share[0], user_share[1], item_share[0], item_share[1])


def solution(mesh):
    in_specs = (
        P("user", None),
        P("user", None),
        P("item", None),
        P("item", None),
        P("user", "item", None),
        P("user", "item", None),
        P("user", "item", None),
        P("user", "item", None),
        P("user", "item", None),
        P("user", "item", None, None, None),
        P("user", "item", None, None, None),
    )
    out_specs = (
        P(("user", "item"), None),
        P(("user", "item"), None),
        P(("item", "user"), None),
        P(("item", "user"), None),
    )
    return jax.shard_map(shards, mesh=mesh, in_specs=in_specs, out_specs=out_specs, check_vma=False)
```
